32 devices in a mesh: seq: 2 (over x), fsdp: 16 (over z, y, core).
Axes of the slice: x: 2, y: 2, z: 4, core: 2. Of those that a mesh axis runs over, the one named last changes fastest.
Arguments:
- frames_in: float32 [16, 256, 768], P('fsdp', 'seq'), may hold values from -6 to 6
- cotangent: float32 [16, 256, 768], P('fsdp', 'seq'), may hold values from -6 to 6
- first_gain: bfloat16 [1, 768], P(None, 'fsdp'), may hold values from 0.099609375 to 1.8984375
- first_bias: bfloat16 [1, 768], P(None, 'fsdp'), may hold values from -3 to 3
- query_weight: bfloat16 [1, 768, 768], P(None, 'fsdp'), may hold values from -0.21875 to 0.21875
- query_bias: bfloat16 [1, 768], P(None, 'fsdp'), may hold values from -3 to 3
- key_weight: bfloat16 [1, 768, 768], P(None, 'fsdp'), may hold values from -0.21875 to 0.21875
- value_weight: bfloat16 [1, 768, 768], P(None, 'fsdp'), may hold values from -0.21875 to 0.21875
- value_bias: bfloat16 [1, 768], P(None, 'fsdp'), may hold values from -3 to 3
- out_weight: bfloat16 [1, 768, 768], P(None, 'fsdp'), may hold values from -3.5 to 3.5
- out_bias: bfloat16 [1, 768], P(None, 'fsdp'), may hold values from -3 to 3
- second_gain: bfloat16 [1, 768], P(None, 'fsdp'), may hold values from 0.099609375 to 1.8984375
- second_bias: bfloat16 [1, 768], P(None, 'fsdp'), may hold values from -3 to 3
- up_weight: bfloat16 [1, 768, 3072], P(None, 'fsdp'), may hold values from -0.21875 to 0.21875
- up_bias: bfloat16 [1, 3072], P(None, 'fsdp'), may hold values from -3 to 3
- down_weight: bfloat16 [1, 3072, 768], P(None, 'fsdp'), may hold values from -0.109375 to 0.109375
- down_bias: bfloat16 [1, 768], P(None, 'fsdp'), may hold values from -3 to 3
Outputs:
- outputs: float32 [16, 256, 768], P('fsdp', 'seq')
- input_gradient: float32 [16, 256, 768], P('fsdp', 'seq')
- first_gain_gradient: float32 [1, 768], P(None, 'fsdp')
- first_bias_gradient: float32 [1, 768], P(None, 'fsdp')
- query_weight_gradient: float32 [1, 768, 768], P(None, 'fsdp')
- query_bias_gradient: float32 [1, 768], P(None, 'fsdp')
- key_weight_gradient: float32 [1, 768, 768], P(None, 'fsdp')
- value_weight_gradient: float32 [1, 768, 768], P(None, 'fsdp')
- value_bias_gradient: float32 [1, 768], P(None, 'fsdp')
- out_weight_gradient: float32 [1, 768, 768], P(None, 'fsdp')
- out_bias_gradient: float32 [1, 768], P(None, 'fsdp')
- second_gain_gradient: float32 [1, 768], P(None, 'fsdp')
- second_bias_gradient: float32 [1, 768], P(None, 'fsdp')
- up_weight_gradient: float32 [1, 768, 3072], P(None, 'fsdp')
- up_bias_gradient: float32 [1, 3072], P(None, 'fsdp')
- down_weight_gradient: float32 [1, 3072, 768], P(None, 'fsdp')
- down_bias_gradient: float32 [1, 768], P(None, 'fsdp')
The draws below stay inside these ranges and needn't reach their ends.
All inputs are finite; a program needn't handle non-finite values.
Results may differ from the reference program's by a relative error of at most 0.012.
The reference program's roundings to bfloat16 on the way count: a program that leaves them out, or rounds other values in their place, can miss the bound.
Values may be sent and summed in bfloat16 or wider, within the bound.
A program may use at most 128 MiB of HBM per device.

```python
import jax
import jax.numpy as jnp
from jax import lax

D = 768
HEAD_DIM = 64
FF = 3072
LAYERS = 1
FRAMES = 256
CLIPS = 16


def strengthened(array, key, source, target, shards_of, factor):
    owner, partner = [(jnp.arange(array.shape[position]) // (array.shape[position] // shards_of)).reshape([-1 if axis == position else 1 for axis in range(array.ndim)]) for position in (source, target)]
    chosen = jax.random.permutation(key, shards_of)[partner]
    strong = (owner == chosen) | (owner == (partner + shards_of // 2) % shards_of)
    return jnp.where(strong, factor * array, array)


def block_levels(own_key, extent, pieces, least, largest):
    def one(axis_at, blocks):
        heights = jax.random.uniform(jax.random.fold_in(jax.random.fold_in(own_key, 6), axis_at), (blocks,), jnp.float32, least / len(pieces), largest / len(pieces))
        return jnp.repeat(jnp.exp(heights), extent[axis_at] // blocks).reshape((-1,) + (1,) * (len(extent) - axis_at - 1))

    level = one(*pieces[0])
    for cut in pieces[1:]:
        level = level * one(*cut)
    return level


def normal_values(key, dims, width, most, cuts=(), kind=jnp.bfloat16):
    factor_of = block_levels(key, dims, cuts, -0.22, 0.18) if cuts else 1.0
    drawn = jax.random.normal(key, dims, jnp.float32) * width * factor_of
    return jnp.minimum(jnp.maximum(drawn, -most), most).astype(kind)


def heavy_noise(key, extent, scale, limit, split, heavy, kind=jnp.bfloat16):
    array = scale * jax.random.normal(key, extent, jnp.float32)
    if split:
        array = array * block_levels(key, extent, split, -0.22, 0.18)
    return jnp.clip(strengthened(array, jax.random.fold_in(key, 3), *heavy), -limit, limit).astype(kind)


def setup_inputs(seed: int = 0) -> dict:
    splits = jax.random.split(jax.random.key(seed), 18)
    return {
        "frames_in": normal_values(splits[0], (CLIPS, FRAMES, D), 1.0, 6.0, ((0, 16), (1, 2)), jnp.float32),
        "cotangent": heavy_noise(splits[1], (CLIPS, FRAMES, D), 1.0, 6.0, ((0, 16), (1, 2)), (0, 2, 16, 2.0), jnp.float32),
        "first_gain": jnp.clip(1.0 + 0.18 * jax.random.normal(splits[2], (LAYERS, D), jnp.float32), 0.099609375, 1.8984375).astype(jnp.bfloat16),
        "first_bias": normal_values(splits[3], (LAYERS, D), 0.5, 3.0, ((1, 16),)),
        "query_weight": normal_values(splits[4], (LAYERS, D, D), D ** -0.5, 0.21875, ((1, 16),)),
        "query_bias": normal_values(splits[5], (LAYERS, D), 0.5, 3.0, ((1, 16),)),
        "key_weight": normal_values(splits[6], (LAYERS, D, D), D ** -0.5, 0.21875, ((1, 16),)),
        "value_weight": normal_values(splits[7], (LAYERS, D, D), D ** -0.5, 0.21875, ((1, 16),)),
        "value_bias": normal_values(splits[8], (LAYERS, D), 0.5, 3.0, ((1, 16),)),
        "out_weight": normal_values(splits[9], (LAYERS, D, D), (max(1, D // FRAMES)) ** -0.5, 3.5, ((1, 16),)),
        "out_bias": normal_values(splits[10], (LAYERS, D), 0.5, 3.0, ((1, 16),)),
        "second_gain": jnp.clip(1.0 + 0.18 * jax.random.normal(splits[11], (LAYERS, D), jnp.float32), 0.099609375, 1.8984375).astype(jnp.bfloat16),
        "second_bias": normal_values(splits[12], (LAYERS, D), 0.5, 3.0, ((1, 16),)),
        "up_weight": normal_values(splits[13], (LAYERS, D, FF), D ** -0.5, 0.21875, ((1, 16),)),
        "up_bias": normal_values(splits[14], (LAYERS, FF), 0.5, 3.0, ((1, 16),)),
        "down_weight": normal_values(splits[15], (LAYERS, FF, D), FF ** -0.5, 0.109375, ((1, 16),)),
        "down_bias": normal_values(splits[16], (LAYERS, D), 0.5, 3.0, ((1, 16),)),
    }


EPSILON = 1e-05
ROOT_HALF = 0.7071067811865476
INV_ROOT_TAU = 0.3989422804014327

def matmul(left, right):
    return jnp.dot(left, right, preferred_element_type=jnp.float32)

def contract_rows(left, right):
    return lax.dot_general(left, right, (((0,), (0,)), ((), ())), preferred_element_type=jnp.float32)

def contract_cols(left, right):
    return lax.dot_general(left, right, (((1,), (1,)), ((), ())), preferred_element_type=jnp.float32)

def round_low(values):
    return lax.optimization_barrier(values.astype(jnp.bfloat16))

def layer_norm(residual, gain, offset):
    centre = residual - lax.optimization_barrier(jnp.mean(residual, axis=-1, keepdims=True))
    inv_std = lax.rsqrt(lax.optimization_barrier(jnp.mean(centre * centre, axis=-1, keepdims=True)) + EPSILON)
    normed = centre * inv_std
    return (normed * gain.astype(jnp.float32) + offset.astype(jnp.float32), normed, inv_std)

def norm_grad(upstream, normed, inv_std, gain):
    scaled = upstream * gain.astype(jnp.float32)
    spread = scaled - lax.optimization_barrier(jnp.mean(scaled, axis=-1, keepdims=True))
    return (spread - normed * lax.optimization_barrier(jnp.mean(scaled * normed, axis=-1, keepdims=True))) * inv_std

def gelu_exact(pre_act):
    return 0.5 * pre_act * (1.0 + lax.erf(pre_act * ROOT_HALF))

def gelu_slope(pre_act):
    return 0.5 * (1.0 + lax.erf(pre_act * ROOT_HALF)) + pre_act * jnp.exp(-0.5 * pre_act * pre_act) * INV_ROOT_TAU

def split_heads(rows):
    return rows.astype(jnp.float32).reshape(rows.shape[0], rows.shape[1] // HEAD_DIM, HEAD_DIM)

def attend(query_rows, key_rows, value_rows):
    score_scale = HEAD_DIM ** (-0.5)
    query_heads = split_heads(query_rows)
    key_heads = split_heads(key_rows)
    value_heads = split_heads(value_rows)
    scores = jnp.einsum('qhd,khd->hqk', query_heads, key_heads) * score_scale
    row_top = lax.optimization_barrier(jnp.max(scores, axis=-1, keepdims=True))
    log_total = row_top + jnp.log(lax.optimization_barrier(jnp.sum(jnp.exp(scores - row_top), axis=-1, keepdims=True)))
    weights_low = round_low(jnp.exp(scores - log_total))
    context = jnp.einsum('hqk,khd->qhd', weights_low.astype(jnp.float32), value_heads)
    return (round_low(context.reshape(query_rows.shape)), log_total)

def attend_back(query_rows, key_rows, value_rows, log_total, context_gradient):
    score_scale = HEAD_DIM ** (-0.5)
    row_shape = query_rows.shape
    query_heads = split_heads(query_rows)
    key_heads = split_heads(key_rows)
    value_heads = split_heads(value_rows)
    gradient_heads = split_heads(context_gradient)
    scores = jnp.einsum('qhd,khd->hqk', query_heads, key_heads) * score_scale
    weights = jnp.exp(scores - log_total)
    weights_low = round_low(weights)
    value_gradient = jnp.einsum('hqk,qhd->khd', weights_low.astype(jnp.float32), gradient_heads)
    prob_gradient = jnp.einsum('qhd,khd->hqk', gradient_heads, value_heads)
    score_gradient = round_low(weights * (prob_gradient - lax.optimization_barrier(jnp.sum(weights * prob_gradient, axis=-1, keepdims=True))) * score_scale)
    score_wide = score_gradient.astype(jnp.float32)
    query_gradient = jnp.einsum('hqk,khd->qhd', score_wide, key_heads)
    key_gradient = jnp.einsum('hqk,qhd->khd', score_wide, query_heads)
    return (round_low(query_gradient.reshape(row_shape)), round_low(key_gradient.reshape(row_shape)), round_low(value_gradient.reshape(row_shape)))

def forward_layer(residual, params):
    hidden_wide, normed_in, inv_in = layer_norm(residual, params[0], params[1])
    hidden = round_low(hidden_wide)
    query_rows = round_low(matmul(hidden, params[2]) + params[3].astype(jnp.float32))
    key_rows = round_low(matmul(hidden, params[4]))
    value_rows = round_low(matmul(hidden, params[5]) + params[6].astype(jnp.float32))
    context, log_total = attend(query_rows, key_rows, value_rows)
    middle = residual + matmul(context, params[7]) + params[8].astype(jnp.float32)
    mid_wide, normed_mid, inv_mid = layer_norm(middle, params[9], params[10])
    hidden_mid = round_low(mid_wide)
    pre_act = matmul(hidden_mid, params[11]) + params[12].astype(jnp.float32)
    activated = round_low(gelu_exact(pre_act))
    result = middle + matmul(activated, params[13]) + params[14].astype(jnp.float32)
    return (result, (hidden, normed_in, inv_in, query_rows, key_rows, value_rows, log_total, context, normed_mid, inv_mid, hidden_mid, pre_act, activated))

def backward_layer(upstream, stored, params):
    hidden, normed_in, inv_in, query_rows, key_rows, value_rows, log_total, context, normed_mid, inv_mid, hidden_mid, pre_act, activated = stored
    upstream_low = round_low(upstream)
    down_weight_gradient = contract_rows(activated, upstream_low)
    down_bias_gradient = lax.optimization_barrier(jnp.sum(upstream, axis=0))
    pre_gradient = contract_cols(upstream_low, params[13]) * gelu_slope(pre_act)
    pre_low = round_low(pre_gradient)
    up_weight_gradient = contract_rows(hidden_mid, pre_low)
    up_bias_gradient = lax.optimization_barrier(jnp.sum(pre_gradient, axis=0))
    mid_hidden_gradient = contract_cols(pre_low, params[11])
    second_gain_gradient = lax.optimization_barrier(jnp.sum(mid_hidden_gradient * normed_mid, axis=0))
    second_bias_gradient = lax.optimization_barrier(jnp.sum(mid_hidden_gradient, axis=0))
    middle_gradient = upstream + norm_grad(mid_hidden_gradient, normed_mid, inv_mid, params[9])
    middle_low = round_low(middle_gradient)
    out_weight_gradient = contract_rows(context, middle_low)
    out_bias_gradient = lax.optimization_barrier(jnp.sum(middle_gradient, axis=0))
    context_gradient = round_low(contract_cols(middle_low, params[7]))
    query_gradient, key_gradient, value_gradient = attend_back(query_rows, key_rows, value_rows, log_total, context_gradient)
    query_weight_gradient = contract_rows(hidden, query_gradient)
    query_bias_gradient = lax.optimization_barrier(jnp.sum(query_gradient.astype(jnp.float32), axis=0))
    key_weight_gradient = contract_rows(hidden, key_gradient)
    value_weight_gradient = contract_rows(hidden, value_gradient)
    value_bias_gradient = lax.optimization_barrier(jnp.sum(value_gradient.astype(jnp.float32), axis=0))
    hidden_gradient = contract_cols(query_gradient, params[2]) + contract_cols(key_gradient, params[4]) + contract_cols(value_gradient, params[5])
    first_gain_gradient = lax.optimization_barrier(jnp.sum(hidden_gradient * normed_in, axis=0))
    first_bias_gradient = lax.optimization_barrier(jnp.sum(hidden_gradient, axis=0))
    input_gradient = middle_gradient + norm_grad(hidden_gradient, normed_in, inv_in, params[0])
    return (input_gradient, (first_gain_gradient, first_bias_gradient, query_weight_gradient, query_bias_gradient, key_weight_gradient, value_weight_gradient, value_bias_gradient, out_weight_gradient, out_bias_gradient, second_gain_gradient, second_bias_gradient, up_weight_gradient, up_bias_gradient, down_weight_gradient, down_bias_gradient))

def reference(frames_in, cotangent, first_gain, first_bias, query_weight, query_bias, key_weight, value_weight, value_bias, out_weight, out_bias, second_gain, second_bias, up_weight, up_bias, down_weight, down_bias):
    stacks = (first_gain, first_bias, query_weight, query_bias, key_weight, value_weight, value_bias, out_weight, out_bias, second_gain, second_bias, up_weight, up_bias, down_weight, down_bias)

    def per_clip(totals, clip_pair):
        residual, upstream = clip_pair
        stored_all = []
        for layer_num in range(LAYERS):
            params = tuple((stack[layer_num] for stack in stacks))
            residual, stored = forward_layer(residual, params)
            stored_all.append(stored)
        layer_grads = [None] * LAYERS
        for layer_num in reversed(range(LAYERS)):
            params = tuple((stack[layer_num] for stack in stacks))
            upstream, gradients = backward_layer(upstream, stored_all[layer_num], params)
            layer_grads[layer_num] = gradients
        summed = tuple((totals[member] + jnp.stack([layer_grads[layer_num][member] for layer_num in range(LAYERS)]) for member in range(len(stacks))))
        return (summed, (residual, upstream))
    zeros = tuple((jnp.zeros(stack.shape, jnp.float32) for stack in stacks))
    totals, finals = lax.scan(per_clip, zeros, (frames_in, cotangent))
    return (finals[0], finals[1], totals[0], totals[1], totals[2], totals[3], totals[4], totals[5], totals[6], totals[7], totals[8], totals[9], totals[10], totals[11], totals[12], totals[13], totals[14])
```

```python
import functools

import jax
import jax.numpy as jnp
from jax import lax
from jax.experimental import pallas as pl
from jax.experimental.pallas import tpu as pltpu
from jax.sharding import PartitionSpec as P

HEAD_DIM = 64


EPSILON = 1e-05
ROOT_HALF = 0.7071067811865476
INV_ROOT_TAU = 0.3989422804014327


def matmul(left, right):
    return jnp.dot(left, right, preferred_element_type=jnp.float32)


def contract_rows(left, right):
    return lax.dot_general(
        left, right, (((0,), (0,)), ((), ())), preferred_element_type=jnp.float32
    )


def contract_cols(left, right):
    return lax.dot_general(
        left, right, (((1,), (1,)), ((), ())), preferred_element_type=jnp.float32
    )


def layer_norm(residual, gain, offset):
    centre = residual - jnp.mean(residual, axis=-1, keepdims=True)
    inv_std = lax.rsqrt(jnp.mean(centre * centre, axis=-1, keepdims=True) + EPSILON)
    normed = centre * inv_std
    return (normed * gain.astype(jnp.float32) + offset.astype(jnp.float32), normed, inv_std)


def norm_grad(upstream, normed, inv_std, gain):
    scaled = upstream * gain.astype(jnp.float32)
    spread = scaled - jnp.mean(scaled, axis=-1, keepdims=True)
    return (spread - normed * jnp.mean(scaled * normed, axis=-1, keepdims=True)) * inv_std


def gelu_exact(pre_act):
    return 0.5 * pre_act * (1.0 + lax.erf(pre_act * ROOT_HALF))


def gelu_slope(pre_act):
    return (
        0.5 * (1.0 + lax.erf(pre_act * ROOT_HALF))
        + pre_act * jnp.exp(-0.5 * pre_act * pre_act) * INV_ROOT_TAU
    )


def split_heads(rows):
    return rows.reshape(rows.shape[0], rows.shape[1] // HEAD_DIM, HEAD_DIM)


def attend(query_rows, key_rows, value_rows):
    score_scale = HEAD_DIM ** (-0.5)
    query_heads = split_heads(query_rows)
    key_heads = split_heads(key_rows)
    value_heads = split_heads(value_rows)
    scores = (
        jnp.einsum("qhd,khd->hqk", query_heads, key_heads, preferred_element_type=jnp.float32)
        * score_scale
    )
    row_top = jnp.max(scores, axis=-1, keepdims=True)
    log_total = row_top + jnp.log(jnp.sum(jnp.exp(scores - row_top), axis=-1, keepdims=True))
    weights = jnp.exp(scores - log_total)
    context = jnp.einsum(
        "hqk,khd->qhd",
        weights.astype(jnp.bfloat16),
        value_heads,
        preferred_element_type=jnp.float32,
    )
    return (context.reshape(query_rows.shape).astype(jnp.bfloat16), weights)


def attend_back(query_rows, key_rows, value_rows, weights, context_gradient):
    score_scale = HEAD_DIM ** (-0.5)
    row_shape = query_rows.shape
    query_heads = split_heads(query_rows)
    key_heads = split_heads(key_rows)
    value_heads = split_heads(value_rows)
    gradient_heads = split_heads(context_gradient)
    value_gradient = jnp.einsum(
        "hqk,qhd->khd",
        weights.astype(jnp.bfloat16),
        gradient_heads,
        preferred_element_type=jnp.float32,
    )
    prob_gradient = jnp.einsum(
        "qhd,khd->hqk", gradient_heads, value_heads, preferred_element_type=jnp.float32
    )
    score_gradient = (
        weights
        * (prob_gradient - jnp.sum(weights * prob_gradient, axis=-1, keepdims=True))
        * score_scale
    ).astype(jnp.bfloat16)
    query_gradient = jnp.einsum(
        "hqk,khd->qhd", score_gradient, key_heads, preferred_element_type=jnp.float32
    )
    key_gradient = jnp.einsum(
        "hqk,qhd->khd", score_gradient, query_heads, preferred_element_type=jnp.float32
    )
    return tuple(
        part.reshape(row_shape).astype(jnp.bfloat16)
        for part in (query_gradient, key_gradient, value_gradient)
    )


VECTORS = (0, 1, 3, 6, 8, 9, 10, 12, 14)
MATRICES = (2, 4, 5, 7, 11, 13)
PAD_ROWS = 16


def cut_columns(rows, width):
    blocks = rows.shape[-1] // width
    if blocks == 1:
        return rows
    return jnp.concatenate(
        [rows[..., i * width : (i + 1) * width] for i in range(blocks)], axis=-2
    )


def join_columns(rows, blocks):
    if blocks == 1:
        return rows
    size = rows.shape[-2] // blocks
    return jnp.concatenate(
        [rows[..., i * size : (i + 1) * size, :] for i in range(blocks)], axis=-1
    )


def gather_layer(shards, width):
    pieces = [cut_columns(shards[i], width) for i in MATRICES]
    vector = jnp.concatenate([shards[i] for i in VECTORS])
    vector = jnp.pad(vector, (0, PAD_ROWS * width - vector.shape[0]))
    pieces.append(vector.reshape(PAD_ROWS, width))
    packed = lax.all_gather(jnp.concatenate(pieces, axis=0), "fsdp", axis=0, tiled=False)
    params = [None] * len(shards)
    start = 0
    for i in MATRICES:
        blocks = shards[i].shape[1] // width
        size = shards[i].shape[0] * blocks
        part = join_columns(packed[:, start : start + size], blocks)
        params[i] = part.reshape(-1, shards[i].shape[1])
        start += size
    vectors = packed[:, start:].reshape(packed.shape[0], -1)
    start = 0
    for i in VECTORS:
        size = shards[i].shape[0]
        params[i] = vectors[:, start : start + size].reshape(-1)
        start += size
    return params


def reduce_gradients(gradients, shards, width, seq_size, seq_index, fsdp_size):
    part_width = width // seq_size
    pieces = []
    for i in MATRICES:
        blocks = shards[i].shape[1] // width
        rows = gradients[i].astype(jnp.bfloat16)
        rows = rows.reshape(fsdp_size, shards[i].shape[0], rows.shape[1])
        pieces.append(cut_columns(rows, part_width))
    vector = jnp.concatenate(
        [gradients[i].reshape(fsdp_size, -1) for i in VECTORS], axis=1
    ).astype(jnp.bfloat16)
    vector = jnp.pad(vector, ((0, 0), (0, PAD_ROWS * width - vector.shape[1])))
    vector = vector.reshape(fsdp_size, PAD_ROWS * seq_size, part_width)
    pieces.append(lax.dynamic_slice_in_dim(vector, seq_index * PAD_ROWS, PAD_ROWS, axis=1))
    packed = jnp.concatenate(pieces, axis=1)
    mine = lax.psum_scatter(packed, "fsdp", scatter_dimension=0, tiled=False)
    both = lax.all_gather(mine, "seq", axis=0, tiled=False)
    reduced = [None] * len(shards)
    start = 0
    for i in MATRICES:
        blocks = shards[i].shape[1] // width
        size = shards[i].shape[0] * blocks
        part = join_columns(both[:, start : start + size], blocks)
        whole = jnp.concatenate([part[s] for s in range(seq_size)], axis=-1)
        reduced[i] = whole.astype(jnp.float32)[None]
        start += size
    vector = both[:, start:].reshape(-1).astype(jnp.float32)
    start = 0
    for i in VECTORS:
        size = shards[i].shape[0]
        reduced[i] = vector[start : start + size][None]
        start += size
    return reduced


def on_device(frames_in, cotangent, *stacks):
    width = frames_in.shape[2]
    seq_size = lax.axis_size("seq")
    seq_index = lax.axis_index("seq")
    fsdp_size = lax.axis_size("fsdp")
    shards = [stack[0] for stack in stacks]
    own = frames_in.shape[1]

    mine = jnp.stack([frames_in[0], cotangent[0]])
    if seq_size == 2:
        other = lax.ppermute(mine, "seq", [(0, 1), (1, 0)])
        first = seq_index == 0
        rows = jnp.concatenate(
            [jnp.where(first, mine, other), jnp.where(first, other, mine)], axis=1
        )
    else:
        rows = lax.all_gather(mine, "seq", axis=1, tiled=True)
    residual, upstream = rows[0], rows[1]
    params = gather_layer(shards, width)

    def own_columns(matrix):
        size = matrix.shape[1] // seq_size
        return lax.dynamic_slice_in_dim(matrix, seq_index * size, size, axis=1)

    def own_rows(matrix):
        return lax.dynamic_slice_in_dim(matrix, seq_index * own, own, axis=0)[None]

    wide = [None if i in MATRICES else p.astype(jnp.float32) for i, p in enumerate(params)]

    hidden_wide, normed_in, inv_in = layer_norm(residual, params[0], params[1])
    hidden = hidden_wide.astype(jnp.bfloat16)
    query_rows = (matmul(hidden, params[2]) + wide[3]).astype(jnp.bfloat16)
    key_rows = matmul(hidden, params[4]).astype(jnp.bfloat16)
    value_rows = (matmul(hidden, params[5]) + wide[6]).astype(jnp.bfloat16)
    context, weights = attend(query_rows, key_rows, value_rows)
    middle = residual + matmul(context, params[7]) + wide[8]
    mid_wide, normed_mid, inv_mid = layer_norm(middle, params[9], params[10])
    hidden_mid = mid_wide.astype(jnp.bfloat16)
    pre_act = matmul(hidden_mid, params[11]) + wide[12]
    activated = gelu_exact(pre_act).astype(jnp.bfloat16)
    own_activated = own_rows(activated)[0]
    outputs = own_rows(middle)[0] + matmul(own_activated, params[13]) + wide[14]

    gradients = [None] * len(stacks)
    upstream_low = upstream.astype(jnp.bfloat16)
    gradients[13] = contract_rows(activated, own_columns(upstream_low))
    gradients[14] = jnp.sum(upstream, axis=0)
    pre_gradient = contract_cols(upstream_low, params[13]) * gelu_slope(pre_act)
    pre_low = pre_gradient.astype(jnp.bfloat16)
    gradients[11] = contract_rows(hidden_mid, own_columns(pre_low))
    gradients[12] = jnp.sum(pre_gradient, axis=0)
    mid_hidden_gradient = contract_cols(pre_low, params[11])
    gradients[9] = jnp.sum(mid_hidden_gradient * normed_mid, axis=0)
    gradients[10] = jnp.sum(mid_hidden_gradient, axis=0)
    middle_gradient = upstream + norm_grad(mid_hidden_gradient, normed_mid, inv_mid, params[9])
    middle_low = middle_gradient.astype(jnp.bfloat16)
    gradients[7] = contract_rows(context, own_columns(middle_low))
    gradients[8] = jnp.sum(middle_gradient, axis=0)
    context_gradient = contract_cols(middle_low, params[7]).astype(jnp.bfloat16)
    query_gradient, key_gradient, value_gradient = attend_back(
        query_rows, key_rows, value_rows, weights, context_gradient
    )
    gradients[2] = contract_rows(hidden, own_columns(query_gradient))
    gradients[3] = jnp.sum(query_gradient.astype(jnp.float32), axis=0)
    gradients[4] = contract_rows(hidden, own_columns(key_gradient))
    gradients[5] = contract_rows(hidden, own_columns(value_gradient))
    gradients[6] = jnp.sum(value_gradient.astype(jnp.float32), axis=0)
    hidden_gradient = (
        contract_cols(query_gradient, params[2])
        + contract_cols(key_gradient, params[4])
        + contract_cols(value_gradient, params[5])
    )
    gradients[0] = jnp.sum(hidden_gradient * normed_in, axis=0)
    gradients[1] = jnp.sum(hidden_gradient, axis=0)
    input_gradient = middle_gradient + norm_grad(hidden_gradient, normed_in, inv_in, params[0])
    reduced = reduce_gradients(gradients, shards, width, seq_size, seq_index, fsdp_size)
    return (outputs[None], own_rows(input_gradient), *reduced)


MESH = pl.DeviceIdType.MESH
F32 = jnp.float32
BF16 = jnp.bfloat16


def dot_nt(left, right):
    return lax.dot_general(left, right, (((1,), (1,)), ((), ())), preferred_element_type=F32)


def dot_tn(left, right):
    return lax.dot_general(left, right, (((0,), (0,)), ((), ())), preferred_element_type=F32)


def low(values):
    return values.astype(BF16)


def wide(values):
    return values.astype(F32)


def row_mean(values):
    return jnp.mean(values, axis=-1, keepdims=True)


def column_sum(values):
    return jnp.sum(values, axis=0, keepdims=True)


class Sizes:
    def __init__(self, own, width, hidden, fsdp):
        self.own, self.width, self.hidden, self.fsdp = own, width, hidden, fsdp
        self.frames = 2 * own
        self.half = width // 2
        self.ff = hidden // 2
        self.depth = fsdp // 4
        self.rows = width // fsdp
        self.slab = hidden // fsdp // 2


def encoder_kernel(sz, *refs):
    half, ff, depth, rows, slab = sz.half, sz.ff, sz.depth, sz.rows, sz.slab
    own, frames, width, fsdp = sz.own, sz.frames, sz.width, sz.fsdp
    hops = depth - 1
    (frames_ref, cot_ref, v_fg, v_fb, wq_ref, v_bq, wk_ref, wv_ref, v_bv, wo_ref, v_bo, v_sg, v_sb,
     wu_ref, v_bu, wd_ref, v_bd) = refs[:17]
    (o_out, o_in, o_fg, o_fb, o_wq, o_bq, o_wk, o_wv, o_bv, o_wo, o_bo, o_sg, o_sb, o_wu, o_bu,
     o_wd, o_bd) = refs[17:34]
    (wqkv, wo, wup, wdown, vecg, vfull, bup, rbuf, gbuf, n_in, n_mid, middle, hidden, hmid, stat_in,
     stat_mid, qkv, prob, cbuf, act, slope, plow, mg, upl, mlow, cg, dqkv, mh_part, mh_send, mh_recv, op_part,
     op_send, op_recv, hg_part, hg_send, hg_recv,
     g_d, s_d, t_d, y_d, zs_d, zr_d, xs_d, xr_d, f_d,
     g_u, s_u, t_u, y_u, zs_u, zr_u, xs_u, xr_u, f_u,
     g_o, s_o, t_o, y_o, zs_o, zr_o, xs_o, xr_o, f_o,
     g_q, s_q, t_q, y_q, zs_q, zr_q, xs_q, xr_q, f_q,
     v0, v1, v2, v3, vs, vy, vz, vx,
     local_sem, ag_send, ag_recv, rs_send, rs_recv, x_send, x_recv) = refs[34:]

    x = lax.axis_index("seq")
    i = lax.axis_index("fsdp")
    z, y, c = i // 4, lax.rem(i // 2, 2), lax.rem(i, 2)

    def at(z_at, y_at, c_at):
        return (x, z_at * 4 + y_at * 2 + c_at)

    sib, ypeer, xpeer = at(z, y, 1 - c), at(z, 1 - y, c), (1 - x, i)
    zother = [lax.rem(z + d, depth) for d in range(1, depth)]
    zpeers = [at(other, y, c) for other in zother]
    mine = pl.multiple_of(x * half, 128)
    theirs = pl.multiple_of((1 - x) * half, 128)

    local = [
        pltpu.make_async_copy(wq_ref.at[:, pl.ds(mine, half)], wqkv.at[0, i], local_sem.at[0]),
        pltpu.make_async_copy(wk_ref.at[:, pl.ds(mine, half)], wqkv.at[1, i], local_sem.at[1]),
        pltpu.make_async_copy(wv_ref.at[:, pl.ds(mine, half)], wqkv.at[2, i], local_sem.at[2]),
        pltpu.make_async_copy(wo_ref, wo.at[i], local_sem.at[3]),
        pltpu.make_async_copy(wd_ref.at[pl.ds(pl.multiple_of(x * slab, 16), slab)], wdown.at[i], local_sem.at[4]),
        pltpu.make_async_copy(frames_ref, rbuf.at[x], local_sem.at[5]),
        pltpu.make_async_copy(cot_ref, gbuf.at[x], local_sem.at[6]),
    ]
    for copy in local:
        copy.start()

    barrier = pltpu.get_barrier_semaphore()
    partners = [sib, ypeer, xpeer, *zpeers]
    for partner in partners:
        pl.semaphore_signal(barrier, inc=1, device_id=partner, device_id_type=MESH)

    vecg[i] = jnp.zeros(vecg.shape[1:], F32)
    for at_row, ref in enumerate((v_fg, v_fb, v_bq, v_bv, v_bo, v_sg, v_sb, v_bd)):
        vecg[i, at_row : at_row + 1, 0:rows] = wide(ref[...])
    up_bias = wide(v_bu[...])
    vecg[i, 8:9, 0:slab] = up_bias[:, :slab]
    vecg[i, 9:10, 0:slab] = up_bias[:, slab:]

    pl.semaphore_wait(barrier, len(partners))

    started = []

    def send(src, dst, send_sem, recv_sem, to):
        copy = pltpu.make_async_remote_copy(
            src_ref=src, dst_ref=dst, send_sem=send_sem, recv_sem=recv_sem, device_id=to, device_id_type=MESH
        )
        copy.start()
        started.append(copy)

    def arrived(dst, recv_sem):
        pltpu.make_async_remote_copy(
            src_ref=dst, dst_ref=dst, send_sem=recv_sem, recv_sem=recv_sem, device_id=xpeer, device_id_type=MESH
        ).wait_recv()

    def block(piece, b):
        return (wqkv.at[:, b], vecg.at[b], wo.at[b], wup.at[b], wdown.at[b])[piece]

    def pass_on(piece, b, slot, to):
        send(block(piece, b), block(piece, b), ag_send.at[piece, slot], ag_recv.at[piece, b], to)

    def send_own(piece):
        for n, to in enumerate(zpeers):
            pass_on(piece, i, n, to)
        pass_on(piece, i, hops, ypeer)
        pass_on(piece, i, hops + 1, sib)

    def relay_z(piece):
        for n, other in enumerate(zother):
            b = other * 4 + y * 2 + c
            arrived(block(piece, b), ag_recv.at[piece, b])
            pass_on(piece, b, hops + 2 + n, ypeer)
            pass_on(piece, b, 2 * hops + 2 + n, sib)

    def relay_y(piece):
        for n in range(depth):
            b = lax.rem(z + n, depth) * 4 + (1 - y) * 2 + c
            arrived(block(piece, b), ag_recv.at[piece, b])
            pass_on(piece, b, 3 * hops + 2 + n, sib)

    def finish(piece):
        for k in range(2 * depth):
            b = 2 * k + (1 - c)
            arrived(block(piece, b), ag_recv.at[piece, b])

    for n in range(3):
        local[n].wait()
    send_own(0)
    send_own(1)
    local[5].wait()
    send(rbuf.at[x], rbuf.at[x], x_send.at[0], x_recv.at[0], xpeer)
    local[3].wait()
    send_own(2)
    local[6].wait()
    send(gbuf.at[x], gbuf.at[x], x_send.at[1], x_recv.at[1], xpeer)
    up = wide(wu_ref[...])
    picked = []
    for b in range(fsdp):
        left = up[:, 2 * slab * b : 2 * slab * b + slab]
        right = up[:, 2 * slab * b + slab : 2 * slab * (b + 1)]
        picked.append(jnp.where(x == 0, left, right))
    wup[i] = low(jnp.concatenate(picked, axis=1))
    local[4].wait()

    relay_z(0)
    relay_z(1)
    send_own(3)
    relay_y(0)
    relay_y(1)
    relay_z(2)
    send_own(4)
    finish(1)
    for b in range(fsdp):
        vfull[:, rows * b : rows * (b + 1)] = vecg[b, 0:8, 0:rows]
        bup[:, slab * b : slab * (b + 1)] = jnp.where(x == 0, vecg[b, 8:9, 0:slab], vecg[b, 9:10, 0:slab])
    v0[...] = jnp.zeros_like(v0)

    step = own // 2

    def by_rows(body):
        def one(n, carry):
            s = n // 2
            r0 = pl.multiple_of(lax.rem(n, 2) * step, step)
            body(s, pl.ds(r0, step), pl.ds(pl.multiple_of(n * step, step), step))
            return carry

        lax.fori_loop(0, 4, one, 0)

    arrived(rbuf.at[1 - x], x_recv.at[0])

    def norm_first(s, part, whole):
        r = rbuf[s, part, :]
        centre = r - row_mean(r)
        inv = lax.rsqrt(row_mean(centre * centre) + EPSILON)
        normed = centre * inv
        n_in[s, part, :] = normed
        stat_in[s, part, :] = jnp.broadcast_to(inv, (step, 128))
        hidden[whole, :] = low(normed * vfull[0:1, :] + vfull[1:2, :])

    by_rows(norm_first)
    finish(0)
    for m, bias in ((0, 2), (1, None), (2, 3)):
        made = jnp.dot(hidden[...], wqkv[m].reshape(width, half), preferred_element_type=F32)
        if bias is not None:
            made = made + vfull[bias : bias + 1, pl.ds(mine, half)]
        qkv[m] = low(made)
    relay_y(2)

    first_lane = lax.broadcasted_iota(jnp.int32, (frames, 2 * HEAD_DIM), 1) < HEAD_DIM
    scale = HEAD_DIM**-0.5

    def masked(pair, which):
        keep = first_lane if which == 0 else jnp.logical_not(first_lane)
        return jnp.where(keep, pair, jnp.zeros_like(pair))

    for pair in range(half // (2 * HEAD_DIM)):
        lanes = slice(pair * 2 * HEAD_DIM, (pair + 1) * 2 * HEAD_DIM)
        q2, k2, v2_ = qkv[0, :, lanes], qkv[1, :, lanes], qkv[2, :, lanes]
        parts = []
        for which in range(2):
            scores = dot_nt(masked(q2, which), k2) * scale
            raised = jnp.exp(scores - jnp.max(scores, axis=-1, keepdims=True))
            weights = raised * (1.0 / jnp.sum(raised, axis=-1, keepdims=True))
            prob[2 * pair + which] = weights
            parts.append(jnp.dot(low(weights), v2_, preferred_element_type=F32))
        cbuf[x, :, lanes] = low(jnp.where(first_lane, parts[0], parts[1]))
    send(cbuf.at[x], cbuf.at[x], x_send.at[2], x_recv.at[2], xpeer)
    relay_z(3)
    finish(2)
    arrived(cbuf.at[1 - x], x_recv.at[2])
    context = jnp.concatenate([cbuf[0], cbuf[1]], axis=1)
    for n in range(2):
        cols = slice(n * half, (n + 1) * half)
        made = jnp.dot(context, wo[:, :, cols].reshape(width, half), preferred_element_type=F32)
        made = made + vfull[4:5, cols]
        for s in range(2):
            middle[s, :, cols] = rbuf[s, :, cols] + made[s * own : (s + 1) * own]

    def norm_second(s, part, whole):
        r = middle[s, part, :]
        centre = r - row_mean(r)
        inv = lax.rsqrt(row_mean(centre * centre) + EPSILON)
        normed = centre * inv
        n_mid[s, part, :] = normed
        stat_mid[s, part, :] = jnp.broadcast_to(inv, (step, 128))
        hmid[whole, :] = low(normed * vfull[5:6, :] + vfull[6:7, :])

    by_rows(norm_second)
    relay_y(3)
    arrived(gbuf.at[1 - x], x_recv.at[1])
    for s in range(2):
        upl[s * own : (s + 1) * own, :] = low(gbuf[s])
    v0[7:8, :] = column_sum(gbuf[0]) + column_sum(gbuf[1])
    finish(3)
    relay_z(4)

    chunk = 4 * slab
    chunks = ff // chunk

    def up_chunk(n, carry):
        cols = pl.ds(pl.multiple_of(n * chunk, 128), chunk)
        pre = jnp.dot(hmid[...], wup[:, :, cols].reshape(width, chunk), preferred_element_type=F32)
        pre = pre + bup[:, cols]
        bell = 0.5 * (1.0 + lax.erf(pre * ROOT_HALF))
        act[:, cols] = low(pre * bell)
        slope[:, cols] = bell + pre * jnp.exp(-0.5 * pre * pre) * INV_ROOT_TAU
        return carry

    lax.fori_loop(0, chunks, up_chunk, 0)
    relay_y(4)
    finish(4)

    def back_chunk(n, carry):
        cols = pl.ds(pl.multiple_of(n * chunk, 128), chunk)
        rhs = wdown[pl.ds(n * 4, 4)].reshape(chunk, width)
        pg = dot_nt(upl[...], rhs) * slope[:, cols]
        plow[:, cols] = low(pg)
        bup_sum[:, cols] = column_sum(pg)
        return carry

    bup_sum = bup
    lax.fori_loop(0, chunks, back_chunk, 0)
    for n in range(2):
        cols = slice(n * half, (n + 1) * half)
        made = dot_nt(plow[...], wup[n * fsdp // 2 : (n + 1) * fsdp // 2].reshape(half, ff))
        mh_part[:, cols] = made
        mh_send[:, cols] = low(made)
    send(mh_send, mh_recv, x_send.at[3], x_recv.at[3], xpeer)

    pieces = {
        "d": (0, g_d, s_d, t_d, y_d, zs_d, zr_d, xs_d, xr_d, f_d),
        "u": (1, g_u, s_u, t_u, y_u, zs_u, zr_u, xs_u, xr_u, f_u),
        "o": (2, g_o, s_o, t_o, y_o, zs_o, zr_o, xs_o, xr_o, f_o),
        "q": (3, g_q, s_q, t_q, y_q, zs_q, zr_q, xs_q, xr_q, f_q),
    }

    def reduce_core(name):
        at_piece, g, s_ = pieces[name][:3]
        send(g.at[:, :, 1 - c], s_, rs_send.at[at_piece, 0], rs_recv.at[at_piece, 0], sib)

    def reduce_y(name):
        at_piece, g, s_, t, yb = pieces[name][:5]
        arrived(s_, rs_recv.at[at_piece, 0])

        def one(n, carry):
            t[n] = low(wide(g[n, 1 - y, c]) + wide(s_[n, 1 - y]))
            return carry

        lax.fori_loop(0, depth, one, 0)
        send(t, yb, rs_send.at[at_piece, 1], rs_recv.at[at_piece, 1], ypeer)

    def reduce_z(name):
        at_piece, g, s_, t, yb, zs, zr, xs, xr, fin = pieces[name]
        arrived(yb, rs_recv.at[at_piece, 1])
        for n, other in enumerate(zother):
            zs[n] = low(wide(g[other, y, c]) + wide(s_[other, y]) + wide(yb[other]))
            send(zs.at[n], zr.at[hops - 1 - n], rs_send.at[at_piece, 2 + n],
                 rs_recv.at[at_piece, 2 + hops - 1 - n], zpeers[n])
        fin[...] = wide(g[z, y, c]) + wide(s_[z, y]) + wide(yb[z])

    def reduce_x(name):
        at_piece, g, s_, t, yb, zs, zr, xs, xr, fin = pieces[name]
        total = fin[...]
        for n in range(hops):
            arrived(zr.at[n], rs_recv.at[at_piece, 2 + n])
            total = total + wide(zr[n])
        fin[...] = total
        xs[...] = low(total)
        send(xs, xr, rs_send.at[at_piece, 2 + hops], rs_recv.at[at_piece, 2 + hops], xpeer)

    def reduced(name):
        at_piece, g, s_, t, yb, zs, zr, xs, xr, fin = pieces[name]
        arrived(xr, rs_recv.at[at_piece, 2 + hops])
        return fin, xr

    def down_chunk(n, carry):
        cols = pl.ds(pl.multiple_of(n * chunk, 128), chunk)
        made = low(dot_tn(act[:, cols], upl[...]))
        g_d[n] = made.reshape(2, 2, slab, width)
        return carry

    lax.fori_loop(0, chunks, down_chunk, 0)
    reduce_core("d")

    def up_back(n, carry):
        cols = pl.ds(pl.multiple_of(n * chunk, 128), chunk)
        made = low(dot_tn(hmid[...], plow[:, cols]))
        g_u[:, :, :, :, cols] = made.reshape(depth, 2, 2, rows, chunk)
        return carry

    lax.fori_loop(0, chunks, up_back, 0)
    reduce_core("u")
    reduce_y("d")

    for n in range(2):
        cols = slice(n * half, (n + 1) * half)
        made = jnp.dot(act[...], wdown[:, :, cols].reshape(ff, half), preferred_element_type=F32)
        for s in range(2):
            op_part[s, :, cols] = made[s * own : (s + 1) * own]
    op_send[...] = low(op_part[1 - x])
    send(op_send, op_recv, x_send.at[4], x_recv.at[4], xpeer)
    reduce_y("u")

    arrived(mh_recv, x_recv.at[3])
    only = jnp.where(x == 0, 1.0, 0.0)

    def norm_second_back(s, part, whole):
        total = mh_part[whole, :] + wide(mh_recv[whole, :])
        normed = n_mid[s, part, :]
        v0[5:6, :] += only * column_sum(total * normed)
        v0[6:7, :] += only * column_sum(total)
        scaled = total * vfull[5:6, :]
        spread = scaled - row_mean(scaled) - normed * row_mean(scaled * normed)
        made = gbuf[s, part, :] + spread * stat_mid[s, part, 0:1]
        mg[s, part, :] = made
        mlow[whole, :] = low(made)
        v0[4:5, :] += only * column_sum(made)

    by_rows(norm_second_back)
    v0[7:8, :] = only * v0[7:8, :]
    cg[...] = low(dot_nt(mlow[...], wo[pl.ds(x * (fsdp // 2), fsdp // 2)].reshape(half, width)))
    reduce_z("d")
    for n in range(2):
        made = low(dot_tn(cbuf[n], mlow[:, pl.ds(mine, half)]))
        g_o[n * depth // 2 : (n + 1) * depth // 2] = made.reshape(depth // 2, 2, 2, rows, half)
    reduce_core("o")

    for pair in range(half // (2 * HEAD_DIM)):
        lanes = slice(pair * 2 * HEAD_DIM, (pair + 1) * 2 * HEAD_DIM)
        q2, k2, v2_, c2 = qkv[0, :, lanes], qkv[1, :, lanes], qkv[2, :, lanes], cg[:, lanes]
        parts = []
        for which in range(2):
            weights = prob[2 * pair + which]
            dv = dot_tn(low(weights), c2)
            dp = dot_nt(masked(c2, which), v2_)
            ds = low(weights * (dp - jnp.sum(weights * dp, axis=-1, keepdims=True)) * scale)
            parts.append((jnp.dot(ds, k2, preferred_element_type=F32), dot_tn(ds, q2), dv))
        for m in range(3):
            dqkv[m, :, lanes] = low(jnp.where(first_lane, parts[0][m], parts[1][m]))
    reduce_y("o")
    for m in range(3):
        made = low(dot_tn(hidden[...], dqkv[m]))
        g_q[:, :, :, m * rows : (m + 1) * rows, :] = made.reshape(depth, 2, 2, rows, half)
    reduce_core("q")
    v0[2:3, pl.ds(mine, half)] = column_sum(wide(dqkv[0]))
    v0[3:4, pl.ds(mine, half)] = column_sum(wide(dqkv[2]))
    reduce_z("u")
    for n in range(2):
        cols = slice(n * half, (n + 1) * half)
        some = slice(n * fsdp // 2, (n + 1) * fsdp // 2)
        made = dot_nt(dqkv[0], wqkv[0, some].reshape(half, half))
        made = made + dot_nt(dqkv[1], wqkv[1, some].reshape(half, half))
        made = made + dot_nt(dqkv[2], wqkv[2, some].reshape(half, half))
        for s in range(2):
            hg_part[s, :, cols] = made[s * own : (s + 1) * own]
    hg_send[...] = low(hg_part[1 - x])
    send(hg_send, hg_recv, x_send.at[5], x_recv.at[5], xpeer)
    reduce_y("q")
    v0[0:1, :] = column_sum(hg_part[0] * n_in[0]) + column_sum(hg_part[1] * n_in[1])
    v0[1:2, :] = column_sum(hg_part[0]) + column_sum(hg_part[1])
    per = ff // width
    for n in range(per):
        sums = bup_sum[:, n * width : (n + 1) * width]
        v0[8 + n : 9 + n, :] = jnp.where(x == 0, sums, jnp.zeros_like(sums))
        v0[8 + per + n : 9 + per + n, :] = jnp.where(x == 0, jnp.zeros_like(sums), sums)
    send(v0, vs, rs_send.at[4, 0], rs_recv.at[4, 0], sib)
    reduce_z("o")
    reduce_x("d")
    arrived(vs, rs_recv.at[4, 0])
    v1[...] = v0[...] + vs[...]
    send(v1, vy, rs_send.at[4, 1], rs_recv.at[4, 1], ypeer)

    arrived(op_recv, x_recv.at[4])
    o_out[...] = middle[x] + (op_part[x] + wide(op_recv[...])) + vfull[7:8, :]
    arrived(hg_recv, x_recv.at[5])
    total = hg_part[x] + wide(hg_recv[...])
    normed = n_in[x]
    scaled = total * vfull[0:1, :]
    spread = scaled - row_mean(scaled) - normed * row_mean(scaled * normed)
    o_in[...] = mg[x] + spread * stat_in[x, :, 0:1]

    reduce_x("u")
    arrived(vy, rs_recv.at[4, 1])
    v2[...] = v1[...] + vy[...]
    for n in range(hops):
        send(v2, vz.at[hops - 1 - n], rs_send.at[4, 2 + n], rs_recv.at[4, 2 + hops - 1 - n], zpeers[n])
    reduce_z("q")
    reduce_x("o")
    total = v2[...]
    for n in range(hops):
        arrived(vz.at[n], rs_recv.at[4, 2 + n])
        total = total + vz[n]
    v3[...] = total
    send(v3, vx, rs_send.at[4, 2 + hops], rs_recv.at[4, 2 + hops], xpeer)

    fin, got = reduced("d")
    o_wd[pl.ds(pl.multiple_of(x * slab, 16), slab), :] = fin[...]
    o_wd[pl.ds(pl.multiple_of((1 - x) * slab, 16), slab), :] = wide(got[...])
    fin, got = reduced("u")
    one, two = fin[...], wide(got[...])
    left, right = jnp.where(x == 0, one, two), jnp.where(x == 0, two, one)
    woven = []
    for b in range(fsdp):
        woven.append(left[:, b * slab : (b + 1) * slab])
        woven.append(right[:, b * slab : (b + 1) * slab])
    o_wu[...] = jnp.concatenate(woven, axis=1)
    reduce_x("q")
    fin, got = reduced("o")
    o_wo[:, pl.ds(mine, half)] = fin[...]
    o_wo[:, pl.ds(theirs, half)] = wide(got[...])
    arrived(vx, rs_recv.at[4, 2 + hops])
    v0_all = v3[...] + vx[...]
    taken = jnp.zeros((8, rows), F32)
    low_part = jnp.zeros((1, slab), F32)
    high_part = jnp.zeros((1, slab), F32)
    in_row = width // slab
    for b in range(fsdp):
        here = jnp.where(i == b, 1.0, 0.0)
        taken = taken + here * v0_all[0:8, b * rows : (b + 1) * rows]
        at_row, lane = 8 + b // in_row, (b % in_row) * slab
        low_part = low_part + here * v0_all[at_row : at_row + 1, lane : lane + slab]
        high_part = high_part + here * v0_all[at_row + per : at_row + per + 1, lane : lane + slab]
    for at_row, ref in enumerate((o_fg, o_fb, o_bq, o_bv, o_bo, o_sg, o_sb, o_bd)):
        ref[...] = taken[at_row : at_row + 1]
    o_bu[...] = jnp.concatenate([low_part, high_part], axis=1)
    fin, got = reduced("q")
    for m, ref in enumerate((o_wq, o_wk, o_wv)):
        ref[:, pl.ds(mine, half)] = fin[m * rows : (m + 1) * rows, :]
        ref[:, pl.ds(theirs, half)] = wide(got[m * rows : (m + 1) * rows, :])

    for copy in started:
        copy.wait_send()


def fused_on_device(frames_in, cotangent, *stacks):
    fsdp = lax.axis_size("fsdp")
    own, width = frames_in.shape[1:]
    sz = Sizes(own, width, stacks[13].shape[1] * fsdp, fsdp)
    half, ff, depth, rows, slab, frames = sz.half, sz.ff, sz.depth, sz.rows, sz.slab, sz.frames
    args = [frames_in[0], cotangent[0]] + [s if s.ndim == 2 else s[0] for s in stacks]
    in_hbm = {0, 1, 4, 6, 7, 9, 15}
    whole = pl.BlockSpec(memory_space=pltpu.VMEM)
    outs = [jax.ShapeDtypeStruct(a.shape, F32) for a in args]

    def vm(dtype, *dims):
        return pltpu.VMEM(dims, dtype)

    def reduce_scratch(r, w):
        return [
            vm(BF16, depth, 2, 2, r, w), vm(BF16, depth, 2, r, w), vm(BF16, depth, r, w),
            vm(BF16, depth, r, w), vm(BF16, depth - 1, r, w), vm(BF16, depth - 1, r, w),
            vm(BF16, r, w), vm(BF16, r, w), vm(F32, r, w),
        ]

    heads = half // HEAD_DIM
    scratch = [
        vm(BF16, 3, fsdp, rows, half), vm(BF16, fsdp, rows, width), vm(BF16, fsdp, rows, ff),
        vm(BF16, fsdp, slab, width), vm(F32, fsdp, 16, 128), vm(F32, 8, width), vm(F32, 1, ff),
        vm(F32, 2, own, width), vm(F32, 2, own, width), vm(F32, 2, own, width), vm(F32, 2, own, width),
        vm(F32, 2, own, width), vm(BF16, frames, width), vm(BF16, frames, width),
        vm(F32, 2, own, 128), vm(F32, 2, own, 128), vm(BF16, 3, frames, half),
        vm(F32, heads, frames, frames), vm(BF16, 2, frames, half), vm(BF16, frames, ff),
        vm(F32, frames, ff), vm(BF16, frames, ff), vm(F32, 2, own, width), vm(BF16, frames, width),
        vm(BF16, frames, width), vm(BF16, frames, half), vm(BF16, 3, frames, half),
        vm(F32, frames, width), vm(BF16, frames, width), vm(BF16, frames, width),
        vm(F32, 2, own, width), vm(BF16, own, width), vm(BF16, own, width),
        vm(F32, 2, own, width), vm(BF16, own, width), vm(BF16, own, width),
        *reduce_scratch(slab, width), *reduce_scratch(rows, ff), *reduce_scratch(rows, half),
        *reduce_scratch(3 * rows, half),
        vm(F32, 16, width), vm(F32, 16, width), vm(F32, 16, width), vm(F32, 16, width),
        vm(F32, 16, width), vm(F32, 16, width), vm(F32, depth - 1, 16, width), vm(F32, 16, width),
        pltpu.SemaphoreType.DMA((7,)),
        pltpu.SemaphoreType.DMA((5, 4 * depth - 1)), pltpu.SemaphoreType.DMA((5, fsdp)),
        pltpu.SemaphoreType.DMA((5, depth + 2)), pltpu.SemaphoreType.DMA((5, depth + 2)),
        pltpu.SemaphoreType.DMA((6,)), pltpu.SemaphoreType.DMA((6,)),
    ]
    made = pl.pallas_call(
        functools.partial(encoder_kernel, sz),
        out_shape=outs,
        in_specs=[pl.BlockSpec(memory_space=pl.ANY) if n in in_hbm else whole for n in range(len(args))],
        out_specs=[whole] * len(outs),
        scratch_shapes=scratch,
        compiler_params=pltpu.CompilerParams(
            collective_id=0, has_side_effects=True, vmem_limit_bytes=60 * 2**20
        ),
    )(*args)
    return tuple(o if p.ndim == 2 else o[None] for o, p in zip(made, (frames_in, cotangent, *stacks)))


def fits_kernel(mesh, frames_in, up_weight):
    seq, fsdp = mesh.shape["seq"], mesh.shape["fsdp"]
    width, hidden = up_weight.shape[1:]
    return (
        seq == 2
        and fsdp % 4 == 0
        and fsdp // 4 in (2, 4)
        and frames_in.shape[0] == fsdp
        and frames_in.shape[1] % 64 == 0
        and width % (16 * fsdp) == 0
        and width % 256 == 0
        and hidden % (32 * fsdp) == 0
        and hidden * 2 % (128 * fsdp) == 0
        and hidden == 4 * width
    )


def solution(mesh):
    def build(body):
        return jax.shard_map(
            body,
            mesh=mesh,
            in_specs=(
                P("fsdp", "seq", None),
                P("fsdp", "seq", None),
                P(None, "fsdp"),
                P(None, "fsdp"),
                P(None, "fsdp", None),
                P(None, "fsdp"),
                P(None, "fsdp", None),
                P(None, "fsdp", None),
                P(None, "fsdp"),
                P(None, "fsdp", None),
                P(None, "fsdp"),
                P(None, "fsdp"),
                P(None, "fsdp"),
                P(None, "fsdp", None),
                P(None, "fsdp"),
                P(None, "fsdp", None),
                P(None, "fsdp"),
            ),
            out_specs=(
                P("fsdp", "seq", None),
                P("fsdp", "seq", None),
                P(None, "fsdp"),
                P(None, "fsdp"),
                P(None, "fsdp", None),
                P(None, "fsdp"),
                P(None, "fsdp", None),
                P(None, "fsdp", None),
                P(None, "fsdp"),
                P(None, "fsdp", None),
                P(None, "fsdp"),
                P(None, "fsdp"),
                P(None, "fsdp"),
                P(None, "fsdp", None),
                P(None, "fsdp"),
                P(None, "fsdp", None),
                P(None, "fsdp"),
            ),
            check_vma=False,
        )

    def run(*arrays):
        body = fused_on_device if fits_kernel(mesh, arrays[0], arrays[13]) else on_device
        return build(body)(*arrays)

    return run
```

```python
import functools

import jax
import jax.numpy as jnp
from jax import lax
from jax.experimental import pallas as pl
from jax.experimental.pallas import tpu as pltpu
from jax.sharding import PartitionSpec as P

HEAD_DIM = 64


EPSILON = 1e-05
ROOT_HALF = 0.7071067811865476
INV_ROOT_TAU = 0.3989422804014327


def matmul(left, right):
    return jnp.dot(left, right, preferred_element_type=jnp.float32)


def contract_rows(left, right):
    return lax.dot_general(
        left, right, (((0,), (0,)), ((), ())), preferred_element_type=jnp.float32
    )


def contract_cols(left, right):
    return lax.dot_general(
        left, right, (((1,), (1,)), ((), ())), preferred_element_type=jnp.float32
    )


def layer_norm(residual, gain, offset):
    centre = residual - jnp.mean(residual, axis=-1, keepdims=True)
    inv_std = lax.rsqrt(jnp.mean(centre * centre, axis=-1, keepdims=True) + EPSILON)
    normed = centre * inv_std
    return (normed * gain.astype(jnp.float32) + offset.astype(jnp.float32), normed, inv_std)


def norm_grad(upstream, normed, inv_std, gain):
    scaled = upstream * gain.astype(jnp.float32)
    spread = scaled - jnp.mean(scaled, axis=-1, keepdims=True)
    return (spread - normed * jnp.mean(scaled * normed, axis=-1, keepdims=True)) * inv_std


def gelu_exact(pre_act):
    return 0.5 * pre_act * (1.0 + lax.erf(pre_act * ROOT_HALF))


def gelu_slope(pre_act):
    return (
        0.5 * (1.0 + lax.erf(pre_act * ROOT_HALF))
        + pre_act * jnp.exp(-0.5 * pre_act * pre_act) * INV_ROOT_TAU
    )


def split_heads(rows):
    return rows.reshape(rows.shape[0], rows.shape[1] // HEAD_DIM, HEAD_DIM)


def attend(query_rows, key_rows, value_rows):
    score_scale = HEAD_DIM ** (-0.5)
    query_heads = split_heads(query_rows)
    key_heads = split_heads(key_rows)
    value_heads = split_heads(value_rows)
    scores = (
        jnp.einsum("qhd,khd->hqk", query_heads, key_heads, preferred_element_type=jnp.float32)
        * score_scale
    )
    row_top = jnp.max(scores, axis=-1, keepdims=True)
    log_total = row_top + jnp.log(jnp.sum(jnp.exp(scores - row_top), axis=-1, keepdims=True))
    weights = jnp.exp(scores - log_total)
    context = jnp.einsum(
        "hqk,khd->qhd",
        weights.astype(jnp.bfloat16),
        value_heads,
        preferred_element_type=jnp.float32,
    )
    return (context.reshape(query_rows.shape).astype(jnp.bfloat16), weights)


def attend_back(query_rows, key_rows, value_rows, weights, context_gradient):
    score_scale = HEAD_DIM ** (-0.5)
    row_shape = query_rows.shape
    query_heads = split_heads(query_rows)
    key_heads = split_heads(key_rows)
    value_heads = split_heads(value_rows)
    gradient_heads = split_heads(context_gradient)
    value_gradient = jnp.einsum(
        "hqk,qhd->khd",
        weights.astype(jnp.bfloat16),
        gradient_heads,
        preferred_element_type=jnp.float32,
    )
    prob_gradient = jnp.einsum(
        "qhd,khd->hqk", gradient_heads, value_heads, preferred_element_type=jnp.float32
    )
    score_gradient = (
        weights
        * (prob_gradient - jnp.sum(weights * prob_gradient, axis=-1, keepdims=True))
        * score_scale
    ).astype(jnp.bfloat16)
    query_gradient = jnp.einsum(
        "hqk,khd->qhd", score_gradient, key_heads, preferred_element_type=jnp.float32
    )
    key_gradient = jnp.einsum(
        "hqk,qhd->khd", score_gradient, query_heads, preferred_element_type=jnp.float32
    )
    return tuple(
        part.reshape(row_shape).astype(jnp.bfloat16)
        for part in (query_gradient, key_gradient, value_gradient)
    )


VECTORS = (0, 1, 3, 6, 8, 9, 10, 12, 14)
MATRICES = (2, 4, 5, 7, 11, 13)
PAD_ROWS = 16


def cut_columns(rows, width):
    blocks = rows.shape[-1] // width
    if blocks == 1:
        return rows
    return jnp.concatenate(
        [rows[..., i * width : (i + 1) * width] for i in range(blocks)], axis=-2
    )


def join_columns(rows, blocks):
    if blocks == 1:
        return rows
    size = rows.shape[-2] // blocks
    return jnp.concatenate(
        [rows[..., i * size : (i + 1) * size, :] for i in range(blocks)], axis=-1
    )


def gather_layer(shards, width):
    pieces = [cut_columns(shards[i], width) for i in MATRICES]
    vector = jnp.concatenate([shards[i] for i in VECTORS])
    vector = jnp.pad(vector, (0, PAD_ROWS * width - vector.shape[0]))
    pieces.append(vector.reshape(PAD_ROWS, width))
    packed = lax.all_gather(jnp.concatenate(pieces, axis=0), "fsdp", axis=0, tiled=False)
    params = [None] * len(shards)
    start = 0
    for i in MATRICES:
        blocks = shards[i].shape[1] // width
        size = shards[i].shape[0] * blocks
        part = join_columns(packed[:, start : start + size], blocks)
        params[i] = part.reshape(-1, shards[i].shape[1])
        start += size
    vectors = packed[:, start:].reshape(packed.shape[0], -1)
    start = 0
    for i in VECTORS:
        size = shards[i].shape[0]
        params[i] = vectors[:, start : start + size].reshape(-1)
        start += size
    return params


def reduce_gradients(gradients, shards, width, seq_size, seq_index, fsdp_size):
    part_width = width // seq_size
    pieces = []
    for i in MATRICES:
        blocks = shards[i].shape[1] // width
        rows = gradients[i].astype(jnp.bfloat16)
        rows = rows.reshape(fsdp_size, shards[i].shape[0], rows.shape[1])
        pieces.append(cut_columns(rows, part_width))
    vector = jnp.concatenate(
        [gradients[i].reshape(fsdp_size, -1) for i in VECTORS], axis=1
    ).astype(jnp.bfloat16)
    vector = jnp.pad(vector, ((0, 0), (0, PAD_ROWS * width - vector.shape[1])))
    vector = vector.reshape(fsdp_size, PAD_ROWS * seq_size, part_width)
    pieces.append(lax.dynamic_slice_in_dim(vector, seq_index * PAD_ROWS, PAD_ROWS, axis=1))
    packed = jnp.concatenate(pieces, axis=1)
    mine = lax.psum_scatter(packed, "fsdp", scatter_dimension=0, tiled=False)
    both = lax.all_gather(mine, "seq", axis=0, tiled=False)
    reduced = [None] * len(shards)
    start = 0
    for i in MATRICES:
        blocks = shards[i].shape[1] // width
        size = shards[i].shape[0] * blocks
        part = join_columns(both[:, start : start + size], blocks)
        whole = jnp.concatenate([part[s] for s in range(seq_size)], axis=-1)
        reduced[i] = whole.astype(jnp.float32)[None]
        start += size
    vector = both[:, start:].reshape(-1).astype(jnp.float32)
    start = 0
    for i in VECTORS:
        size = shards[i].shape[0]
        reduced[i] = vector[start : start + size][None]
        start += size
    return reduced


def on_device(frames_in, cotangent, *stacks):
    width = frames_in.shape[2]
    seq_size = lax.axis_size("seq")
    seq_index = lax.axis_index("seq")
    fsdp_size = lax.axis_size("fsdp")
    shards = [stack[0] for stack in stacks]
    own = frames_in.shape[1]

    mine = jnp.stack([frames_in[0], cotangent[0]])
    if seq_size == 2:
        other = lax.ppermute(mine, "seq", [(0, 1), (1, 0)])
        first = seq_index == 0
        rows = jnp.concatenate(
            [jnp.where(first, mine, other), jnp.where(first, other, mine)], axis=1
        )
    else:
        rows = lax.all_gather(mine, "seq", axis=1, tiled=True)
    residual, upstream = rows[0], rows[1]
    params = gather_layer(shards, width)

    def own_columns(matrix):
        size = matrix.shape[1] // seq_size
        return lax.dynamic_slice_in_dim(matrix, seq_index * size, size, axis=1)

    def own_rows(matrix):
        return lax.dynamic_slice_in_dim(matrix, seq_index * own, own, axis=0)[None]

    wide = [None if i in MATRICES else p.astype(jnp.float32) for i, p in enumerate(params)]

    hidden_wide, normed_in, inv_in = layer_norm(residual, params[0], params[1])
    hidden = hidden_wide.astype(jnp.bfloat16)
    query_rows = (matmul(hidden, params[2]) + wide[3]).astype(jnp.bfloat16)
    key_rows = matmul(hidden, params[4]).astype(jnp.bfloat16)
    value_rows = (matmul(hidden, params[5]) + wide[6]).astype(jnp.bfloat16)
    context, weights = attend(query_rows, key_rows, value_rows)
    middle = residual + matmul(context, params[7]) + wide[8]
    mid_wide, normed_mid, inv_mid = layer_norm(middle, params[9], params[10])
    hidden_mid = mid_wide.astype(jnp.bfloat16)
    pre_act = matmul(hidden_mid, params[11]) + wide[12]
    activated = gelu_exact(pre_act).astype(jnp.bfloat16)
    own_activated = own_rows(activated)[0]
    outputs = own_rows(middle)[0] + matmul(own_activated, params[13]) + wide[14]

    gradients = [None] * len(stacks)
    upstream_low = upstream.astype(jnp.bfloat16)
    gradients[13] = contract_rows(activated, own_columns(upstream_low))
    gradients[14] = jnp.sum(upstream, axis=0)
    pre_gradient = contract_cols(upstream_low, params[13]) * gelu_slope(pre_act)
    pre_low = pre_gradient.astype(jnp.bfloat16)
    gradients[11] = contract_rows(hidden_mid, own_columns(pre_low))
    gradients[12] = jnp.sum(pre_gradient, axis=0)
    mid_hidden_gradient = contract_cols(pre_low, params[11])
    gradients[9] = jnp.sum(mid_hidden_gradient * normed_mid, axis=0)
    gradients[10] = jnp.sum(mid_hidden_gradient, axis=0)
    middle_gradient = upstream + norm_grad(mid_hidden_gradient, normed_mid, inv_mid, params[9])
    middle_low = middle_gradient.astype(jnp.bfloat16)
    gradients[7] = contract_rows(context, own_columns(middle_low))
    gradients[8] = jnp.sum(middle_gradient, axis=0)
    context_gradient = contract_cols(middle_low, params[7]).astype(jnp.bfloat16)
    query_gradient, key_gradient, value_gradient = attend_back(
        query_rows, key_rows, value_rows, weights, context_gradient
    )
    gradients[2] = contract_rows(hidden, own_columns(query_gradient))
    gradients[3] = jnp.sum(query_gradient.astype(jnp.float32), axis=0)
    gradients[4] = contract_rows(hidden, own_columns(key_gradient))
    gradients[5] = contract_rows(hidden, own_columns(value_gradient))
    gradients[6] = jnp.sum(value_gradient.astype(jnp.float32), axis=0)
    hidden_gradient = (
        contract_cols(query_gradient, params[2])
        + contract_cols(key_gradient, params[4])
        + contract_cols(value_gradient, params[5])
    )
    gradients[0] = jnp.sum(hidden_gradient * normed_in, axis=0)
    gradients[1] = jnp.sum(hidden_gradient, axis=0)
    input_gradient = middle_gradient + norm_grad(hidden_gradient, normed_in, inv_in, params[0])
    reduced = reduce_gradients(gradients, shards, width, seq_size, seq_index, fsdp_size)
    return (outputs[None], own_rows(input_gradient), *reduced)


MESH = pl.DeviceIdType.MESH
F32 = jnp.float32
BF16 = jnp.bfloat16


def dot_nt(left, right):
    return lax.dot_general(left, right, (((1,), (1,)), ((), ())), preferred_element_type=F32)


def dot_tn(left, right):
    return lax.dot_general(left, right, (((0,), (0,)), ((), ())), preferred_element_type=F32)


def low(values):
    return values.astype(BF16)


def wide(values):
    return values.astype(F32)


def row_mean(values):
    return jnp.mean(values, axis=-1, keepdims=True)


def column_sum(values):
    return jnp.sum(values, axis=0, keepdims=True)


class Sizes:
    def __init__(self, own, width, hidden, fsdp):
        self.own, self.width, self.hidden, self.fsdp = own, width, hidden, fsdp
        self.frames = 2 * own
        self.half = width // 2
        self.ff = hidden // 2
        self.depth = fsdp // 4
        self.rows = width // fsdp
        self.slab = hidden // fsdp // 2


def encoder_kernel(sz, *refs):
    half, ff, depth, rows, slab = sz.half, sz.ff, sz.depth, sz.rows, sz.slab
    own, frames, width, fsdp = sz.own, sz.frames, sz.width, sz.fsdp
    hops = depth - 1
    (frames_ref, cot_ref, v_fg, v_fb, wq_ref, v_bq, wk_ref, wv_ref, v_bv, wo_ref, v_bo, v_sg, v_sb,
     wu_ref, v_bu, wd_ref, v_bd) = refs[:17]
    (o_out, o_in, o_fg, o_fb, o_wq, o_bq, o_wk, o_wv, o_bv, o_wo, o_bo, o_sg, o_sb, o_wu, o_bu,
     o_wd, o_bd) = refs[17:34]
    (wqkv, wo, wup, wdown, vecg, vfull, bup, rbuf, gbuf, n_in, n_mid, middle, hidden, hmid, stat_in,
     stat_mid, qkv, prob, cbuf, act, slope, plow, mg, upl, mlow, cg, dqkv, mh_part, mh_send, mh_recv, op_part,
     op_send, op_recv, hg_part, hg_send, hg_recv,
     g_d, s_d, t_d, y_d, zs_d, zr_d, xs_d, xr_d, f_d,
     g_u, s_u, t_u, y_u, zs_u, zr_u, xs_u, xr_u, f_u,
     g_o, s_o, t_o, y_o, zs_o, zr_o, xs_o, xr_o, f_o,
     g_q, s_q, t_q, y_q, zs_q, zr_q, xs_q, xr_q, f_q,
     g_k, s_k, t_k, y_k, zs_k, zr_k, xs_k, xr_k, f_k,
     g_v, s_v, t_v, y_v, zs_v, zr_v, xs_v, xr_v, f_v,
     v0, v1, v2, v3, vs, vy, vz, vx,
     local_sem, ag_send, ag_recv, rs_send, rs_recv, x_send, x_recv) = refs[34:]

    x = lax.axis_index("seq")
    i = lax.axis_index("fsdp")
    z, y, c = i // 4, lax.rem(i // 2, 2), lax.rem(i, 2)

    def at(z_at, y_at, c_at):
        return (x, z_at * 4 + y_at * 2 + c_at)

    sib, ypeer, xpeer = at(z, y, 1 - c), at(z, 1 - y, c), (1 - x, i)
    zother = [lax.rem(z + d, depth) for d in range(1, depth)]
    zpeers = [at(other, y, c) for other in zother]
    inner = jnp.logical_or(z == 1, z == 2)
    beside = z + 1 - 2 * lax.rem(z, 2)
    second = jnp.where(z < 2, 2, 1)
    far_end = 6 - z - beside - second
    near = [beside, second]
    mine = pl.multiple_of(x * half, 128)
    theirs = pl.multiple_of((1 - x) * half, 128)

    local = [
        pltpu.make_async_copy(wq_ref.at[:, pl.ds(mine, half)], wqkv.at[0, i], local_sem.at[0]),
        pltpu.make_async_copy(wk_ref.at[:, pl.ds(mine, half)], wqkv.at[1, i], local_sem.at[1]),
        pltpu.make_async_copy(wv_ref.at[:, pl.ds(mine, half)], wqkv.at[2, i], local_sem.at[2]),
        pltpu.make_async_copy(wo_ref, wo.at[i], local_sem.at[3]),
        pltpu.make_async_copy(wd_ref.at[pl.ds(pl.multiple_of(x * slab, 16), slab)], wdown.at[i], local_sem.at[4]),
        pltpu.make_async_copy(frames_ref, rbuf.at[x], local_sem.at[5]),
        pltpu.make_async_copy(cot_ref, gbuf.at[x], local_sem.at[6]),
    ]
    for copy in local:
        copy.start()

    barrier = pltpu.get_barrier_semaphore()
    partners = [sib, ypeer, xpeer, *zpeers]
    for partner in partners:
        pl.semaphore_signal(barrier, inc=1, device_id=partner, device_id_type=MESH)

    vecg[i] = jnp.zeros(vecg.shape[1:], F32)
    for at_row, ref in enumerate((v_fg, v_fb, v_bq, v_bv, v_bo, v_sg, v_sb, v_bd)):
        vecg[i, at_row : at_row + 1, 0:rows] = wide(ref[...])
    up_bias = wide(v_bu[...])
    vecg[i, 8:9, 0:slab] = up_bias[:, :slab]
    vecg[i, 9:10, 0:slab] = up_bias[:, slab:]

    pl.semaphore_wait(barrier, len(partners))

    started = []

    def send(src, dst, send_sem, recv_sem, to):
        copy = pltpu.make_async_remote_copy(
            src_ref=src, dst_ref=dst, send_sem=send_sem, recv_sem=recv_sem, device_id=to, device_id_type=MESH
        )
        copy.start()
        started.append(copy)

    def arrived(dst, recv_sem):
        pltpu.make_async_remote_copy(
            src_ref=dst, dst_ref=dst, send_sem=recv_sem, recv_sem=recv_sem, device_id=xpeer, device_id_type=MESH
        ).wait_recv()

    def block(piece, b):
        return (wqkv.at[:, b], vecg.at[b], wo.at[b], wup.at[b], wdown.at[b])[piece]

    def pass_on(piece, b, slot, to):
        send(block(piece, b), block(piece, b), ag_send.at[piece, slot], ag_recv.at[piece, b], to)

    inner_copies = []

    def pass_inner(piece, b, slot, to):
        copy = pltpu.make_async_remote_copy(
            src_ref=block(piece, b), dst_ref=block(piece, b), send_sem=ag_send.at[piece, slot],
            recv_sem=ag_recv.at[piece, b], device_id=to, device_id_type=MESH
        )
        inner_copies.append(copy)

        @pl.when(inner)
        def _():
            copy.start()

    def own_z(piece):
        pass_on(piece, i, 0, at(second, y, c))
        pass_on(piece, i, 1, at(beside, y, c))
        pass_inner(piece, i, 2, at(far_end, y, c))

    def own_near(piece):
        pass_on(piece, i, hops, ypeer)
        pass_on(piece, i, hops + 1, sib)

    def relay_near(piece):
        for n, other in enumerate(near):
            b = other * 4 + y * 2 + c
            arrived(block(piece, b), ag_recv.at[piece, b])
            pass_on(piece, b, hops + 2 + n, ypeer)
            pass_on(piece, b, 2 * hops + 2 + n, sib)

    def relay_far(piece):
        b = far_end * 4 + y * 2 + c
        arrived(block(piece, b), ag_recv.at[piece, b])
        pass_inner(piece, b, 4 * hops + 3, at(beside, y, c))
        pass_on(piece, b, hops + 4, ypeer)
        pass_on(piece, b, 2 * hops + 4, sib)

    def relay_y(piece):
        for n, other in enumerate((z, beside, second, far_end)):
            b = other * 4 + (1 - y) * 2 + c
            arrived(block(piece, b), ag_recv.at[piece, b])
            pass_on(piece, b, 3 * hops + 2 + n, sib)

    def finish(piece):
        for k in range(2 * depth):
            b = 2 * k + (1 - c)
            arrived(block(piece, b), ag_recv.at[piece, b])

    for n in range(3):
        local[n].wait()
    own_z(0)
    own_near(0)
    own_z(1)
    own_near(1)
    local[5].wait()
    send(rbuf.at[x], rbuf.at[x], x_send.at[0], x_recv.at[0], xpeer)
    local[3].wait()
    own_z(2)
    own_near(2)
    local[6].wait()
    send(gbuf.at[x], gbuf.at[x], x_send.at[1], x_recv.at[1], xpeer)
    up = wide(wu_ref[...])
    picked = []
    for b in range(fsdp):
        left = up[:, 2 * slab * b : 2 * slab * b + slab]
        right = up[:, 2 * slab * b + slab : 2 * slab * (b + 1)]
        picked.append(jnp.where(x == 0, left, right))
    wup[i] = low(jnp.concatenate(picked, axis=1))
    own_near(3)
    local[4].wait()
    own_near(4)

    relay_near(0)
    relay_near(1)
    own_z(3)
    relay_far(0)
    relay_far(1)
    relay_near(2)
    own_z(4)
    relay_y(0)
    relay_y(1)
    finish(1)
    for b in range(fsdp):
        vfull[:, rows * b : rows * (b + 1)] = vecg[b, 0:8, 0:rows]
        bup[:, slab * b : slab * (b + 1)] = jnp.where(x == 0, vecg[b, 8:9, 0:slab], vecg[b, 9:10, 0:slab])
    v0[...] = jnp.zeros_like(v0)

    step = own // 2

    def by_rows(body):
        def one(n, carry):
            s = n // 2
            r0 = pl.multiple_of(lax.rem(n, 2) * step, step)
            body(s, pl.ds(r0, step), pl.ds(pl.multiple_of(n * step, step), step))
            return carry

        lax.fori_loop(0, 4, one, 0)

    arrived(rbuf.at[1 - x], x_recv.at[0])

    def norm_first(s, part, whole):
        r = rbuf[s, part, :]
        centre = r - row_mean(r)
        inv = lax.rsqrt(row_mean(centre * centre) + EPSILON)
        normed = centre * inv
        n_in[s, part, :] = normed
        stat_in[s, part, :] = jnp.broadcast_to(inv, (step, 128))
        hidden[whole, :] = low(normed * vfull[0:1, :] + vfull[1:2, :])

    by_rows(norm_first)
    relay_far(2)
    finish(0)
    for m, bias in ((0, 2), (1, None), (2, 3)):
        made = jnp.dot(hidden[...], wqkv[m].reshape(width, half), preferred_element_type=F32)
        if bias is not None:
            made = made + vfull[bias : bias + 1, pl.ds(mine, half)]
        qkv[m] = low(made)

    first_lane = lax.broadcasted_iota(jnp.int32, (frames, 2 * HEAD_DIM), 1) < HEAD_DIM
    scale = HEAD_DIM**-0.5

    def masked(pair, which):
        keep = first_lane if which == 0 else jnp.logical_not(first_lane)
        return jnp.where(keep, pair, jnp.zeros_like(pair))

    for pair in range(half // (2 * HEAD_DIM)):
        lanes = slice(pair * 2 * HEAD_DIM, (pair + 1) * 2 * HEAD_DIM)
        q2, k2, v2_ = qkv[0, :, lanes], qkv[1, :, lanes], qkv[2, :, lanes]
        parts = []
        for which in range(2):
            scores = dot_nt(masked(q2, which), k2) * scale
            raised = jnp.exp(scores - jnp.max(scores, axis=-1, keepdims=True))
            weights = raised * (1.0 / jnp.sum(raised, axis=-1, keepdims=True))
            prob[2 * pair + which] = weights
            parts.append(jnp.dot(low(weights), v2_, preferred_element_type=F32))
        cbuf[x, :, lanes] = low(jnp.where(first_lane, parts[0], parts[1]))
        if pair == 0:
            relay_y(2)
        if pair == 1:
            relay_near(3)
    send(cbuf.at[x], cbuf.at[x], x_send.at[2], x_recv.at[2], xpeer)
    finish(2)
    relay_far(3)
    arrived(cbuf.at[1 - x], x_recv.at[2])
    context = jnp.concatenate([cbuf[0], cbuf[1]], axis=1)
    for n in range(2):
        cols = slice(n * half, (n + 1) * half)
        made = jnp.dot(context, wo[:, :, cols].reshape(width, half), preferred_element_type=F32)
        made = made + vfull[4:5, cols]
        for s in range(2):
            middle[s, :, cols] = rbuf[s, :, cols] + made[s * own : (s + 1) * own]

    def norm_second(s, part, whole):
        r = middle[s, part, :]
        centre = r - row_mean(r)
        inv = lax.rsqrt(row_mean(centre * centre) + EPSILON)
        normed = centre * inv
        n_mid[s, part, :] = normed
        stat_mid[s, part, :] = jnp.broadcast_to(inv, (step, 128))
        hmid[whole, :] = low(normed * vfull[5:6, :] + vfull[6:7, :])

    by_rows(norm_second)
    relay_near(4)
    relay_y(3)
    arrived(gbuf.at[1 - x], x_recv.at[1])
    for s in range(2):
        upl[s * own : (s + 1) * own, :] = low(gbuf[s])
    v0[7:8, :] = column_sum(gbuf[0]) + column_sum(gbuf[1])
    finish(3)

    chunk = 4 * slab
    chunks = ff // chunk

    def up_chunk(n, carry):
        cols = pl.ds(pl.multiple_of(n * chunk, 128), chunk)
        pre = jnp.dot(hmid[...], wup[:, :, cols].reshape(width, chunk), preferred_element_type=F32)
        pre = pre + bup[:, cols]
        bell = 0.5 * (1.0 + lax.erf(pre * ROOT_HALF))
        act[:, cols] = low(pre * bell)
        slope[:, cols] = bell + pre * jnp.exp(-0.5 * pre * pre) * INV_ROOT_TAU
        return carry

    lax.fori_loop(0, chunks, up_chunk, 0)
    relay_far(4)

    pieces = {
        "d": (0, g_d, s_d, t_d, y_d, zs_d, zr_d, xs_d, xr_d, f_d),
        "u": (1, g_u, s_u, t_u, y_u, zs_u, zr_u, xs_u, xr_u, f_u),
        "o": (2, g_o, s_o, t_o, y_o, zs_o, zr_o, xs_o, xr_o, f_o),
        "q": (3, g_q, s_q, t_q, y_q, zs_q, zr_q, xs_q, xr_q, f_q),
        "k": (5, g_k, s_k, t_k, y_k, zs_k, zr_k, xs_k, xr_k, f_k),
        "v": (6, g_v, s_v, t_v, y_v, zs_v, zr_v, xs_v, xr_v, f_v),
    }

    def reduce_core(name):
        at_piece, g, s_ = pieces[name][:3]
        send(g.at[:, :, 1 - c], s_, rs_send.at[at_piece, 0], rs_recv.at[at_piece, 0], sib)

    def reduce_y(name):
        at_piece, g, s_, t, yb = pieces[name][:5]
        arrived(s_, rs_recv.at[at_piece, 0])

        def one(n, carry):
            t[n] = low(wide(g[n, 1 - y, c]) + wide(s_[n, 1 - y]))
            return carry

        lax.fori_loop(0, depth, one, 0)
        send(t, yb, rs_send.at[at_piece, 1], rs_recv.at[at_piece, 1], ypeer)

    def reduce_z(name):
        at_piece, g, s_, t, yb, zs, zr, xs, xr, fin = pieces[name]
        arrived(yb, rs_recv.at[at_piece, 1])
        for n, other in enumerate(zother):
            zs[n] = low(wide(g[other, y, c]) + wide(s_[other, y]) + wide(yb[other]))
            send(zs.at[n], zr.at[hops - 1 - n], rs_send.at[at_piece, 2 + n],
                 rs_recv.at[at_piece, 2 + hops - 1 - n], zpeers[n])
        fin[...] = wide(g[z, y, c]) + wide(s_[z, y]) + wide(yb[z])

    def reduce_x(name):
        at_piece, g, s_, t, yb, zs, zr, xs, xr, fin = pieces[name]
        total = fin[...]
        for n in range(hops):
            arrived(zr.at[n], rs_recv.at[at_piece, 2 + n])
            total = total + wide(zr[n])
        fin[...] = total
        xs[...] = low(total)
        send(xs, xr, rs_send.at[at_piece, 2 + hops], rs_recv.at[at_piece, 2 + hops], xpeer)

    def reduced(name):
        at_piece, g, s_, t, yb, zs, zr, xs, xr, fin = pieces[name]
        arrived(xr, rs_recv.at[at_piece, 2 + hops])
        return fin, xr

    def down_chunk(n, carry):
        cols = pl.ds(pl.multiple_of(n * chunk, 128), chunk)
        made = low(dot_tn(act[:, cols], upl[...]))
        g_d[n] = made.reshape(2, 2, slab, width)
        return carry

    lax.fori_loop(0, chunks, down_chunk, 0)
    reduce_core("d")
    relay_y(4)
    reduce_y("d")
    finish(4)


    def back_chunk(n, carry):
        cols = pl.ds(pl.multiple_of(n * chunk, 128), chunk)
        rhs = wdown[pl.ds(n * 4, 4)].reshape(chunk, width)
        pg = dot_nt(upl[...], rhs) * slope[:, cols]
        plow[:, cols] = low(pg)
        bup_sum[:, cols] = column_sum(pg)
        return carry

    bup_sum = bup
    lax.fori_loop(0, chunks, back_chunk, 0)
    for n in range(2):
        cols = slice(n * half, (n + 1) * half)
        made = dot_nt(plow[...], wup[n * fsdp // 2 : (n + 1) * fsdp // 2].reshape(half, ff))
        mh_part[:, cols] = made
        mh_send[n] = low(made)
        send(mh_send.at[n], mh_recv.at[n], x_send.at[3 + 3 * n], x_recv.at[3 + 3 * n], xpeer)

    def up_back(n, carry):
        cols = pl.ds(pl.multiple_of(n * chunk, 128), chunk)
        made = low(dot_tn(hmid[...], plow[:, cols]))
        g_u[:, :, :, :, cols] = made.reshape(depth, 2, 2, rows, chunk)
        return carry

    lax.fori_loop(0, chunks, up_back, 0)
    reduce_core("u")
    reduce_z("d")

    for n in range(2):
        cols = slice(n * half, (n + 1) * half)
        made = jnp.dot(act[...], wdown[:, :, cols].reshape(ff, half), preferred_element_type=F32)
        for s in range(2):
            op_part[s, :, cols] = made[s * own : (s + 1) * own]
    op_send[...] = low(op_part[1 - x])
    send(op_send, op_recv, x_send.at[4], x_recv.at[4], xpeer)
    reduce_y("u")

    arrived(mh_recv.at[0], x_recv.at[3])
    arrived(mh_recv.at[1], x_recv.at[6])
    only = jnp.where(x == 0, 1.0, 0.0)

    def norm_second_back(s, part, whole):
        total = mh_part[whole, :] + wide(jnp.concatenate([mh_recv[0, whole, :], mh_recv[1, whole, :]], axis=1))
        normed = n_mid[s, part, :]
        v0[5:6, :] += only * column_sum(total * normed)
        v0[6:7, :] += only * column_sum(total)
        scaled = total * vfull[5:6, :]
        spread = scaled - row_mean(scaled) - normed * row_mean(scaled * normed)
        made = gbuf[s, part, :] + spread * stat_mid[s, part, 0:1]
        mg[s, part, :] = made
        mlow[whole, :] = low(made)
        v0[4:5, :] += only * column_sum(made)

    by_rows(norm_second_back)
    v0[7:8, :] = only * v0[7:8, :]
    cg[...] = low(dot_nt(mlow[...], wo[pl.ds(x * (fsdp // 2), fsdp // 2)].reshape(half, width)))
    for n in range(2):
        made = low(dot_tn(cbuf[n], mlow[:, pl.ds(mine, half)]))
        g_o[n * depth // 2 : (n + 1) * depth // 2] = made.reshape(depth // 2, 2, 2, rows, half)
    reduce_core("o")

    for pair in range(half // (2 * HEAD_DIM)):
        lanes = slice(pair * 2 * HEAD_DIM, (pair + 1) * 2 * HEAD_DIM)
        q2, k2, v2_, c2 = qkv[0, :, lanes], qkv[1, :, lanes], qkv[2, :, lanes], cg[:, lanes]
        parts = []
        for which in range(2):
            weights = prob[2 * pair + which]
            dv = dot_tn(low(weights), c2)
            dp = dot_nt(masked(c2, which), v2_)
            ds = low(weights * (dp - jnp.sum(weights * dp, axis=-1, keepdims=True)) * scale)
            parts.append((jnp.dot(ds, k2, preferred_element_type=F32), dot_tn(ds, q2), dv))
        for m in range(3):
            dqkv[m, :, lanes] = low(jnp.where(first_lane, parts[0][m], parts[1][m]))
    reduce_y("o")
    for m, g, name in ((0, g_q, "q"), (1, g_k, "k"), (2, g_v, "v")):
        made = low(dot_tn(hidden[...], dqkv[m]))
        g[...] = made.reshape(depth, 2, 2, rows, half)
        reduce_core(name)
        if m > 0:
            reduce_y("qk"[m - 1])
    v0[2:3, pl.ds(mine, half)] = column_sum(wide(dqkv[0]))
    v0[3:4, pl.ds(mine, half)] = column_sum(wide(dqkv[2]))
    reduce_z("u")
    for n in range(2):
        cols = slice(n * half, (n + 1) * half)
        some = slice(n * fsdp // 2, (n + 1) * fsdp // 2)
        made = dot_nt(dqkv[0], wqkv[0, some].reshape(half, half))
        made = made + dot_nt(dqkv[1], wqkv[1, some].reshape(half, half))
        made = made + dot_nt(dqkv[2], wqkv[2, some].reshape(half, half))
        for s in range(2):
            hg_part[s, :, cols] = made[s * own : (s + 1) * own]
    hg_send[...] = low(hg_part[1 - x])
    send(hg_send, hg_recv, x_send.at[5], x_recv.at[5], xpeer)
    reduce_y("v")
    v0[0:1, :] = column_sum(hg_part[0] * n_in[0]) + column_sum(hg_part[1] * n_in[1])
    v0[1:2, :] = column_sum(hg_part[0]) + column_sum(hg_part[1])
    per = ff // width
    for n in range(per):
        sums = bup_sum[:, n * width : (n + 1) * width]
        v0[8 + n : 9 + n, :] = jnp.where(x == 0, sums, jnp.zeros_like(sums))
        v0[8 + per + n : 9 + per + n, :] = jnp.where(x == 0, jnp.zeros_like(sums), sums)
    send(v0, vs, rs_send.at[4, 0], rs_recv.at[4, 0], sib)
    reduce_z("o")
    reduce_z("q")
    reduce_x("d")
    arrived(vs, rs_recv.at[4, 0])
    v1[...] = v0[...] + vs[...]
    send(v1, vy, rs_send.at[4, 1], rs_recv.at[4, 1], ypeer)

    arrived(op_recv, x_recv.at[4])
    reduce_z("k")
    o_out[...] = middle[x] + (op_part[x] + wide(op_recv[...])) + vfull[7:8, :]
    arrived(hg_recv, x_recv.at[5])
    total = hg_part[x] + wide(hg_recv[...])
    normed = n_in[x]
    scaled = total * vfull[0:1, :]
    spread = scaled - row_mean(scaled) - normed * row_mean(scaled * normed)
    o_in[...] = mg[x] + spread * stat_in[x, :, 0:1]

    reduce_z("v")
    reduce_x("u")
    arrived(vy, rs_recv.at[4, 1])
    v2[...] = v1[...] + vy[...]
    for n in range(hops):
        send(v2, vz.at[hops - 1 - n], rs_send.at[4, 2 + n], rs_recv.at[4, 2 + hops - 1 - n], zpeers[n])
    reduce_x("o")
    reduce_x("q")
    reduce_x("k")
    reduce_x("v")
    total = v2[...]
    for n in range(hops):
        arrived(vz.at[n], rs_recv.at[4, 2 + n])
        total = total + vz[n]
    v3[...] = total
    send(v3, vx, rs_send.at[4, 2 + hops], rs_recv.at[4, 2 + hops], xpeer)

    fin, got = reduced("d")
    o_wd[pl.ds(pl.multiple_of(x * slab, 16), slab), :] = fin[...]
    o_wd[pl.ds(pl.multiple_of((1 - x) * slab, 16), slab), :] = wide(got[...])
    fin, got = reduced("u")
    one, two = fin[...], wide(got[...])
    left, right = jnp.where(x == 0, one, two), jnp.where(x == 0, two, one)
    woven = []
    for b in range(fsdp):
        woven.append(left[:, b * slab : (b + 1) * slab])
        woven.append(right[:, b * slab : (b + 1) * slab])
    o_wu[...] = jnp.concatenate(woven, axis=1)
    fin, got = reduced("o")
    o_wo[:, pl.ds(mine, half)] = fin[...]
    o_wo[:, pl.ds(theirs, half)] = wide(got[...])
    arrived(vx, rs_recv.at[4, 2 + hops])
    v0_all = v3[...] + vx[...]
    taken = jnp.zeros((8, rows), F32)
    low_part = jnp.zeros((1, slab), F32)
    high_part = jnp.zeros((1, slab), F32)
    in_row = width // slab
    for b in range(fsdp):
        here = jnp.where(i == b, 1.0, 0.0)
        taken = taken + here * v0_all[0:8, b * rows : (b + 1) * rows]
        at_row, lane = 8 + b // in_row, (b % in_row) * slab
        low_part = low_part + here * v0_all[at_row : at_row + 1, lane : lane + slab]
        high_part = high_part + here * v0_all[at_row + per : at_row + per + 1, lane : lane + slab]
    for at_row, ref in enumerate((o_fg, o_fb, o_bq, o_bv, o_bo, o_sg, o_sb, o_bd)):
        ref[...] = taken[at_row : at_row + 1]
    o_bu[...] = jnp.concatenate([low_part, high_part], axis=1)
    for name, ref in (("q", o_wq), ("k", o_wk), ("v", o_wv)):
        fin, got = reduced(name)
        ref[:, pl.ds(mine, half)] = fin[...]
        ref[:, pl.ds(theirs, half)] = wide(got[...])

    for copy in started:
        copy.wait_send()
    for copy in inner_copies:
        pl.when(inner)(copy.wait_send)


def hand_over(*refs):
    count = (len(refs) - 2) // 3
    came, gone = refs[-2:]
    held = refs[2 * count : 3 * count]
    into = [pltpu.make_async_copy(refs[n], held[n], came.at[n]) for n in range(count)]
    out = [pltpu.make_async_copy(held[n], refs[count + n], gone.at[n]) for n in range(count)]
    for copy in into:
        copy.start()
    for n in range(count):
        into[n].wait()
        out[n].start()
    for copy in out:
        copy.wait()


def fused_on_device(frames_in, cotangent, *stacks):
    fsdp = lax.axis_size("fsdp")
    own, width = frames_in.shape[1:]
    sz = Sizes(own, width, stacks[13].shape[1] * fsdp, fsdp)
    half, ff, depth, rows, slab, frames = sz.half, sz.ff, sz.depth, sz.rows, sz.slab, sz.frames
    args = [frames_in[0], cotangent[0]] + [s if s.ndim == 2 else s[0] for s in stacks]
    in_hbm = {0, 1, 4, 6, 7, 9, 15}
    whole = pl.BlockSpec(memory_space=pltpu.VMEM)
    outs = [jax.ShapeDtypeStruct(a.shape, F32) for a in args]

    def vm(dtype, *dims):
        return pltpu.VMEM(dims, dtype)

    def reduce_scratch(r, w):
        return [
            vm(BF16, depth, 2, 2, r, w), vm(BF16, depth, 2, r, w), vm(BF16, depth, r, w),
            vm(BF16, depth, r, w), vm(BF16, depth - 1, r, w), vm(BF16, depth - 1, r, w),
            vm(BF16, r, w), vm(BF16, r, w), vm(F32, r, w),
        ]

    heads = half // HEAD_DIM
    scratch = [
        vm(BF16, 3, fsdp, rows, half), vm(BF16, fsdp, rows, width), vm(BF16, fsdp, rows, ff),
        vm(BF16, fsdp, slab, width), vm(F32, fsdp, 16, 128), vm(F32, 8, width), vm(F32, 1, ff),
        vm(F32, 2, own, width), vm(F32, 2, own, width), vm(F32, 2, own, width), vm(F32, 2, own, width),
        vm(F32, 2, own, width), vm(BF16, frames, width), vm(BF16, frames, width),
        vm(F32, 2, own, 128), vm(F32, 2, own, 128), vm(BF16, 3, frames, half),
        vm(F32, heads, frames, frames), vm(BF16, 2, frames, half), vm(BF16, frames, ff),
        vm(F32, frames, ff), vm(BF16, frames, ff), vm(F32, 2, own, width), vm(BF16, frames, width),
        vm(BF16, frames, width), vm(BF16, frames, half), vm(BF16, 3, frames, half),
        vm(F32, frames, width), vm(BF16, 2, frames, half), vm(BF16, 2, frames, half),
        vm(F32, 2, own, width), vm(BF16, own, width), vm(BF16, own, width),
        vm(F32, 2, own, width), vm(BF16, own, width), vm(BF16, own, width),
        *reduce_scratch(slab, width), *reduce_scratch(rows, ff), *reduce_scratch(rows, half),
        *reduce_scratch(rows, half), *reduce_scratch(rows, half), *reduce_scratch(rows, half),
        vm(F32, 16, width), vm(F32, 16, width), vm(F32, 16, width), vm(F32, 16, width),
        vm(F32, 16, width), vm(F32, 16, width), vm(F32, depth - 1, 16, width), vm(F32, 16, width),
        pltpu.SemaphoreType.DMA((7,)),
        pltpu.SemaphoreType.DMA((5, 4 * depth)), pltpu.SemaphoreType.DMA((5, fsdp)),
        pltpu.SemaphoreType.DMA((7, depth + 2)), pltpu.SemaphoreType.DMA((7, depth + 2)),
        pltpu.SemaphoreType.DMA((7,)), pltpu.SemaphoreType.DMA((7,)),
    ]
    made = pl.pallas_call(
        functools.partial(encoder_kernel, sz),
        out_shape=outs,
        in_specs=[pl.BlockSpec(memory_space=pl.ANY) if n in in_hbm else whole for n in range(len(args))],
        out_specs=[whole] * len(outs),
        scratch_shapes=scratch,
        compiler_params=pltpu.CompilerParams(
            collective_id=0, has_side_effects=True, vmem_limit_bytes=60 * 2**20
        ),
    )(*args)
    anywhere = [pl.BlockSpec(memory_space=pl.ANY)] * len(outs)
    made = pl.pallas_call(
        hand_over,
        out_shape=outs,
        in_specs=anywhere,
        out_specs=anywhere,
        scratch_shapes=[vm(F32, *o.shape) for o in outs] + [pltpu.SemaphoreType.DMA((len(outs),))] * 2,
    )(*made)
    return tuple(o if p.ndim == 2 else o[None] for o, p in zip(made, (frames_in, cotangent, *stacks)))


def fits_kernel(mesh, frames_in, up_weight):
    seq, fsdp = mesh.shape["seq"], mesh.shape["fsdp"]
    width, hidden = up_weight.shape[1:]
    return (
        seq == 2
        and fsdp == 16
        and frames_in.shape[0] == fsdp
        and frames_in.shape[1] % 64 == 0
        and width % (16 * fsdp) == 0
        and width % 256 == 0
        and hidden % (32 * fsdp) == 0
        and hidden * 2 % (128 * fsdp) == 0
        and hidden == 4 * width
    )


def solution(mesh):
    def build(body):
        return jax.shard_map(
            body,
            mesh=mesh,
            in_specs=(
                P("fsdp", "seq", None),
                P("fsdp", "seq", None),
                P(None, "fsdp"),
                P(None, "fsdp"),
                P(None, "fsdp", None),
                P(None, "fsdp"),
                P(None, "fsdp", None),
                P(None, "fsdp", None),
                P(None, "fsdp"),
                P(None, "fsdp", None),
                P(None, "fsdp"),
                P(None, "fsdp"),
                P(None, "fsdp"),
                P(None, "fsdp", None),
                P(None, "fsdp"),
                P(None, "fsdp", None),
                P(None, "fsdp"),
            ),
            out_specs=(
                P("fsdp", "seq", None),
                P("fsdp", "seq", None),
                P(None, "fsdp"),
                P(None, "fsdp"),
                P(None, "fsdp", None),
                P(None, "fsdp"),
                P(None, "fsdp", None),
                P(None, "fsdp", None),
                P(None, "fsdp"),
                P(None, "fsdp", None),
                P(None, "fsdp"),
                P(None, "fsdp"),
                P(None, "fsdp"),
                P(None, "fsdp", None),
                P(None, "fsdp"),
                P(None, "fsdp", None),
                P(None, "fsdp"),
            ),
            check_vma=False,
        )

    def run(*arrays):
        body = fused_on_device if fits_kernel(mesh, arrays[0], arrays[13]) else on_device
        return build(body)(*arrays)

    return run
```

```python
import functools

import jax
import jax.numpy as jnp
from jax import lax
from jax.experimental import pallas as pl
from jax.experimental.pallas import tpu as pltpu
from jax.sharding import PartitionSpec as P

HEAD_DIM = 64


EPSILON = 1e-05
ROOT_HALF = 0.7071067811865476
INV_ROOT_TAU = 0.3989422804014327


def matmul(left, right):
    return jnp.dot(left, right, preferred_element_type=jnp.float32)


def contract_rows(left, right):
    return lax.dot_general(
        left, right, (((0,), (0,)), ((), ())), preferred_element_type=jnp.float32
    )


def contract_cols(left, right):
    return lax.dot_general(
        left, right, (((1,), (1,)), ((), ())), preferred_element_type=jnp.float32
    )


def layer_norm(residual, gain, offset):
    centre = residual - jnp.mean(residual, axis=-1, keepdims=True)
    inv_std = lax.rsqrt(jnp.mean(centre * centre, axis=-1, keepdims=True) + EPSILON)
    normed = centre * inv_std
    return (normed * gain.astype(jnp.float32) + offset.astype(jnp.float32), normed, inv_std)


def norm_grad(upstream, normed, inv_std, gain):
    scaled = upstream * gain.astype(jnp.float32)
    spread = scaled - jnp.mean(scaled, axis=-1, keepdims=True)
    return (spread - normed * jnp.mean(scaled * normed, axis=-1, keepdims=True)) * inv_std


def gelu_exact(pre_act):
    return 0.5 * pre_act * (1.0 + lax.erf(pre_act * ROOT_HALF))


def gelu_slope(pre_act):
    return (
        0.5 * (1.0 + lax.erf(pre_act * ROOT_HALF))
        + pre_act * jnp.exp(-0.5 * pre_act * pre_act) * INV_ROOT_TAU
    )


def split_heads(rows):
    return rows.reshape(rows.shape[0], rows.shape[1] // HEAD_DIM, HEAD_DIM)


def attend(query_rows, key_rows, value_rows):
    score_scale = HEAD_DIM ** (-0.5)
    query_heads = split_heads(query_rows)
    key_heads = split_heads(key_rows)
    value_heads = split_heads(value_rows)
    scores = (
        jnp.einsum("qhd,khd->hqk", query_heads, key_heads, preferred_element_type=jnp.float32)
        * score_scale
    )
    row_top = jnp.max(scores, axis=-1, keepdims=True)
    log_total = row_top + jnp.log(jnp.sum(jnp.exp(scores - row_top), axis=-1, keepdims=True))
    weights = jnp.exp(scores - log_total)
    context = jnp.einsum(
        "hqk,khd->qhd",
        weights.astype(jnp.bfloat16),
        value_heads,
        preferred_element_type=jnp.float32,
    )
    return (context.reshape(query_rows.shape).astype(jnp.bfloat16), weights)


def attend_back(query_rows, key_rows, value_rows, weights, context_gradient):
    score_scale = HEAD_DIM ** (-0.5)
    row_shape = query_rows.shape
    query_heads = split_heads(query_rows)
    key_heads = split_heads(key_rows)
    value_heads = split_heads(value_rows)
    gradient_heads = split_heads(context_gradient)
    value_gradient = jnp.einsum(
        "hqk,qhd->khd",
        weights.astype(jnp.bfloat16),
        gradient_heads,
        preferred_element_type=jnp.float32,
    )
    prob_gradient = jnp.einsum(
        "qhd,khd->hqk", gradient_heads, value_heads, preferred_element_type=jnp.float32
    )
    score_gradient = (
        weights
        * (prob_gradient - jnp.sum(weights * prob_gradient, axis=-1, keepdims=True))
        * score_scale
    ).astype(jnp.bfloat16)
    query_gradient = jnp.einsum(
        "hqk,khd->qhd", score_gradient, key_heads, preferred_element_type=jnp.float32
    )
    key_gradient = jnp.einsum(
        "hqk,qhd->khd", score_gradient, query_heads, preferred_element_type=jnp.float32
    )
    return tuple(
        part.reshape(row_shape).astype(jnp.bfloat16)
        for part in (query_gradient, key_gradient, value_gradient)
    )


VECTORS = (0, 1, 3, 6, 8, 9, 10, 12, 14)
MATRICES = (2, 4, 5, 7, 11, 13)
PAD_ROWS = 16


def cut_columns(rows, width):
    blocks = rows.shape[-1] // width
    if blocks == 1:
        return rows
    return jnp.concatenate(
        [rows[..., i * width : (i + 1) * width] for i in range(blocks)], axis=-2
    )


def join_columns(rows, blocks):
    if blocks == 1:
        return rows
    size = rows.shape[-2] // blocks
    return jnp.concatenate(
        [rows[..., i * size : (i + 1) * size, :] for i in range(blocks)], axis=-1
    )


def gather_layer(shards, width):
    pieces = [cut_columns(shards[i], width) for i in MATRICES]
    vector = jnp.concatenate([shards[i] for i in VECTORS])
    vector = jnp.pad(vector, (0, PAD_ROWS * width - vector.shape[0]))
    pieces.append(vector.reshape(PAD_ROWS, width))
    packed = lax.all_gather(jnp.concatenate(pieces, axis=0), "fsdp", axis=0, tiled=False)
    params = [None] * len(shards)
    start = 0
    for i in MATRICES:
        blocks = shards[i].shape[1] // width
        size = shards[i].shape[0] * blocks
        part = join_columns(packed[:, start : start + size], blocks)
        params[i] = part.reshape(-1, shards[i].shape[1])
        start += size
    vectors = packed[:, start:].reshape(packed.shape[0], -1)
    start = 0
    for i in VECTORS:
        size = shards[i].shape[0]
        params[i] = vectors[:, start : start + size].reshape(-1)
        start += size
    return params


def reduce_gradients(gradients, shards, width, seq_size, seq_index, fsdp_size):
    part_width = width // seq_size
    pieces = []
    for i in MATRICES:
        blocks = shards[i].shape[1] // width
        rows = gradients[i].astype(jnp.bfloat16)
        rows = rows.reshape(fsdp_size, shards[i].shape[0], rows.shape[1])
        pieces.append(cut_columns(rows, part_width))
    vector = jnp.concatenate(
        [gradients[i].reshape(fsdp_size, -1) for i in VECTORS], axis=1
    ).astype(jnp.bfloat16)
    vector = jnp.pad(vector, ((0, 0), (0, PAD_ROWS * width - vector.shape[1])))
    vector = vector.reshape(fsdp_size, PAD_ROWS * seq_size, part_width)
    pieces.append(lax.dynamic_slice_in_dim(vector, seq_index * PAD_ROWS, PAD_ROWS, axis=1))
    packed = jnp.concatenate(pieces, axis=1)
    mine = lax.psum_scatter(packed, "fsdp", scatter_dimension=0, tiled=False)
    both = lax.all_gather(mine, "seq", axis=0, tiled=False)
    reduced = [None] * len(shards)
    start = 0
    for i in MATRICES:
        blocks = shards[i].shape[1] // width
        size = shards[i].shape[0] * blocks
        part = join_columns(both[:, start : start + size], blocks)
        whole = jnp.concatenate([part[s] for s in range(seq_size)], axis=-1)
        reduced[i] = whole.astype(jnp.float32)[None]
        start += size
    vector = both[:, start:].reshape(-1).astype(jnp.float32)
    start = 0
    for i in VECTORS:
        size = shards[i].shape[0]
        reduced[i] = vector[start : start + size][None]
        start += size
    return reduced


def on_device(frames_in, cotangent, *stacks):
    width = frames_in.shape[2]
    seq_size = lax.axis_size("seq")
    seq_index = lax.axis_index("seq")
    fsdp_size = lax.axis_size("fsdp")
    shards = [stack[0] for stack in stacks]
    own = frames_in.shape[1]

    mine = jnp.stack([frames_in[0], cotangent[0]])
    if seq_size == 2:
        other = lax.ppermute(mine, "seq", [(0, 1), (1, 0)])
        first = seq_index == 0
        rows = jnp.concatenate(
            [jnp.where(first, mine, other), jnp.where(first, other, mine)], axis=1
        )
    else:
        rows = lax.all_gather(mine, "seq", axis=1, tiled=True)
    residual, upstream = rows[0], rows[1]
    params = gather_layer(shards, width)

    def own_columns(matrix):
        size = matrix.shape[1] // seq_size
        return lax.dynamic_slice_in_dim(matrix, seq_index * size, size, axis=1)

    def own_rows(matrix):
        return lax.dynamic_slice_in_dim(matrix, seq_index * own, own, axis=0)[None]

    wide = [None if i in MATRICES else p.astype(jnp.float32) for i, p in enumerate(params)]

    hidden_wide, normed_in, inv_in = layer_norm(residual, params[0], params[1])
    hidden = hidden_wide.astype(jnp.bfloat16)
    query_rows = (matmul(hidden, params[2]) + wide[3]).astype(jnp.bfloat16)
    key_rows = matmul(hidden, params[4]).astype(jnp.bfloat16)
    value_rows = (matmul(hidden, params[5]) + wide[6]).astype(jnp.bfloat16)
    context, weights = attend(query_rows, key_rows, value_rows)
    middle = residual + matmul(context, params[7]) + wide[8]
    mid_wide, normed_mid, inv_mid = layer_norm(middle, params[9], params[10])
    hidden_mid = mid_wide.astype(jnp.bfloat16)
    pre_act = matmul(hidden_mid, params[11]) + wide[12]
    activated = gelu_exact(pre_act).astype(jnp.bfloat16)
    own_activated = own_rows(activated)[0]
    outputs = own_rows(middle)[0] + matmul(own_activated, params[13]) + wide[14]

    gradients = [None] * len(stacks)
    upstream_low = upstream.astype(jnp.bfloat16)
    gradients[13] = contract_rows(activated, own_columns(upstream_low))
    gradients[14] = jnp.sum(upstream, axis=0)
    pre_gradient = contract_cols(upstream_low, params[13]) * gelu_slope(pre_act)
    pre_low = pre_gradient.astype(jnp.bfloat16)
    gradients[11] = contract_rows(hidden_mid, own_columns(pre_low))
    gradients[12] = jnp.sum(pre_gradient, axis=0)
    mid_hidden_gradient = contract_cols(pre_low, params[11])
    gradients[9] = jnp.sum(mid_hidden_gradient * normed_mid, axis=0)
    gradients[10] = jnp.sum(mid_hidden_gradient, axis=0)
    middle_gradient = upstream + norm_grad(mid_hidden_gradient, normed_mid, inv_mid, params[9])
    middle_low = middle_gradient.astype(jnp.bfloat16)
    gradients[7] = contract_rows(context, own_columns(middle_low))
    gradients[8] = jnp.sum(middle_gradient, axis=0)
    context_gradient = contract_cols(middle_low, params[7]).astype(jnp.bfloat16)
    query_gradient, key_gradient, value_gradient = attend_back(
        query_rows, key_rows, value_rows, weights, context_gradient
    )
    gradients[2] = contract_rows(hidden, own_columns(query_gradient))
    gradients[3] = jnp.sum(query_gradient.astype(jnp.float32), axis=0)
    gradients[4] = contract_rows(hidden, own_columns(key_gradient))
    gradients[5] = contract_rows(hidden, own_columns(value_gradient))
    gradients[6] = jnp.sum(value_gradient.astype(jnp.float32), axis=0)
    hidden_gradient = (
        contract_cols(query_gradient, params[2])
        + contract_cols(key_gradient, params[4])
        + contract_cols(value_gradient, params[5])
    )
    gradients[0] = jnp.sum(hidden_gradient * normed_in, axis=0)
    gradients[1] = jnp.sum(hidden_gradient, axis=0)
    input_gradient = middle_gradient + norm_grad(hidden_gradient, normed_in, inv_in, params[0])
    reduced = reduce_gradients(gradients, shards, width, seq_size, seq_index, fsdp_size)
    return (outputs[None], own_rows(input_gradient), *reduced)


MESH = pl.DeviceIdType.MESH
F32 = jnp.float32
BF16 = jnp.bfloat16


def dot_nt(left, right):
    return lax.dot_general(left, right, (((1,), (1,)), ((), ())), preferred_element_type=F32)


def dot_tn(left, right):
    return lax.dot_general(left, right, (((0,), (0,)), ((), ())), preferred_element_type=F32)


def low(values):
    return values.astype(BF16)


def wide(values):
    return values.astype(F32)


def row_mean(values):
    return jnp.mean(values, axis=-1, keepdims=True)


def column_sum(values):
    return jnp.sum(values, axis=0, keepdims=True)


class Sizes:
    def __init__(self, own, width, hidden, fsdp):
        self.own, self.width, self.hidden, self.fsdp = own, width, hidden, fsdp
        self.frames = 2 * own
        self.half = width // 2
        self.ff = hidden // 2
        self.depth = fsdp // 4
        self.rows = width // fsdp
        self.slab = hidden // fsdp // 2


def encoder_kernel(sz, *refs):
    half, ff, depth, rows, slab = sz.half, sz.ff, sz.depth, sz.rows, sz.slab
    own, frames, width, fsdp = sz.own, sz.frames, sz.width, sz.fsdp
    hops = depth - 1
    sub = slab // 2
    (frames_ref, cot_ref, v_fg, v_fb, wq_ref, v_bq, wk_ref, wv_ref, v_bv, wo_ref, v_bo, v_sg, v_sb,
     wu_ref, v_bu, wd_ref, v_bd) = refs[:17]
    (o_out, o_in, o_fg, o_fb, o_wq, o_bq, o_wk, o_wv, o_bv, o_wo, o_bo, o_sg, o_sb, o_wu, o_bu,
     o_wd, o_bd) = refs[17:34]
    (wqkv, wo, wup, wdown, vecg, vfull, bup, rbuf, gbuf, n_in, n_mid, middle, hidden, hmid, stat_in,
     stat_mid, qkv, prob, cbuf, act, slope, plow, mg, upl, mlow, cg, dqkv, mh_part, mh_send, mh_recv, op_part,
     op_send, op_recv, hg_part, hg_send, hg_recv,
     g_d, s_d, t_d, y_d, zs_d, zr_d, xs_d, xr_d, f_d,
     g_e, s_e, t_e, y_e, zs_e, zr_e, xs_e, xr_e, f_e, both_e,
     g_u, s_u, t_u, y_u, zs_u, zr_u, xs_u, xr_u, f_u,
     g_o, s_o, t_o, y_o, zs_o, zr_o, xs_o, xr_o, f_o,
     g_q, s_q, t_q, y_q, zs_q, zr_q, xs_q, xr_q, f_q,
     g_k, s_k, t_k, y_k, zs_k, zr_k, xs_k, xr_k, f_k,
     g_v, s_v, t_v, y_v, zs_v, zr_v, xs_v, xr_v, f_v,
     v0, v1, v2, v3, vs, vy, vz, vx,
     local_sem, ag_send, ag_recv, rs_send, rs_recv, x_send, x_recv) = refs[34:]

    x = lax.axis_index("seq")
    i = lax.axis_index("fsdp")
    z, y, c = i // 4, lax.rem(i // 2, 2), lax.rem(i, 2)

    def at(z_at, y_at, c_at):
        return (x, z_at * 4 + y_at * 2 + c_at)

    sib, ypeer, xpeer = at(z, y, 1 - c), at(z, 1 - y, c), (1 - x, i)
    zother = [lax.rem(z + d, depth) for d in range(1, depth)]
    zpeers = [at(other, y, c) for other in zother]
    inner = jnp.logical_or(z == 1, z == 2)
    beside = z + 1 - 2 * lax.rem(z, 2)
    second = jnp.where(z < 2, 2, 1)
    far_end = 6 - z - beside - second
    near = [beside, second]
    mine = pl.multiple_of(x * half, 128)
    theirs = pl.multiple_of((1 - x) * half, 128)

    local = [
        pltpu.make_async_copy(wq_ref.at[:, pl.ds(mine, half)], wqkv.at[0, i], local_sem.at[0]),
        pltpu.make_async_copy(wk_ref.at[:, pl.ds(mine, half)], wqkv.at[1, i], local_sem.at[1]),
        pltpu.make_async_copy(wv_ref.at[:, pl.ds(mine, half)], wqkv.at[2, i], local_sem.at[2]),
        pltpu.make_async_copy(wo_ref, wo.at[i], local_sem.at[3]),
        pltpu.make_async_copy(wd_ref.at[pl.ds(pl.multiple_of(x * slab, 16), slab)], wdown.at[i], local_sem.at[4]),
        pltpu.make_async_copy(frames_ref, rbuf.at[x], local_sem.at[5]),
        pltpu.make_async_copy(cot_ref, gbuf.at[x], local_sem.at[6]),
    ]
    for copy in local:
        copy.start()

    barrier = pltpu.get_barrier_semaphore()
    partners = [sib, ypeer, xpeer, *zpeers]
    for partner in partners:
        pl.semaphore_signal(barrier, inc=1, device_id=partner, device_id_type=MESH)

    vecg[i] = jnp.zeros(vecg.shape[1:], F32)
    for at_row, ref in enumerate((v_fg, v_fb, v_bq, v_bv, v_bo, v_sg, v_sb, v_bd)):
        vecg[i, at_row : at_row + 1, 0:rows] = wide(ref[...])
    up_bias = wide(v_bu[...])
    vecg[i, 8:9, 0:slab] = up_bias[:, :slab]
    vecg[i, 9:10, 0:slab] = up_bias[:, slab:]

    pl.semaphore_wait(barrier, len(partners))

    started = []

    def send(src, dst, send_sem, recv_sem, to):
        copy = pltpu.make_async_remote_copy(
            src_ref=src, dst_ref=dst, send_sem=send_sem, recv_sem=recv_sem, device_id=to, device_id_type=MESH
        )
        copy.start()
        started.append(copy)

    def arrived(dst, recv_sem):
        pltpu.make_async_remote_copy(
            src_ref=dst, dst_ref=dst, send_sem=recv_sem, recv_sem=recv_sem, device_id=xpeer, device_id_type=MESH
        ).wait_recv()

    def block(piece, b):
        upper, lower = wdown.at[b, 0:sub], wdown.at[b, sub:slab]
        return (wqkv.at[:, b], vecg.at[b], wo.at[b], wup.at[b], upper, lower)[piece]

    def pass_on(piece, b, slot, to):
        send(block(piece, b), block(piece, b), ag_send.at[piece, slot], ag_recv.at[piece, b], to)

    inner_copies = []

    def pass_inner(piece, b, slot, to):
        copy = pltpu.make_async_remote_copy(
            src_ref=block(piece, b), dst_ref=block(piece, b), send_sem=ag_send.at[piece, slot],
            recv_sem=ag_recv.at[piece, b], device_id=to, device_id_type=MESH
        )
        inner_copies.append(copy)

        @pl.when(inner)
        def _():
            copy.start()

    def own_z(piece):
        pass_on(piece, i, 0, at(second, y, c))
        pass_on(piece, i, 1, at(beside, y, c))
        pass_inner(piece, i, 2, at(far_end, y, c))

    def own_near(piece):
        pass_on(piece, i, hops, ypeer)
        pass_on(piece, i, hops + 1, sib)

    def relay_near(piece):
        for n, other in enumerate(near):
            b = other * 4 + y * 2 + c
            arrived(block(piece, b), ag_recv.at[piece, b])
            pass_on(piece, b, hops + 2 + n, ypeer)
            pass_on(piece, b, 2 * hops + 2 + n, sib)

    def relay_far(piece):
        b = far_end * 4 + y * 2 + c
        arrived(block(piece, b), ag_recv.at[piece, b])
        pass_inner(piece, b, 4 * hops + 3, at(beside, y, c))
        pass_on(piece, b, hops + 4, ypeer)
        pass_on(piece, b, 2 * hops + 4, sib)

    def turned_y():
        b = z * 4 + (1 - y) * 2 + c
        arrived(block(5, b), ag_recv.at[5, b])
        pass_on(5, b, 5, at(second, y, c))
        pass_on(5, b, 6, at(beside, y, c))
        pass_inner(5, b, 7, at(far_end, y, c))
        pass_on(5, b, 8, sib)

    def turned_near():
        for n, other in enumerate(near):
            for m in range(2):
                b = other * 4 + m * 2 + c
                arrived(block(5, b), ag_recv.at[5, b])
                pass_on(5, b, 9 + 2 * n + m, sib)

    def turned_far():
        for m in range(2):
            b = far_end * 4 + m * 2 + c
            arrived(block(5, b), ag_recv.at[5, b])
            pass_inner(5, b, 13 + m, at(beside, y, c))
            pass_on(5, b, 15 + m, sib)

    def relay_y(piece):
        for n, other in enumerate((z, beside, second, far_end)):
            b = other * 4 + (1 - y) * 2 + c
            arrived(block(piece, b), ag_recv.at[piece, b])
            pass_on(piece, b, 3 * hops + 2 + n, sib)

    def finish(piece):
        for k in range(2 * depth):
            b = 2 * k + (1 - c)
            arrived(block(piece, b), ag_recv.at[piece, b])

    for n in range(3):
        local[n].wait()
    own_z(0)
    own_near(0)
    own_z(1)
    own_near(1)
    local[5].wait()
    send(rbuf.at[x], rbuf.at[x], x_send.at[0], x_recv.at[0], xpeer)
    local[3].wait()
    own_z(2)
    own_near(2)
    local[6].wait()
    send(gbuf.at[x], gbuf.at[x], x_send.at[1], x_recv.at[1], xpeer)
    up = wide(wu_ref[...])
    picked = []
    for b in range(fsdp):
        left = up[:, 2 * slab * b : 2 * slab * b + slab]
        right = up[:, 2 * slab * b + slab : 2 * slab * (b + 1)]
        picked.append(jnp.where(x == 0, left, right))
    wup[i] = low(jnp.concatenate(picked, axis=1))
    own_near(3)
    local[4].wait()
    own_near(4)
    own_near(5)

    relay_near(0)
    relay_near(1)
    own_z(3)
    relay_far(0)
    relay_far(1)
    relay_near(2)
    own_z(4)
    relay_y(0)
    relay_y(1)
    finish(1)
    for b in range(fsdp):
        vfull[:, rows * b : rows * (b + 1)] = vecg[b, 0:8, 0:rows]
        bup[:, slab * b : slab * (b + 1)] = jnp.where(x == 0, vecg[b, 8:9, 0:slab], vecg[b, 9:10, 0:slab])
    v0[...] = jnp.zeros_like(v0)

    step = own // 2

    def by_rows(body):
        def one(n, carry):
            s = n // 2
            r0 = pl.multiple_of(lax.rem(n, 2) * step, step)
            body(s, pl.ds(r0, step), pl.ds(pl.multiple_of(n * step, step), step))
            return carry

        lax.fori_loop(0, 4, one, 0)

    arrived(rbuf.at[1 - x], x_recv.at[0])

    def norm_first(s, part, whole):
        r = rbuf[s, part, :]
        centre = r - row_mean(r)
        inv = lax.rsqrt(row_mean(centre * centre) + EPSILON)
        normed = centre * inv
        n_in[s, part, :] = normed
        stat_in[s, part, :] = jnp.broadcast_to(inv, (step, 128))
        hidden[whole, :] = low(normed * vfull[0:1, :] + vfull[1:2, :])

    by_rows(norm_first)
    relay_far(2)
    finish(0)
    for m, bias in ((0, 2), (1, None), (2, 3)):
        made = jnp.dot(hidden[...], wqkv[m].reshape(width, half), preferred_element_type=F32)
        if bias is not None:
            made = made + vfull[bias : bias + 1, pl.ds(mine, half)]
        qkv[m] = low(made)

    first_lane = lax.broadcasted_iota(jnp.int32, (frames, 2 * HEAD_DIM), 1) < HEAD_DIM
    scale = HEAD_DIM**-0.5

    def masked(pair, which):
        keep = first_lane if which == 0 else jnp.logical_not(first_lane)
        return jnp.where(keep, pair, jnp.zeros_like(pair))

    for pair in range(half // (2 * HEAD_DIM)):
        lanes = slice(pair * 2 * HEAD_DIM, (pair + 1) * 2 * HEAD_DIM)
        q2, k2, v2_ = qkv[0, :, lanes], qkv[1, :, lanes], qkv[2, :, lanes]
        parts = []
        for which in range(2):
            scores = dot_nt(masked(q2, which), k2) * scale
            raised = jnp.exp(scores - jnp.max(scores, axis=-1, keepdims=True))
            weights = raised * (1.0 / jnp.sum(raised, axis=-1, keepdims=True))
            prob[2 * pair + which] = weights
            parts.append(jnp.dot(low(weights), v2_, preferred_element_type=F32))
        cbuf[x, :, lanes] = low(jnp.where(first_lane, parts[0], parts[1]))
        if pair == 0:
            relay_y(2)
        if pair == 1:
            relay_near(3)
            own_z(5)
            turned_y()
    send(cbuf.at[x], cbuf.at[x], x_send.at[2], x_recv.at[2], xpeer)
    finish(2)
    relay_far(3)
    arrived(cbuf.at[1 - x], x_recv.at[2])
    context = jnp.concatenate([cbuf[0], cbuf[1]], axis=1)
    for n in range(2):
        cols = slice(n * half, (n + 1) * half)
        made = jnp.dot(context, wo[:, :, cols].reshape(width, half), preferred_element_type=F32)
        made = made + vfull[4:5, cols]
        for s in range(2):
            middle[s, :, cols] = rbuf[s, :, cols] + made[s * own : (s + 1) * own]

    def norm_second(s, part, whole):
        r = middle[s, part, :]
        centre = r - row_mean(r)
        inv = lax.rsqrt(row_mean(centre * centre) + EPSILON)
        normed = centre * inv
        n_mid[s, part, :] = normed
        stat_mid[s, part, :] = jnp.broadcast_to(inv, (step, 128))
        hmid[whole, :] = low(normed * vfull[5:6, :] + vfull[6:7, :])

    by_rows(norm_second)
    relay_near(4)
    relay_y(3)
    arrived(gbuf.at[1 - x], x_recv.at[1])
    for s in range(2):
        upl[s * own : (s + 1) * own, :] = low(gbuf[s])
    v0[7:8, :] = column_sum(gbuf[0]) + column_sum(gbuf[1])
    finish(3)

    chunk = 4 * slab
    chunks = ff // chunk

    def up_chunk(n, carry):
        cols = pl.ds(pl.multiple_of(n * chunk, 128), chunk)
        pre = jnp.dot(hmid[...], wup[:, :, cols].reshape(width, chunk), preferred_element_type=F32)
        pre = pre + bup[:, cols]
        bell = 0.5 * (1.0 + lax.erf(pre * ROOT_HALF))
        act[:, cols] = low(pre * bell)
        slope[:, cols] = bell + pre * jnp.exp(-0.5 * pre * pre) * INV_ROOT_TAU
        return carry

    lax.fori_loop(0, chunks, up_chunk, 0)
    relay_far(4)

    pieces = {
        "d": (0, g_d, s_d, t_d, y_d, zs_d, zr_d, xs_d, xr_d, f_d),
        "e": (7, g_e, s_e, t_e, y_e, zs_e, zr_e, xs_e, xr_e, f_e),
        "u": (1, g_u, s_u, t_u, y_u, zs_u, zr_u, xs_u, xr_u, f_u),
        "o": (2, g_o, s_o, t_o, y_o, zs_o, zr_o, xs_o, xr_o, f_o),
        "q": (3, g_q, s_q, t_q, y_q, zs_q, zr_q, xs_q, xr_q, f_q),
        "k": (5, g_k, s_k, t_k, y_k, zs_k, zr_k, xs_k, xr_k, f_k),
        "v": (6, g_v, s_v, t_v, y_v, zs_v, zr_v, xs_v, xr_v, f_v),
    }

    def reduce_core(name):
        at_piece, g, s_ = pieces[name][:3]
        send(g.at[:, :, 1 - c], s_, rs_send.at[at_piece, 0], rs_recv.at[at_piece, 0], sib)

    def reduce_y(name):
        at_piece, g, s_, t, yb = pieces[name][:5]
        arrived(s_, rs_recv.at[at_piece, 0])

        def one(n, carry):
            t[n] = low(wide(g[n, 1 - y, c]) + wide(s_[n, 1 - y]))
            return carry

        lax.fori_loop(0, depth, one, 0)
        send(t, yb, rs_send.at[at_piece, 1], rs_recv.at[at_piece, 1], ypeer)

    def reduce_z(name):
        at_piece, g, s_, t, yb, zs, zr, xs, xr, fin = pieces[name]
        arrived(yb, rs_recv.at[at_piece, 1])
        for n, other in enumerate(zother):
            zs[n] = low(wide(g[other, y, c]) + wide(s_[other, y]) + wide(yb[other]))
            send(zs.at[n], zr.at[hops - 1 - n], rs_send.at[at_piece, 2 + n],
                 rs_recv.at[at_piece, 2 + hops - 1 - n], zpeers[n])
        fin[...] = wide(g[z, y, c]) + wide(s_[z, y]) + wide(yb[z])

    def reduce_x(name):
        at_piece, g, s_, t, yb, zs, zr, xs, xr, fin = pieces[name]
        total = fin[...]
        for n in range(hops):
            arrived(zr.at[n], rs_recv.at[at_piece, 2 + n])
            total = total + wide(zr[n])
        fin[...] = total
        xs[...] = low(total)
        send(xs, xr, rs_send.at[at_piece, 2 + hops], rs_recv.at[at_piece, 2 + hops], xpeer)

    def turned_send():
        arrived(s_e, rs_recv.at[7, 0])
        for n, other in enumerate(zother):
            zs_e[n] = low(wide(g_e[other, :, c]) + wide(s_e[other]))
            send(zs_e.at[n], zr_e.at[hops - 1 - n], rs_send.at[7, 2 + n], rs_recv.at[7, 2 + hops - 1 - n], zpeers[n])
        both_e[...] = wide(g_e[z, :, c]) + wide(s_e[z])

    def turned_over():
        for n in range(hops):
            arrived(zr_e.at[n], rs_recv.at[7, 2 + n])
            both_e[...] = both_e[...] + wide(zr_e[n])
        t_e[0] = low(both_e[1 - y])
        send(t_e.at[0], y_e.at[0], rs_send.at[7, 1], rs_recv.at[7, 1], ypeer)

    def turned_x():
        arrived(y_e.at[0], rs_recv.at[7, 1])
        f_e[...] = both_e[y] + wide(y_e[0])
        xs_e[...] = low(f_e[...])
        send(xs_e, xr_e, rs_send.at[7, 2 + hops], rs_recv.at[7, 2 + hops], xpeer)

    def reduced(name):
        at_piece, g, s_, t, yb, zs, zr, xs, xr, fin = pieces[name]
        arrived(xr, rs_recv.at[at_piece, 2 + hops])
        return fin, xr

    def down_chunk(n, carry):
        cols = pl.ds(pl.multiple_of(n * chunk, 128), chunk)
        made = low(dot_tn(act[:, cols], upl[...]))
        made = made.reshape(2, 2, 2, sub, width)
        g_d[n] = made[:, :, 0]
        g_e[n] = made[:, :, 1]
        return carry

    lax.fori_loop(0, chunks, down_chunk, 0)
    reduce_core("e")
    reduce_core("d")
    turned_near()
    relay_y(4)
    turned_far()
    reduce_y("d")
    turned_send()
    finish(4)
    finish(5)


    def back_chunk(n, carry):
        cols = pl.ds(pl.multiple_of(n * chunk, 128), chunk)
        rhs = wdown[pl.ds(n * 4, 4)].reshape(chunk, width)
        pg = dot_nt(upl[...], rhs) * slope[:, cols]
        plow[:, cols] = low(pg)
        bup_sum[:, cols] = column_sum(pg)
        return carry

    bup_sum = bup
    lax.fori_loop(0, chunks, back_chunk, 0)
    for n in range(2):
        cols = slice(n * half, (n + 1) * half)
        made = dot_nt(plow[...], wup[n * fsdp // 2 : (n + 1) * fsdp // 2].reshape(half, ff))
        mh_part[:, cols] = made
        mh_send[n] = low(made)
        send(mh_send.at[n], mh_recv.at[n], x_send.at[3 + 3 * n], x_recv.at[3 + 3 * n], xpeer)

    def up_back(n, carry):
        cols = pl.ds(pl.multiple_of(n * chunk, 128), chunk)
        made = low(dot_tn(hmid[...], plow[:, cols]))
        g_u[:, :, :, :, cols] = made.reshape(depth, 2, 2, rows, chunk)
        return carry

    lax.fori_loop(0, chunks, up_back, 0)
    reduce_core("u")
    reduce_z("d")

    for n in range(2):
        cols = slice(n * half, (n + 1) * half)
        made = jnp.dot(act[...], wdown[:, :, cols].reshape(ff, half), preferred_element_type=F32)
        for s in range(2):
            op_part[s, :, cols] = made[s * own : (s + 1) * own]
    op_send[...] = low(op_part[1 - x])
    send(op_send, op_recv, x_send.at[4], x_recv.at[4], xpeer)
    reduce_y("u")

    arrived(mh_recv.at[0], x_recv.at[3])
    arrived(mh_recv.at[1], x_recv.at[6])
    only = jnp.where(x == 0, 1.0, 0.0)

    def norm_second_back(s, part, whole):
        total = mh_part[whole, :] + wide(jnp.concatenate([mh_recv[0, whole, :], mh_recv[1, whole, :]], axis=1))
        normed = n_mid[s, part, :]
        v0[5:6, :] += only * column_sum(total * normed)
        v0[6:7, :] += only * column_sum(total)
        scaled = total * vfull[5:6, :]
        spread = scaled - row_mean(scaled) - normed * row_mean(scaled * normed)
        made = gbuf[s, part, :] + spread * stat_mid[s, part, 0:1]
        mg[s, part, :] = made
        mlow[whole, :] = low(made)
        v0[4:5, :] += only * column_sum(made)

    by_rows(norm_second_back)
    v0[7:8, :] = only * v0[7:8, :]
    cg[...] = low(dot_nt(mlow[...], wo[pl.ds(x * (fsdp // 2), fsdp // 2)].reshape(half, width)))
    for n in range(2):
        made = low(dot_tn(cbuf[n], mlow[:, pl.ds(mine, half)]))
        g_o[n * depth // 2 : (n + 1) * depth // 2] = made.reshape(depth // 2, 2, 2, rows, half)
    reduce_core("o")

    for pair in range(half // (2 * HEAD_DIM)):
        lanes = slice(pair * 2 * HEAD_DIM, (pair + 1) * 2 * HEAD_DIM)
        q2, k2, v2_, c2 = qkv[0, :, lanes], qkv[1, :, lanes], qkv[2, :, lanes], cg[:, lanes]
        parts = []
        for which in range(2):
            weights = prob[2 * pair + which]
            dv = dot_tn(low(weights), c2)
            dp = dot_nt(masked(c2, which), v2_)
            ds = low(weights * (dp - jnp.sum(weights * dp, axis=-1, keepdims=True)) * scale)
            parts.append((jnp.dot(ds, k2, preferred_element_type=F32), dot_tn(ds, q2), dv))
        for m in range(3):
            dqkv[m, :, lanes] = low(jnp.where(first_lane, parts[0][m], parts[1][m]))
    reduce_y("o")
    turned_over()
    for m, g, name in ((0, g_q, "q"), (1, g_k, "k"), (2, g_v, "v")):
        made = low(dot_tn(hidden[...], dqkv[m]))
        g[...] = made.reshape(depth, 2, 2, rows, half)
        reduce_core(name)
        if m > 0:
            reduce_y("qk"[m - 1])
    v0[2:3, pl.ds(mine, half)] = column_sum(wide(dqkv[0]))
    v0[3:4, pl.ds(mine, half)] = column_sum(wide(dqkv[2]))
    reduce_z("u")
    for n in range(2):
        cols = slice(n * half, (n + 1) * half)
        some = slice(n * fsdp // 2, (n + 1) * fsdp // 2)
        made = dot_nt(dqkv[0], wqkv[0, some].reshape(half, half))
        made = made + dot_nt(dqkv[1], wqkv[1, some].reshape(half, half))
        made = made + dot_nt(dqkv[2], wqkv[2, some].reshape(half, half))
        for s in range(2):
            hg_part[s, :, cols] = made[s * own : (s + 1) * own]
    hg_send[...] = low(hg_part[1 - x])
    send(hg_send, hg_recv, x_send.at[5], x_recv.at[5], xpeer)
    reduce_y("v")
    v0[0:1, :] = column_sum(hg_part[0] * n_in[0]) + column_sum(hg_part[1] * n_in[1])
    v0[1:2, :] = column_sum(hg_part[0]) + column_sum(hg_part[1])
    per = ff // width
    for n in range(per):
        sums = bup_sum[:, n * width : (n + 1) * width]
        v0[8 + n : 9 + n, :] = jnp.where(x == 0, sums, jnp.zeros_like(sums))
        v0[8 + per + n : 9 + per + n, :] = jnp.where(x == 0, jnp.zeros_like(sums), sums)
    send(v0, vs, rs_send.at[4, 0], rs_recv.at[4, 0], sib)
    reduce_z("o")
    reduce_z("q")
    reduce_x("d")
    arrived(vs, rs_recv.at[4, 0])
    v1[...] = v0[...] + vs[...]
    send(v1, vy, rs_send.at[4, 1], rs_recv.at[4, 1], ypeer)

    arrived(op_recv, x_recv.at[4])
    reduce_z("k")
    o_out[...] = middle[x] + (op_part[x] + wide(op_recv[...])) + vfull[7:8, :]
    arrived(hg_recv, x_recv.at[5])
    total = hg_part[x] + wide(hg_recv[...])
    normed = n_in[x]
    scaled = total * vfull[0:1, :]
    spread = scaled - row_mean(scaled) - normed * row_mean(scaled * normed)
    o_in[...] = mg[x] + spread * stat_in[x, :, 0:1]

    reduce_z("v")
    reduce_x("u")
    turned_x()
    arrived(vy, rs_recv.at[4, 1])
    v2[...] = v1[...] + vy[...]
    for n in range(hops):
        send(v2, vz.at[hops - 1 - n], rs_send.at[4, 2 + n], rs_recv.at[4, 2 + hops - 1 - n], zpeers[n])
    reduce_x("o")
    reduce_x("q")
    reduce_x("k")
    reduce_x("v")
    total = v2[...]
    for n in range(hops):
        arrived(vz.at[n], rs_recv.at[4, 2 + n])
        total = total + vz[n]
    v3[...] = total
    send(v3, vx, rs_send.at[4, 2 + hops], rs_recv.at[4, 2 + hops], xpeer)

    fin, got = reduced("d")
    o_wd[pl.ds(pl.multiple_of(x * slab, 16), sub), :] = fin[...]
    o_wd[pl.ds(pl.multiple_of((1 - x) * slab, 16), sub), :] = wide(got[...])
    fin, got = reduced("e")
    o_wd[pl.ds(pl.multiple_of(x * slab + sub, 16), sub), :] = fin[...]
    o_wd[pl.ds(pl.multiple_of((1 - x) * slab + sub, 16), sub), :] = wide(got[...])
    fin, got = reduced("u")
    one, two = fin[...], wide(got[...])
    left, right = jnp.where(x == 0, one, two), jnp.where(x == 0, two, one)
    woven = []
    for b in range(fsdp):
        woven.append(left[:, b * slab : (b + 1) * slab])
        woven.append(right[:, b * slab : (b + 1) * slab])
    o_wu[...] = jnp.concatenate(woven, axis=1)
    fin, got = reduced("o")
    o_wo[:, pl.ds(mine, half)] = fin[...]
    o_wo[:, pl.ds(theirs, half)] = wide(got[...])
    arrived(vx, rs_recv.at[4, 2 + hops])
    v0_all = v3[...] + vx[...]
    taken = jnp.zeros((8, rows), F32)
    low_part = jnp.zeros((1, slab), F32)
    high_part = jnp.zeros((1, slab), F32)
    in_row = width // slab
    for b in range(fsdp):
        here = jnp.where(i == b, 1.0, 0.0)
        taken = taken + here * v0_all[0:8, b * rows : (b + 1) * rows]
        at_row, lane = 8 + b // in_row, (b % in_row) * slab
        low_part = low_part + here * v0_all[at_row : at_row + 1, lane : lane + slab]
        high_part = high_part + here * v0_all[at_row + per : at_row + per + 1, lane : lane + slab]
    for at_row, ref in enumerate((o_fg, o_fb, o_bq, o_bv, o_bo, o_sg, o_sb, o_bd)):
        ref[...] = taken[at_row : at_row + 1]
    o_bu[...] = jnp.concatenate([low_part, high_part], axis=1)
    for name, ref in (("q", o_wq), ("k", o_wk), ("v", o_wv)):
        fin, got = reduced(name)
        ref[:, pl.ds(mine, half)] = fin[...]
        ref[:, pl.ds(theirs, half)] = wide(got[...])

    for copy in started:
        copy.wait_send()
    for copy in inner_copies:
        pl.when(inner)(copy.wait_send)


def hand_over(*refs):
    count = (len(refs) - 2) // 3
    came, gone = refs[-2:]
    held = refs[2 * count : 3 * count]
    into = [pltpu.make_async_copy(refs[n], held[n], came.at[n]) for n in range(count)]
    out = [pltpu.make_async_copy(held[n], refs[count + n], gone.at[n]) for n in range(count)]
    for copy in into:
        copy.start()
    for n in range(count):
        into[n].wait()
        out[n].start()
    for copy in out:
        copy.wait()


def fused_on_device(frames_in, cotangent, *stacks):
    fsdp = lax.axis_size("fsdp")
    own, width = frames_in.shape[1:]
    sz = Sizes(own, width, stacks[13].shape[1] * fsdp, fsdp)
    half, ff, depth, rows, slab, frames = sz.half, sz.ff, sz.depth, sz.rows, sz.slab, sz.frames
    args = [frames_in[0], cotangent[0]] + [s if s.ndim == 2 else s[0] for s in stacks]
    in_hbm = {0, 1, 4, 6, 7, 9, 15}
    whole = pl.BlockSpec(memory_space=pltpu.VMEM)
    outs = [jax.ShapeDtypeStruct(a.shape, F32) for a in args]

    def vm(dtype, *dims):
        return pltpu.VMEM(dims, dtype)

    def reduce_scratch(r, w, *both):
        return [
            vm(BF16, depth, 2, 2, r, w), vm(BF16, depth, 2, r, w), vm(BF16, depth, r, w),
            vm(BF16, depth, r, w), vm(BF16, depth - 1, *both, r, w), vm(BF16, depth - 1, *both, r, w),
            vm(BF16, r, w), vm(BF16, r, w), vm(F32, r, w),
        ]

    heads = half // HEAD_DIM
    scratch = [
        vm(BF16, 3, fsdp, rows, half), vm(BF16, fsdp, rows, width), vm(BF16, fsdp, rows, ff),
        vm(BF16, fsdp, slab, width), vm(F32, fsdp, 16, 128), vm(F32, 8, width), vm(F32, 1, ff),
        vm(F32, 2, own, width), vm(F32, 2, own, width), vm(F32, 2, own, width), vm(F32, 2, own, width),
        vm(F32, 2, own, width), vm(BF16, frames, width), vm(BF16, frames, width),
        vm(F32, 2, own, 128), vm(F32, 2, own, 128), vm(BF16, 3, frames, half),
        vm(F32, heads, frames, frames), vm(BF16, 2, frames, half), vm(BF16, frames, ff),
        vm(F32, frames, ff), vm(BF16, frames, ff), vm(F32, 2, own, width), vm(BF16, frames, width),
        vm(BF16, frames, width), vm(BF16, frames, half), vm(BF16, 3, frames, half),
        vm(F32, frames, width), vm(BF16, 2, frames, half), vm(BF16, 2, frames, half),
        vm(F32, 2, own, width), vm(BF16, own, width), vm(BF16, own, width),
        vm(F32, 2, own, width), vm(BF16, own, width), vm(BF16, own, width),
        *reduce_scratch(slab // 2, width), *reduce_scratch(slab // 2, width, 2), vm(F32, 2, slab // 2, width),
        *reduce_scratch(rows, ff), *reduce_scratch(rows, half),
        *reduce_scratch(rows, half), *reduce_scratch(rows, half), *reduce_scratch(rows, half),
        vm(F32, 16, width), vm(F32, 16, width), vm(F32, 16, width), vm(F32, 16, width),
        vm(F32, 16, width), vm(F32, 16, width), vm(F32, depth - 1, 16, width), vm(F32, 16, width),
        pltpu.SemaphoreType.DMA((7,)),
        pltpu.SemaphoreType.DMA((6, 4 * depth + 2)), pltpu.SemaphoreType.DMA((6, fsdp)),
        pltpu.SemaphoreType.DMA((8, depth + 2)), pltpu.SemaphoreType.DMA((8, depth + 2)),
        pltpu.SemaphoreType.DMA((7,)), pltpu.SemaphoreType.DMA((7,)),
    ]
    made = pl.pallas_call(
        functools.partial(encoder_kernel, sz),
        out_shape=outs,
        in_specs=[pl.BlockSpec(memory_space=pl.ANY) if n in in_hbm else whole for n in range(len(args))],
        out_specs=[whole] * len(outs),
        scratch_shapes=scratch,
        compiler_params=pltpu.CompilerParams(
            collective_id=0, has_side_effects=True, vmem_limit_bytes=60 * 2**20
        ),
    )(*args)
    anywhere = [pl.BlockSpec(memory_space=pl.ANY)] * len(outs)
    made = pl.pallas_call(
        hand_over,
        out_shape=outs,
        in_specs=anywhere,
        out_specs=anywhere,
        scratch_shapes=[vm(F32, *o.shape) for o in outs] + [pltpu.SemaphoreType.DMA((len(outs),))] * 2,
    )(*made)
    return tuple(o if p.ndim == 2 else o[None] for o, p in zip(made, (frames_in, cotangent, *stacks)))


def fits_kernel(mesh, frames_in, up_weight):
    seq, fsdp = mesh.shape["seq"], mesh.shape["fsdp"]
    width, hidden = up_weight.shape[1:]
    return (
        seq == 2
        and fsdp == 16
        and frames_in.shape[0] == fsdp
        and frames_in.shape[1] % 64 == 0
        and width % (16 * fsdp) == 0
        and width % 256 == 0
        and hidden % (64 * fsdp) == 0
        and hidden * 2 % (128 * fsdp) == 0
        and hidden == 4 * width
    )


def solution(mesh):
    def build(body):
        return jax.shard_map(
            body,
            mesh=mesh,
            in_specs=(
                P("fsdp", "seq", None),
                P("fsdp", "seq", None),
                P(None, "fsdp"),
                P(None, "fsdp"),
                P(None, "fsdp", None),
                P(None, "fsdp"),
                P(None, "fsdp", None),
                P(None, "fsdp", None),
                P(None, "fsdp"),
                P(None, "fsdp", None),
                P(None, "fsdp"),
                P(None, "fsdp"),
                P(None, "fsdp"),
                P(None, "fsdp", None),
                P(None, "fsdp"),
                P(None, "fsdp", None),
                P(None, "fsdp"),
            ),
            out_specs=(
                P("fsdp", "seq", None),
                P("fsdp", "seq", None),
                P(None, "fsdp"),
                P(None, "fsdp"),
                P(None, "fsdp", None),
                P(None, "fsdp"),
                P(None, "fsdp", None),
                P(None, "fsdp", None),
                P(None, "fsdp"),
                P(None, "fsdp", None),
                P(None, "fsdp"),
                P(None, "fsdp"),
                P(None, "fsdp"),
                P(None, "fsdp", None),
                P(None, "fsdp"),
                P(None, "fsdp", None),
                P(None, "fsdp"),
            ),
            check_vma=False,
        )

    def run(*arrays):
        body = fused_on_device if fits_kernel(mesh, arrays[0], arrays[13]) else on_device
        return build(body)(*arrays)

    return run
```

```python
import functools

import jax
import jax.numpy as jnp
from jax import lax
from jax.experimental import pallas as pl
from jax.experimental.pallas import tpu as pltpu
from jax.sharding import PartitionSpec as P

HEAD_DIM = 64


EPSILON = 1e-05
ROOT_HALF = 0.7071067811865476
INV_ROOT_TAU = 0.3989422804014327


def matmul(left, right):
    return jnp.dot(left, right, preferred_element_type=jnp.float32)


def contract_rows(left, right):
    return lax.dot_general(
        left, right, (((0,), (0,)), ((), ())), preferred_element_type=jnp.float32
    )


def contract_cols(left, right):
    return lax.dot_general(
        left, right, (((1,), (1,)), ((), ())), preferred_element_type=jnp.float32
    )


def layer_norm(residual, gain, offset):
    centre = residual - jnp.mean(residual, axis=-1, keepdims=True)
    inv_std = lax.rsqrt(jnp.mean(centre * centre, axis=-1, keepdims=True) + EPSILON)
    normed = centre * inv_std
    return (normed * gain.astype(jnp.float32) + offset.astype(jnp.float32), normed, inv_std)


def norm_grad(upstream, normed, inv_std, gain):
    scaled = upstream * gain.astype(jnp.float32)
    spread = scaled - jnp.mean(scaled, axis=-1, keepdims=True)
    return (spread - normed * jnp.mean(scaled * normed, axis=-1, keepdims=True)) * inv_std


def gelu_exact(pre_act):
    return 0.5 * pre_act * (1.0 + lax.erf(pre_act * ROOT_HALF))


def gelu_slope(pre_act):
    return (
        0.5 * (1.0 + lax.erf(pre_act * ROOT_HALF))
        + pre_act * jnp.exp(-0.5 * pre_act * pre_act) * INV_ROOT_TAU
    )


def split_heads(rows):
    return rows.reshape(rows.shape[0], rows.shape[1] // HEAD_DIM, HEAD_DIM)


def attend(query_rows, key_rows, value_rows):
    score_scale = HEAD_DIM ** (-0.5)
    query_heads = split_heads(query_rows)
    key_heads = split_heads(key_rows)
    value_heads = split_heads(value_rows)
    scores = (
        jnp.einsum("qhd,khd->hqk", query_heads, key_heads, preferred_element_type=jnp.float32)
        * score_scale
    )
    row_top = jnp.max(scores, axis=-1, keepdims=True)
    log_total = row_top + jnp.log(jnp.sum(jnp.exp(scores - row_top), axis=-1, keepdims=True))
    weights = jnp.exp(scores - log_total)
    context = jnp.einsum(
        "hqk,khd->qhd",
        weights.astype(jnp.bfloat16),
        value_heads,
        preferred_element_type=jnp.float32,
    )
    return (context.reshape(query_rows.shape).astype(jnp.bfloat16), weights)


def attend_back(query_rows, key_rows, value_rows, weights, context_gradient):
    score_scale = HEAD_DIM ** (-0.5)
    row_shape = query_rows.shape
    query_heads = split_heads(query_rows)
    key_heads = split_heads(key_rows)
    value_heads = split_heads(value_rows)
    gradient_heads = split_heads(context_gradient)
    value_gradient = jnp.einsum(
        "hqk,qhd->khd",
        weights.astype(jnp.bfloat16),
        gradient_heads,
        preferred_element_type=jnp.float32,
    )
    prob_gradient = jnp.einsum(
        "qhd,khd->hqk", gradient_heads, value_heads, preferred_element_type=jnp.float32
    )
    score_gradient = (
        weights
        * (prob_gradient - jnp.sum(weights * prob_gradient, axis=-1, keepdims=True))
        * score_scale
    ).astype(jnp.bfloat16)
    query_gradient = jnp.einsum(
        "hqk,khd->qhd", score_gradient, key_heads, preferred_element_type=jnp.float32
    )
    key_gradient = jnp.einsum(
        "hqk,qhd->khd", score_gradient, query_heads, preferred_element_type=jnp.float32
    )
    return tuple(
        part.reshape(row_shape).astype(jnp.bfloat16)
        for part in (query_gradient, key_gradient, value_gradient)
    )


VECTORS = (0, 1, 3, 6, 8, 9, 10, 12, 14)
MATRICES = (2, 4, 5, 7, 11, 13)
PAD_ROWS = 16


def cut_columns(rows, width):
    blocks = rows.shape[-1] // width
    if blocks == 1:
        return rows
    return jnp.concatenate(
        [rows[..., i * width : (i + 1) * width] for i in range(blocks)], axis=-2
    )


def join_columns(rows, blocks):
    if blocks == 1:
        return rows
    size = rows.shape[-2] // blocks
    return jnp.concatenate(
        [rows[..., i * size : (i + 1) * size, :] for i in range(blocks)], axis=-1
    )


def gather_layer(shards, width):
    pieces = [cut_columns(shards[i], width) for i in MATRICES]
    vector = jnp.concatenate([shards[i] for i in VECTORS])
    vector = jnp.pad(vector, (0, PAD_ROWS * width - vector.shape[0]))
    pieces.append(vector.reshape(PAD_ROWS, width))
    packed = lax.all_gather(jnp.concatenate(pieces, axis=0), "fsdp", axis=0, tiled=False)
    params = [None] * len(shards)
    start = 0
    for i in MATRICES:
        blocks = shards[i].shape[1] // width
        size = shards[i].shape[0] * blocks
        part = join_columns(packed[:, start : start + size], blocks)
        params[i] = part.reshape(-1, shards[i].shape[1])
        start += size
    vectors = packed[:, start:].reshape(packed.shape[0], -1)
    start = 0
    for i in VECTORS:
        size = shards[i].shape[0]
        params[i] = vectors[:, start : start + size].reshape(-1)
        start += size
    return params


def reduce_gradients(gradients, shards, width, seq_size, seq_index, fsdp_size):
    part_width = width // seq_size
    pieces = []
    for i in MATRICES:
        blocks = shards[i].shape[1] // width
        rows = gradients[i].astype(jnp.bfloat16)
        rows = rows.reshape(fsdp_size, shards[i].shape[0], rows.shape[1])
        pieces.append(cut_columns(rows, part_width))
    vector = jnp.concatenate(
        [gradients[i].reshape(fsdp_size, -1) for i in VECTORS], axis=1
    ).astype(jnp.bfloat16)
    vector = jnp.pad(vector, ((0, 0), (0, PAD_ROWS * width - vector.shape[1])))
    vector = vector.reshape(fsdp_size, PAD_ROWS * seq_size, part_width)
    pieces.append(lax.dynamic_slice_in_dim(vector, seq_index * PAD_ROWS, PAD_ROWS, axis=1))
    packed = jnp.concatenate(pieces, axis=1)
    mine = lax.psum_scatter(packed, "fsdp", scatter_dimension=0, tiled=False)
    both = lax.all_gather(mine, "seq", axis=0, tiled=False)
    reduced = [None] * len(shards)
    start = 0
    for i in MATRICES:
        blocks = shards[i].shape[1] // width
        size = shards[i].shape[0] * blocks
        part = join_columns(both[:, start : start + size], blocks)
        whole = jnp.concatenate([part[s] for s in range(seq_size)], axis=-1)
        reduced[i] = whole.astype(jnp.float32)[None]
        start += size
    vector = both[:, start:].reshape(-1).astype(jnp.float32)
    start = 0
    for i in VECTORS:
        size = shards[i].shape[0]
        reduced[i] = vector[start : start + size][None]
        start += size
    return reduced


def on_device(frames_in, cotangent, *stacks):
    width = frames_in.shape[2]
    seq_size = lax.axis_size("seq")
    seq_index = lax.axis_index("seq")
    fsdp_size = lax.axis_size("fsdp")
    shards = [stack[0] for stack in stacks]
    own = frames_in.shape[1]

    mine = jnp.stack([frames_in[0], cotangent[0]])
    if seq_size == 2:
        other = lax.ppermute(mine, "seq", [(0, 1), (1, 0)])
        first = seq_index == 0
        rows = jnp.concatenate(
            [jnp.where(first, mine, other), jnp.where(first, other, mine)], axis=1
        )
    else:
        rows = lax.all_gather(mine, "seq", axis=1, tiled=True)
    residual, upstream = rows[0], rows[1]
    params = gather_layer(shards, width)

    def own_columns(matrix):
        size = matrix.shape[1] // seq_size
        return lax.dynamic_slice_in_dim(matrix, seq_index * size, size, axis=1)

    def own_rows(matrix):
        return lax.dynamic_slice_in_dim(matrix, seq_index * own, own, axis=0)[None]

    wide = [None if i in MATRICES else p.astype(jnp.float32) for i, p in enumerate(params)]

    hidden_wide, normed_in, inv_in = layer_norm(residual, params[0], params[1])
    hidden = hidden_wide.astype(jnp.bfloat16)
    query_rows = (matmul(hidden, params[2]) + wide[3]).astype(jnp.bfloat16)
    key_rows = matmul(hidden, params[4]).astype(jnp.bfloat16)
    value_rows = (matmul(hidden, params[5]) + wide[6]).astype(jnp.bfloat16)
    context, weights = attend(query_rows, key_rows, value_rows)
    middle = residual + matmul(context, params[7]) + wide[8]
    mid_wide, normed_mid, inv_mid = layer_norm(middle, params[9], params[10])
    hidden_mid = mid_wide.astype(jnp.bfloat16)
    pre_act = matmul(hidden_mid, params[11]) + wide[12]
    activated = gelu_exact(pre_act).astype(jnp.bfloat16)
    own_activated = own_rows(activated)[0]
    outputs = own_rows(middle)[0] + matmul(own_activated, params[13]) + wide[14]

    gradients = [None] * len(stacks)
    upstream_low = upstream.astype(jnp.bfloat16)
    gradients[13] = contract_rows(activated, own_columns(upstream_low))
    gradients[14] = jnp.sum(upstream, axis=0)
    pre_gradient = contract_cols(upstream_low, params[13]) * gelu_slope(pre_act)
    pre_low = pre_gradient.astype(jnp.bfloat16)
    gradients[11] = contract_rows(hidden_mid, own_columns(pre_low))
    gradients[12] = jnp.sum(pre_gradient, axis=0)
    mid_hidden_gradient = contract_cols(pre_low, params[11])
    gradients[9] = jnp.sum(mid_hidden_gradient * normed_mid, axis=0)
    gradients[10] = jnp.sum(mid_hidden_gradient, axis=0)
    middle_gradient = upstream + norm_grad(mid_hidden_gradient, normed_mid, inv_mid, params[9])
    middle_low = middle_gradient.astype(jnp.bfloat16)
    gradients[7] = contract_rows(context, own_columns(middle_low))
    gradients[8] = jnp.sum(middle_gradient, axis=0)
    context_gradient = contract_cols(middle_low, params[7]).astype(jnp.bfloat16)
    query_gradient, key_gradient, value_gradient = attend_back(
        query_rows, key_rows, value_rows, weights, context_gradient
    )
    gradients[2] = contract_rows(hidden, own_columns(query_gradient))
    gradients[3] = jnp.sum(query_gradient.astype(jnp.float32), axis=0)
    gradients[4] = contract_rows(hidden, own_columns(key_gradient))
    gradients[5] = contract_rows(hidden, own_columns(value_gradient))
    gradients[6] = jnp.sum(value_gradient.astype(jnp.float32), axis=0)
    hidden_gradient = (
        contract_cols(query_gradient, params[2])
        + contract_cols(key_gradient, params[4])
        + contract_cols(value_gradient, params[5])
    )
    gradients[0] = jnp.sum(hidden_gradient * normed_in, axis=0)
    gradients[1] = jnp.sum(hidden_gradient, axis=0)
    input_gradient = middle_gradient + norm_grad(hidden_gradient, normed_in, inv_in, params[0])
    reduced = reduce_gradients(gradients, shards, width, seq_size, seq_index, fsdp_size)
    return (outputs[None], own_rows(input_gradient), *reduced)


MESH = pl.DeviceIdType.MESH
F32 = jnp.float32
BF16 = jnp.bfloat16


def dot_nt(left, right):
    return lax.dot_general(left, right, (((1,), (1,)), ((), ())), preferred_element_type=F32)


def dot_tn(left, right):
    return lax.dot_general(left, right, (((0,), (0,)), ((), ())), preferred_element_type=F32)


def low(values):
    return values.astype(BF16)


def wide(values):
    return values.astype(F32)


def row_mean(values):
    return jnp.mean(values, axis=-1, keepdims=True)


def column_sum(values):
    return jnp.sum(values, axis=0, keepdims=True)


class Sizes:
    def __init__(self, own, width, hidden, fsdp):
        self.own, self.width, self.hidden, self.fsdp = own, width, hidden, fsdp
        self.frames = 2 * own
        self.half = width // 2
        self.ff = hidden // 2
        self.depth = fsdp // 4
        self.rows = width // fsdp
        self.slab = hidden // fsdp // 2


def encoder_kernel(sz, *refs):
    half, ff, depth, rows, slab = sz.half, sz.ff, sz.depth, sz.rows, sz.slab
    own, frames, width, fsdp = sz.own, sz.frames, sz.width, sz.fsdp
    hops = depth - 1
    sub = slab // 2
    (frames_ref, cot_ref, v_fg, v_fb, wq_ref, v_bq, wk_ref, wv_ref, v_bv, wo_ref, v_bo, v_sg, v_sb,
     wu_ref, v_bu, wd_ref, v_bd) = refs[:17]
    (o_out, o_in, o_fg, o_fb, o_wq, o_bq, o_wk, o_wv, o_bv, o_wo, o_bo, o_sg, o_sb, o_wu, o_bu,
     o_wd, o_bd) = refs[17:34]
    (wqkv, wo, wup, wdown, vecg, vfull, bup, rbuf, gbuf, n_in, n_mid, middle, hidden, hmid, stat_in,
     stat_mid, qkv, prob, cbuf, act, slope, plow, mg, upl, mlow, cg, dqkv, mh_part, mh_send, mh_recv, op_part,
     op_send, op_recv, hg_part, hg_send, hg_recv,
     g_d, s_d, t_d, y_d, zs_d, zr_d, xs_d, xr_d, f_d,
     g_e, s_e, t_e, y_e, zs_e, zr_e, xs_e, xr_e, f_e, both_e,
     g_u0, s_u0, t_u0, y_u0, zs_u0, zr_u0, xs_u0, xr_u0, f_u0,
     g_u1, s_u1, t_u1, y_u1, zs_u1, zr_u1, xs_u1, xr_u1, f_u1,
     g_u2, s_u2, t_u2, y_u2, zs_u2, zr_u2, xs_u2, xr_u2, f_u2,
     g_u3, s_u3, t_u3, y_u3, zs_u3, zr_u3, xs_u3, xr_u3, f_u3,
     g_o, s_o, t_o, y_o, zs_o, zr_o, xs_o, xr_o, f_o,
     g_q, s_q, t_q, y_q, zs_q, zr_q, xs_q, xr_q, f_q,
     g_k, s_k, t_k, y_k, zs_k, zr_k, xs_k, xr_k, f_k,
     g_v, s_v, t_v, y_v, zs_v, zr_v, xs_v, xr_v, f_v,
     v0, v1, v2, v3, vs, vy, vz, vx,
     local_sem, ag_send, ag_recv, rs_send, rs_recv, x_send, x_recv) = refs[34:]

    x = lax.axis_index("seq")
    i = lax.axis_index("fsdp")
    z, y, c = i // 4, lax.rem(i // 2, 2), lax.rem(i, 2)

    def at(z_at, y_at, c_at):
        return (x, z_at * 4 + y_at * 2 + c_at)

    sib, ypeer, xpeer = at(z, y, 1 - c), at(z, 1 - y, c), (1 - x, i)
    zother = [lax.rem(z + d, depth) for d in range(1, depth)]
    zpeers = [at(other, y, c) for other in zother]
    inner = jnp.logical_or(z == 1, z == 2)
    beside = z + 1 - 2 * lax.rem(z, 2)
    second = jnp.where(z < 2, 2, 1)
    far_end = 6 - z - beside - second
    near = [beside, second]
    mine = pl.multiple_of(x * half, 128)
    theirs = pl.multiple_of((1 - x) * half, 128)

    local = [
        pltpu.make_async_copy(wq_ref.at[:, pl.ds(mine, half)], wqkv.at[0, i], local_sem.at[0]),
        pltpu.make_async_copy(wk_ref.at[:, pl.ds(mine, half)], wqkv.at[1, i], local_sem.at[1]),
        pltpu.make_async_copy(wv_ref.at[:, pl.ds(mine, half)], wqkv.at[2, i], local_sem.at[2]),
        pltpu.make_async_copy(wo_ref, wo.at[i], local_sem.at[3]),
        pltpu.make_async_copy(wd_ref.at[pl.ds(pl.multiple_of(x * slab, 16), slab)], wdown.at[i], local_sem.at[4]),
        pltpu.make_async_copy(frames_ref, rbuf.at[x], local_sem.at[5]),
        pltpu.make_async_copy(cot_ref, gbuf.at[x], local_sem.at[6]),
    ]
    for copy in local:
        copy.start()

    barrier = pltpu.get_barrier_semaphore()
    partners = [sib, ypeer, xpeer, *zpeers]
    for partner in partners:
        pl.semaphore_signal(barrier, inc=1, device_id=partner, device_id_type=MESH)

    vecg[i] = jnp.zeros(vecg.shape[1:], F32)
    for at_row, ref in enumerate((v_fg, v_fb, v_bq, v_bv, v_bo, v_sg, v_sb, v_bd)):
        vecg[i, at_row : at_row + 1, 0:rows] = wide(ref[...])
    up_bias = wide(v_bu[...])
    vecg[i, 8:9, 0:slab] = up_bias[:, :slab]
    vecg[i, 9:10, 0:slab] = up_bias[:, slab:]

    pl.semaphore_wait(barrier, len(partners))

    started = []

    def send(src, dst, send_sem, recv_sem, to):
        copy = pltpu.make_async_remote_copy(
            src_ref=src, dst_ref=dst, send_sem=send_sem, recv_sem=recv_sem, device_id=to, device_id_type=MESH
        )
        copy.start()
        started.append(copy)

    def arrived(dst, recv_sem):
        pltpu.make_async_remote_copy(
            src_ref=dst, dst_ref=dst, send_sem=recv_sem, recv_sem=recv_sem, device_id=xpeer, device_id_type=MESH
        ).wait_recv()

    def block(piece, b):
        upper, lower = wdown.at[b, 0:sub], wdown.at[b, sub:slab]
        return (wqkv.at[:, b], vecg.at[b], wo.at[b], wup.at[b], upper, lower)[piece]

    def pass_on(piece, b, slot, to):
        send(block(piece, b), block(piece, b), ag_send.at[piece, slot], ag_recv.at[piece, b], to)

    inner_copies = []

    def pass_inner(piece, b, slot, to):
        copy = pltpu.make_async_remote_copy(
            src_ref=block(piece, b), dst_ref=block(piece, b), send_sem=ag_send.at[piece, slot],
            recv_sem=ag_recv.at[piece, b], device_id=to, device_id_type=MESH
        )
        inner_copies.append(copy)

        @pl.when(inner)
        def _():
            copy.start()

    def own_z(piece):
        pass_on(piece, i, 0, at(second, y, c))
        pass_on(piece, i, 1, at(beside, y, c))
        pass_inner(piece, i, 2, at(far_end, y, c))

    def own_near(piece):
        pass_on(piece, i, hops, ypeer)
        pass_on(piece, i, hops + 1, sib)

    def relay_near(piece):
        for n, other in enumerate(near):
            b = other * 4 + y * 2 + c
            arrived(block(piece, b), ag_recv.at[piece, b])
            pass_on(piece, b, hops + 2 + n, ypeer)
            pass_on(piece, b, 2 * hops + 2 + n, sib)

    def relay_far(piece):
        b = far_end * 4 + y * 2 + c
        arrived(block(piece, b), ag_recv.at[piece, b])
        pass_inner(piece, b, 4 * hops + 3, at(beside, y, c))
        pass_on(piece, b, hops + 4, ypeer)
        pass_on(piece, b, 2 * hops + 4, sib)

    def turned_y():
        b = z * 4 + (1 - y) * 2 + c
        arrived(block(5, b), ag_recv.at[5, b])
        pass_on(5, b, 5, at(second, y, c))
        pass_on(5, b, 6, at(beside, y, c))
        pass_inner(5, b, 7, at(far_end, y, c))
        pass_on(5, b, 8, sib)

    def turned_near():
        for n, other in enumerate(near):
            for m in range(2):
                b = other * 4 + m * 2 + c
                arrived(block(5, b), ag_recv.at[5, b])
                pass_on(5, b, 9 + 2 * n + m, sib)

    def turned_far():
        for m in range(2):
            b = far_end * 4 + m * 2 + c
            arrived(block(5, b), ag_recv.at[5, b])
            pass_inner(5, b, 13 + m, at(beside, y, c))
            pass_on(5, b, 15 + m, sib)

    def relay_y(piece):
        for n, other in enumerate((z, beside, second, far_end)):
            b = other * 4 + (1 - y) * 2 + c
            arrived(block(piece, b), ag_recv.at[piece, b])
            pass_on(piece, b, 3 * hops + 2 + n, sib)

    def finish(piece):
        for k in range(2 * depth):
            b = 2 * k + (1 - c)
            arrived(block(piece, b), ag_recv.at[piece, b])

    for n in range(3):
        local[n].wait()
    own_z(0)
    own_near(0)
    own_z(1)
    own_near(1)
    local[5].wait()
    send(rbuf.at[x], rbuf.at[x], x_send.at[0], x_recv.at[0], xpeer)
    local[3].wait()
    own_z(2)
    own_near(2)
    local[6].wait()
    send(gbuf.at[x], gbuf.at[x], x_send.at[1], x_recv.at[1], xpeer)
    up = wide(wu_ref[...])
    picked = []
    for b in range(fsdp):
        left = up[:, 2 * slab * b : 2 * slab * b + slab]
        right = up[:, 2 * slab * b + slab : 2 * slab * (b + 1)]
        picked.append(jnp.where(x == 0, left, right))
    wup[i] = low(jnp.concatenate(picked, axis=1))
    own_near(3)
    local[4].wait()
    own_near(4)
    own_near(5)

    relay_near(0)
    relay_near(1)
    own_z(3)
    relay_far(0)
    relay_far(1)
    relay_near(2)
    own_z(4)
    relay_y(0)
    relay_y(1)
    finish(1)
    for b in range(fsdp):
        vfull[:, rows * b : rows * (b + 1)] = vecg[b, 0:8, 0:rows]
        bup[:, slab * b : slab * (b + 1)] = jnp.where(x == 0, vecg[b, 8:9, 0:slab], vecg[b, 9:10, 0:slab])
    v0[...] = jnp.zeros_like(v0)

    step = own // 2

    def by_rows(body):
        def one(n, carry):
            s = n // 2
            r0 = pl.multiple_of(lax.rem(n, 2) * step, step)
            body(s, pl.ds(r0, step), pl.ds(pl.multiple_of(n * step, step), step))
            return carry

        lax.fori_loop(0, 4, one, 0)

    arrived(rbuf.at[1 - x], x_recv.at[0])

    def norm_first(s, part, whole):
        r = rbuf[s, part, :]
        centre = r - row_mean(r)
        inv = lax.rsqrt(row_mean(centre * centre) + EPSILON)
        normed = centre * inv
        n_in[s, part, :] = normed
        stat_in[s, part, :] = jnp.broadcast_to(inv, (step, 128))
        hidden[whole, :] = low(normed * vfull[0:1, :] + vfull[1:2, :])

    by_rows(norm_first)
    relay_far(2)
    finish(0)
    for m, bias in ((0, 2), (1, None), (2, 3)):
        made = jnp.dot(hidden[...], wqkv[m].reshape(width, half), preferred_element_type=F32)
        if bias is not None:
            made = made + vfull[bias : bias + 1, pl.ds(mine, half)]
        qkv[m] = low(made)

    first_lane = lax.broadcasted_iota(jnp.int32, (frames, 2 * HEAD_DIM), 1) < HEAD_DIM
    scale = HEAD_DIM**-0.5

    def masked(pair, which):
        keep = first_lane if which == 0 else jnp.logical_not(first_lane)
        return jnp.where(keep, pair, jnp.zeros_like(pair))

    for pair in range(half // (2 * HEAD_DIM)):
        lanes = slice(pair * 2 * HEAD_DIM, (pair + 1) * 2 * HEAD_DIM)
        q2, k2, v2_ = qkv[0, :, lanes], qkv[1, :, lanes], qkv[2, :, lanes]
        parts = []
        for which in range(2):
            scores = dot_nt(masked(q2, which), k2) * scale
            raised = jnp.exp(scores - jnp.max(scores, axis=-1, keepdims=True))
            weights = raised * (1.0 / jnp.sum(raised, axis=-1, keepdims=True))
            prob[2 * pair + which] = weights
            parts.append(jnp.dot(low(weights), v2_, preferred_element_type=F32))
        cbuf[x, :, lanes] = low(jnp.where(first_lane, parts[0], parts[1]))
        if pair == 0:
            relay_y(2)
        if pair == 1:
            relay_near(3)
            own_z(5)
            turned_y()
    send(cbuf.at[x], cbuf.at[x], x_send.at[2], x_recv.at[2], xpeer)
    finish(2)
    relay_far(3)
    arrived(cbuf.at[1 - x], x_recv.at[2])
    context = jnp.concatenate([cbuf[0], cbuf[1]], axis=1)
    for n in range(2):
        cols = slice(n * half, (n + 1) * half)
        made = jnp.dot(context, wo[:, :, cols].reshape(width, half), preferred_element_type=F32)
        made = made + vfull[4:5, cols]
        for s in range(2):
            middle[s, :, cols] = rbuf[s, :, cols] + made[s * own : (s + 1) * own]

    def norm_second(s, part, whole):
        r = middle[s, part, :]
        centre = r - row_mean(r)
        inv = lax.rsqrt(row_mean(centre * centre) + EPSILON)
        normed = centre * inv
        n_mid[s, part, :] = normed
        stat_mid[s, part, :] = jnp.broadcast_to(inv, (step, 128))
        hmid[whole, :] = low(normed * vfull[5:6, :] + vfull[6:7, :])

    by_rows(norm_second)
    relay_near(4)
    relay_y(3)
    arrived(gbuf.at[1 - x], x_recv.at[1])
    for s in range(2):
        upl[s * own : (s + 1) * own, :] = low(gbuf[s])
    v0[7:8, :] = column_sum(gbuf[0]) + column_sum(gbuf[1])
    finish(3)

    chunk = 4 * slab
    chunks = ff // chunk

    def up_chunk(n, carry):
        cols = pl.ds(pl.multiple_of(n * chunk, 128), chunk)
        pre = jnp.dot(hmid[...], wup[:, :, cols].reshape(width, chunk), preferred_element_type=F32)
        pre = pre + bup[:, cols]
        bell = 0.5 * (1.0 + lax.erf(pre * ROOT_HALF))
        act[:, cols] = low(pre * bell)
        slope[:, cols] = bell + pre * jnp.exp(-0.5 * pre * pre) * INV_ROOT_TAU
        return carry

    lax.fori_loop(0, chunks, up_chunk, 0)
    relay_far(4)

    pieces = {
        "d": (0, g_d, s_d, t_d, y_d, zs_d, zr_d, xs_d, xr_d, f_d),
        "e": (7, g_e, s_e, t_e, y_e, zs_e, zr_e, xs_e, xr_e, f_e),
        "u0": (1, g_u0, s_u0, t_u0, y_u0, zs_u0, zr_u0, xs_u0, xr_u0, f_u0),
        "u1": (8, g_u1, s_u1, t_u1, y_u1, zs_u1, zr_u1, xs_u1, xr_u1, f_u1),
        "u2": (9, g_u2, s_u2, t_u2, y_u2, zs_u2, zr_u2, xs_u2, xr_u2, f_u2),
        "u3": (10, g_u3, s_u3, t_u3, y_u3, zs_u3, zr_u3, xs_u3, xr_u3, f_u3),
        "o": (2, g_o, s_o, t_o, y_o, zs_o, zr_o, xs_o, xr_o, f_o),
        "q": (3, g_q, s_q, t_q, y_q, zs_q, zr_q, xs_q, xr_q, f_q),
        "k": (5, g_k, s_k, t_k, y_k, zs_k, zr_k, xs_k, xr_k, f_k),
        "v": (6, g_v, s_v, t_v, y_v, zs_v, zr_v, xs_v, xr_v, f_v),
    }

    def reduce_core(name):
        at_piece, g, s_ = pieces[name][:3]
        send(g.at[:, :, 1 - c], s_, rs_send.at[at_piece, 0], rs_recv.at[at_piece, 0], sib)

    def reduce_y(name):
        at_piece, g, s_, t, yb = pieces[name][:5]
        arrived(s_, rs_recv.at[at_piece, 0])

        def one(n, carry):
            t[n] = low(wide(g[n, 1 - y, c]) + wide(s_[n, 1 - y]))
            return carry

        lax.fori_loop(0, depth, one, 0)
        send(t, yb, rs_send.at[at_piece, 1], rs_recv.at[at_piece, 1], ypeer)

    def reduce_z(name):
        at_piece, g, s_, t, yb, zs, zr, xs, xr, fin = pieces[name]
        arrived(yb, rs_recv.at[at_piece, 1])
        for n, other in enumerate(zother):
            zs[n] = low(wide(g[other, y, c]) + wide(s_[other, y]) + wide(yb[other]))
            send(zs.at[n], zr.at[hops - 1 - n], rs_send.at[at_piece, 2 + n],
                 rs_recv.at[at_piece, 2 + hops - 1 - n], zpeers[n])
        fin[...] = wide(g[z, y, c]) + wide(s_[z, y]) + wide(yb[z])

    def reduce_x(name):
        at_piece, g, s_, t, yb, zs, zr, xs, xr, fin = pieces[name]
        total = fin[...]
        for n in range(hops):
            arrived(zr.at[n], rs_recv.at[at_piece, 2 + n])
            total = total + wide(zr[n])
        fin[...] = total
        xs[...] = low(total)
        send(xs, xr, rs_send.at[at_piece, 2 + hops], rs_recv.at[at_piece, 2 + hops], xpeer)

    def turned_send():
        arrived(s_e, rs_recv.at[7, 0])
        for n, other in enumerate(zother):
            zs_e[n] = low(wide(g_e[other, :, c]) + wide(s_e[other]))
            send(zs_e.at[n], zr_e.at[hops - 1 - n], rs_send.at[7, 2 + n], rs_recv.at[7, 2 + hops - 1 - n], zpeers[n])
        both_e[...] = wide(g_e[z, :, c]) + wide(s_e[z])

    def turned_over():
        for n in range(hops):
            arrived(zr_e.at[n], rs_recv.at[7, 2 + n])
            both_e[...] = both_e[...] + wide(zr_e[n])
        t_e[0] = low(both_e[1 - y])
        send(t_e.at[0], y_e.at[0], rs_send.at[7, 1], rs_recv.at[7, 1], ypeer)

    def turned_x():
        arrived(y_e.at[0], rs_recv.at[7, 1])
        f_e[...] = both_e[y] + wide(y_e[0])
        xs_e[...] = low(f_e[...])
        send(xs_e, xr_e, rs_send.at[7, 2 + hops], rs_recv.at[7, 2 + hops], xpeer)

    def reduced(name):
        at_piece, g, s_, t, yb, zs, zr, xs, xr, fin = pieces[name]
        arrived(xr, rs_recv.at[at_piece, 2 + hops])
        return fin, xr

    def down_chunk(n, carry):
        cols = pl.ds(pl.multiple_of(n * chunk, 128), chunk)
        made = low(dot_tn(act[:, cols], upl[...]))
        made = made.reshape(2, 2, 2, sub, width)
        g_d[n] = made[:, :, 0]
        g_e[n] = made[:, :, 1]
        return carry

    lax.fori_loop(0, chunks, down_chunk, 0)
    reduce_core("e")
    reduce_core("d")
    turned_near()
    relay_y(4)
    turned_far()
    reduce_y("d")
    turned_send()
    finish(4)
    finish(5)


    def back_chunk(n, carry):
        cols = pl.ds(pl.multiple_of(n * chunk, 128), chunk)
        rhs = wdown[pl.ds(n * 4, 4)].reshape(chunk, width)
        pg = dot_nt(upl[...], rhs) * slope[:, cols]
        plow[:, cols] = low(pg)
        bup_sum[:, cols] = column_sum(pg)
        return carry

    bup_sum = bup
    lax.fori_loop(0, chunks, back_chunk, 0)
    for n in range(2):
        cols = slice(n * half, (n + 1) * half)
        made = dot_nt(plow[...], wup[n * fsdp // 2 : (n + 1) * fsdp // 2].reshape(half, ff))
        mh_part[:, cols] = made
        mh_send[n] = low(made)
        send(mh_send.at[n], mh_recv.at[n], x_send.at[3 + 3 * n], x_recv.at[3 + 3 * n], xpeer)

    quarters = ("u0", "u1", "u2", "u3")
    for n, g in enumerate((g_u0, g_u1, g_u2, g_u3)):
        made = low(dot_tn(hmid[...], plow[:, n * ff // 4 : (n + 1) * ff // 4]))
        g[...] = made.reshape(depth, 2, 2, rows, ff // 4)
        reduce_core(quarters[n])

    for n in range(2):
        cols = slice(n * half, (n + 1) * half)
        made = jnp.dot(act[...], wdown[:, :, cols].reshape(ff, half), preferred_element_type=F32)
        for s in range(2):
            op_part[s, :, cols] = made[s * own : (s + 1) * own]
    op_send[...] = low(op_part[1 - x])
    send(op_send, op_recv, x_send.at[4], x_recv.at[4], xpeer)
    for name in quarters:
        reduce_y(name)
    reduce_z("d")

    arrived(mh_recv.at[0], x_recv.at[3])
    arrived(mh_recv.at[1], x_recv.at[6])
    only = jnp.where(x == 0, 1.0, 0.0)

    def norm_second_back(s, part, whole):
        total = mh_part[whole, :] + wide(jnp.concatenate([mh_recv[0, whole, :], mh_recv[1, whole, :]], axis=1))
        normed = n_mid[s, part, :]
        v0[5:6, :] += only * column_sum(total * normed)
        v0[6:7, :] += only * column_sum(total)
        scaled = total * vfull[5:6, :]
        spread = scaled - row_mean(scaled) - normed * row_mean(scaled * normed)
        made = gbuf[s, part, :] + spread * stat_mid[s, part, 0:1]
        mg[s, part, :] = made
        mlow[whole, :] = low(made)
        v0[4:5, :] += only * column_sum(made)

    by_rows(norm_second_back)
    v0[7:8, :] = only * v0[7:8, :]
    cg[...] = low(dot_nt(mlow[...], wo[pl.ds(x * (fsdp // 2), fsdp // 2)].reshape(half, width)))
    reduce_z("u0")
    for n in range(2):
        made = low(dot_tn(cbuf[n], mlow[:, pl.ds(mine, half)]))
        g_o[n * depth // 2 : (n + 1) * depth // 2] = made.reshape(depth // 2, 2, 2, rows, half)
    reduce_core("o")
    reduce_z("u1")

    for pair in range(half // (2 * HEAD_DIM)):
        lanes = slice(pair * 2 * HEAD_DIM, (pair + 1) * 2 * HEAD_DIM)
        q2, k2, v2_, c2 = qkv[0, :, lanes], qkv[1, :, lanes], qkv[2, :, lanes], cg[:, lanes]
        parts = []
        for which in range(2):
            weights = prob[2 * pair + which]
            dv = dot_tn(low(weights), c2)
            dp = dot_nt(masked(c2, which), v2_)
            ds = low(weights * (dp - jnp.sum(weights * dp, axis=-1, keepdims=True)) * scale)
            parts.append((jnp.dot(ds, k2, preferred_element_type=F32), dot_tn(ds, q2), dv))
        for m in range(3):
            dqkv[m, :, lanes] = low(jnp.where(first_lane, parts[0][m], parts[1][m]))
    reduce_y("o")
    reduce_z("u2")
    turned_over()
    for m, g, name in ((0, g_q, "q"), (1, g_k, "k"), (2, g_v, "v")):
        made = low(dot_tn(hidden[...], dqkv[m]))
        g[...] = made.reshape(depth, 2, 2, rows, half)
        reduce_core(name)
        if m > 0:
            reduce_y("qk"[m - 1])
    v0[2:3, pl.ds(mine, half)] = column_sum(wide(dqkv[0]))
    v0[3:4, pl.ds(mine, half)] = column_sum(wide(dqkv[2]))
    reduce_z("u3")
    for n in range(2):
        cols = slice(n * half, (n + 1) * half)
        some = slice(n * fsdp // 2, (n + 1) * fsdp // 2)
        made = dot_nt(dqkv[0], wqkv[0, some].reshape(half, half))
        made = made + dot_nt(dqkv[1], wqkv[1, some].reshape(half, half))
        made = made + dot_nt(dqkv[2], wqkv[2, some].reshape(half, half))
        for s in range(2):
            hg_part[s, :, cols] = made[s * own : (s + 1) * own]
    hg_send[...] = low(hg_part[1 - x])
    send(hg_send, hg_recv, x_send.at[5], x_recv.at[5], xpeer)
    reduce_y("v")
    v0[0:1, :] = column_sum(hg_part[0] * n_in[0]) + column_sum(hg_part[1] * n_in[1])
    v0[1:2, :] = column_sum(hg_part[0]) + column_sum(hg_part[1])
    per = ff // width
    for n in range(per):
        sums = bup_sum[:, n * width : (n + 1) * width]
        v0[8 + n : 9 + n, :] = jnp.where(x == 0, sums, jnp.zeros_like(sums))
        v0[8 + per + n : 9 + per + n, :] = jnp.where(x == 0, jnp.zeros_like(sums), sums)
    send(v0, vs, rs_send.at[4, 0], rs_recv.at[4, 0], sib)
    reduce_z("o")
    reduce_z("q")
    reduce_x("d")
    arrived(vs, rs_recv.at[4, 0])
    v1[...] = v0[...] + vs[...]
    send(v1, vy, rs_send.at[4, 1], rs_recv.at[4, 1], ypeer)

    arrived(op_recv, x_recv.at[4])
    reduce_z("k")
    o_out[...] = middle[x] + (op_part[x] + wide(op_recv[...])) + vfull[7:8, :]
    arrived(hg_recv, x_recv.at[5])
    total = hg_part[x] + wide(hg_recv[...])
    normed = n_in[x]
    scaled = total * vfull[0:1, :]
    spread = scaled - row_mean(scaled) - normed * row_mean(scaled * normed)
    o_in[...] = mg[x] + spread * stat_in[x, :, 0:1]

    reduce_z("v")
    for name in quarters:
        reduce_x(name)
    turned_x()
    arrived(vy, rs_recv.at[4, 1])
    v2[...] = v1[...] + vy[...]
    for n in range(hops):
        send(v2, vz.at[hops - 1 - n], rs_send.at[4, 2 + n], rs_recv.at[4, 2 + hops - 1 - n], zpeers[n])
    reduce_x("o")
    reduce_x("q")
    reduce_x("k")
    reduce_x("v")
    total = v2[...]
    for n in range(hops):
        arrived(vz.at[n], rs_recv.at[4, 2 + n])
        total = total + vz[n]
    v3[...] = total
    send(v3, vx, rs_send.at[4, 2 + hops], rs_recv.at[4, 2 + hops], xpeer)

    fin, got = reduced("d")
    o_wd[pl.ds(pl.multiple_of(x * slab, 16), sub), :] = fin[...]
    o_wd[pl.ds(pl.multiple_of((1 - x) * slab, 16), sub), :] = wide(got[...])
    fin, got = reduced("e")
    o_wd[pl.ds(pl.multiple_of(x * slab + sub, 16), sub), :] = fin[...]
    o_wd[pl.ds(pl.multiple_of((1 - x) * slab + sub, 16), sub), :] = wide(got[...])
    parts = [reduced(name) for name in quarters]
    one = jnp.concatenate([fin[...] for fin, got in parts], axis=1)
    two = jnp.concatenate([wide(got[...]) for fin, got in parts], axis=1)
    left, right = jnp.where(x == 0, one, two), jnp.where(x == 0, two, one)
    woven = []
    for b in range(fsdp):
        woven.append(left[:, b * slab : (b + 1) * slab])
        woven.append(right[:, b * slab : (b + 1) * slab])
    o_wu[...] = jnp.concatenate(woven, axis=1)
    fin, got = reduced("o")
    o_wo[:, pl.ds(mine, half)] = fin[...]
    o_wo[:, pl.ds(theirs, half)] = wide(got[...])
    arrived(vx, rs_recv.at[4, 2 + hops])
    v0_all = v3[...] + vx[...]
    taken = jnp.zeros((8, rows), F32)
    low_part = jnp.zeros((1, slab), F32)
    high_part = jnp.zeros((1, slab), F32)
    in_row = width // slab
    for b in range(fsdp):
        here = jnp.where(i == b, 1.0, 0.0)
        taken = taken + here * v0_all[0:8, b * rows : (b + 1) * rows]
        at_row, lane = 8 + b // in_row, (b % in_row) * slab
        low_part = low_part + here * v0_all[at_row : at_row + 1, lane : lane + slab]
        high_part = high_part + here * v0_all[at_row + per : at_row + per + 1, lane : lane + slab]
    for at_row, ref in enumerate((o_fg, o_fb, o_bq, o_bv, o_bo, o_sg, o_sb, o_bd)):
        ref[...] = taken[at_row : at_row + 1]
    o_bu[...] = jnp.concatenate([low_part, high_part], axis=1)
    for name, ref in (("q", o_wq), ("k", o_wk), ("v", o_wv)):
        fin, got = reduced(name)
        ref[:, pl.ds(mine, half)] = fin[...]
        ref[:, pl.ds(theirs, half)] = wide(got[...])

    for copy in started:
        copy.wait_send()
    for copy in inner_copies:
        pl.when(inner)(copy.wait_send)


def hand_over(*refs):
    count = (len(refs) - 1) // 2
    copies = [pltpu.make_async_copy(refs[n], refs[count + n], refs[-1].at[n]) for n in range(count)]
    for copy in copies:
        copy.start()
    for copy in copies:
        copy.wait()


def fused_on_device(frames_in, cotangent, *stacks):
    fsdp = lax.axis_size("fsdp")
    own, width = frames_in.shape[1:]
    sz = Sizes(own, width, stacks[13].shape[1] * fsdp, fsdp)
    half, ff, depth, rows, slab, frames = sz.half, sz.ff, sz.depth, sz.rows, sz.slab, sz.frames
    args = [frames_in[0], cotangent[0]] + [s if s.ndim == 2 else s[0] for s in stacks]
    in_hbm = {0, 1, 4, 6, 7, 9, 15}
    whole = pl.BlockSpec(memory_space=pltpu.VMEM)
    outs = [jax.ShapeDtypeStruct(a.shape, F32) for a in args]

    def vm(dtype, *dims):
        return pltpu.VMEM(dims, dtype)

    def reduce_scratch(r, w, *both):
        return [
            vm(BF16, depth, 2, 2, r, w), vm(BF16, depth, 2, r, w), vm(BF16, depth, r, w),
            vm(BF16, depth, r, w), vm(BF16, depth - 1, *both, r, w), vm(BF16, depth - 1, *both, r, w),
            vm(BF16, r, w), vm(BF16, r, w), vm(F32, r, w),
        ]

    heads = half // HEAD_DIM
    scratch = [
        vm(BF16, 3, fsdp, rows, half), vm(BF16, fsdp, rows, width), vm(BF16, fsdp, rows, ff),
        vm(BF16, fsdp, slab, width), vm(F32, fsdp, 16, 128), vm(F32, 8, width), vm(F32, 1, ff),
        vm(F32, 2, own, width), vm(F32, 2, own, width), vm(F32, 2, own, width), vm(F32, 2, own, width),
        vm(F32, 2, own, width), vm(BF16, frames, width), vm(BF16, frames, width),
        vm(F32, 2, own, 128), vm(F32, 2, own, 128), vm(BF16, 3, frames, half),
        vm(F32, heads, frames, frames), vm(BF16, 2, frames, half), vm(BF16, frames, ff),
        vm(F32, frames, ff), vm(BF16, frames, ff), vm(F32, 2, own, width), vm(BF16, frames, width),
        vm(BF16, frames, width), vm(BF16, frames, half), vm(BF16, 3, frames, half),
        vm(F32, frames, width), vm(BF16, 2, frames, half), vm(BF16, 2, frames, half),
        vm(F32, 2, own, width), vm(BF16, own, width), vm(BF16, own, width),
        vm(F32, 2, own, width), vm(BF16, own, width), vm(BF16, own, width),
        *reduce_scratch(slab // 2, width), *reduce_scratch(slab // 2, width, 2), vm(F32, 2, slab // 2, width),
        *reduce_scratch(rows, ff // 4), *reduce_scratch(rows, ff // 4),
        *reduce_scratch(rows, ff // 4), *reduce_scratch(rows, ff // 4), *reduce_scratch(rows, half),
        *reduce_scratch(rows, half), *reduce_scratch(rows, half), *reduce_scratch(rows, half),
        vm(F32, 16, width), vm(F32, 16, width), vm(F32, 16, width), vm(F32, 16, width),
        vm(F32, 16, width), vm(F32, 16, width), vm(F32, depth - 1, 16, width), vm(F32, 16, width),
        pltpu.SemaphoreType.DMA((7,)),
        pltpu.SemaphoreType.DMA((6, 4 * depth + 2)), pltpu.SemaphoreType.DMA((6, fsdp)),
        pltpu.SemaphoreType.DMA((11, depth + 2)), pltpu.SemaphoreType.DMA((11, depth + 2)),
        pltpu.SemaphoreType.DMA((7,)), pltpu.SemaphoreType.DMA((7,)),
    ]
    made = pl.pallas_call(
        functools.partial(encoder_kernel, sz),
        out_shape=[vm(F32, *o.shape) for o in outs],
        in_specs=[pl.BlockSpec(memory_space=pl.ANY) if n in in_hbm else whole for n in range(len(args))],
        out_specs=[whole] * len(outs),
        scratch_shapes=scratch,
        compiler_params=pltpu.CompilerParams(
            collective_id=0, has_side_effects=True, vmem_limit_bytes=56 * 2**20
        ),
    )(*args)
    anywhere = [pl.BlockSpec(memory_space=pl.ANY)] * len(outs)
    made = pl.pallas_call(
        hand_over,
        out_shape=outs,
        in_specs=anywhere,
        out_specs=anywhere,
        scratch_shapes=[pltpu.SemaphoreType.DMA((len(outs),))],
    )(*[pltpu.with_memory_space_constraint(m, pltpu.VMEM) for m in made])
    return tuple(o if p.ndim == 2 else o[None] for o, p in zip(made, (frames_in, cotangent, *stacks)))


def fits_kernel(mesh, frames_in, up_weight):
    seq, fsdp = mesh.shape["seq"], mesh.shape["fsdp"]
    width, hidden = up_weight.shape[1:]
    return (
        seq == 2
        and fsdp == 16
        and frames_in.shape[0] == fsdp
        and frames_in.shape[1] % 64 == 0
        and width % (16 * fsdp) == 0
        and width % 256 == 0
        and hidden % (64 * fsdp) == 0
        and hidden * 2 % (128 * fsdp) == 0
        and hidden == 4 * width
    )


def solution(mesh):
    def build(body):
        return jax.shard_map(
            body,
            mesh=mesh,
            in_specs=(
                P("fsdp", "seq", None),
                P("fsdp", "seq", None),
                P(None, "fsdp"),
                P(None, "fsdp"),
                P(None, "fsdp", None),
                P(None, "fsdp"),
                P(None, "fsdp", None),
                P(None, "fsdp", None),
                P(None, "fsdp"),
                P(None, "fsdp", None),
                P(None, "fsdp"),
                P(None, "fsdp"),
                P(None, "fsdp"),
                P(None, "fsdp", None),
                P(None, "fsdp"),
                P(None, "fsdp", None),
                P(None, "fsdp"),
            ),
            out_specs=(
                P("fsdp", "seq", None),
                P("fsdp", "seq", None),
                P(None, "fsdp"),
                P(None, "fsdp"),
                P(None, "fsdp", None),
                P(None, "fsdp"),
                P(None, "fsdp", None),
                P(None, "fsdp", None),
                P(None, "fsdp"),
                P(None, "fsdp", None),
                P(None, "fsdp"),
                P(None, "fsdp"),
                P(None, "fsdp"),
                P(None, "fsdp", None),
                P(None, "fsdp"),
                P(None, "fsdp", None),
                P(None, "fsdp"),
            ),
            check_vma=False,
        )

    def run(*arrays):
        body = fused_on_device if fits_kernel(mesh, arrays[0], arrays[13]) else on_device
        return build(body)(*arrays)

    return run
```

```python
import functools

import jax
import jax.numpy as jnp
from jax import lax
from jax.experimental import pallas as pl
from jax.experimental.pallas import tpu as pltpu
from jax.sharding import PartitionSpec as P

HEAD_DIM = 64


EPSILON = 1e-05
ROOT_HALF = 0.7071067811865476
INV_ROOT_TAU = 0.3989422804014327


def matmul(left, right):
    return jnp.dot(left, right, preferred_element_type=jnp.float32)


def contract_rows(left, right):
    return lax.dot_general(
        left, right, (((0,), (0,)), ((), ())), preferred_element_type=jnp.float32
    )


def contract_cols(left, right):
    return lax.dot_general(
        left, right, (((1,), (1,)), ((), ())), preferred_element_type=jnp.float32
    )


def layer_norm(residual, gain, offset):
    centre = residual - jnp.mean(residual, axis=-1, keepdims=True)
    inv_std = lax.rsqrt(jnp.mean(centre * centre, axis=-1, keepdims=True) + EPSILON)
    normed = centre * inv_std
    return (normed * gain.astype(jnp.float32) + offset.astype(jnp.float32), normed, inv_std)


def norm_grad(upstream, normed, inv_std, gain):
    scaled = upstream * gain.astype(jnp.float32)
    spread = scaled - jnp.mean(scaled, axis=-1, keepdims=True)
    return (spread - normed * jnp.mean(scaled * normed, axis=-1, keepdims=True)) * inv_std


def gelu_exact(pre_act):
    return 0.5 * pre_act * (1.0 + lax.erf(pre_act * ROOT_HALF))


def gelu_slope(pre_act):
    return (
        0.5 * (1.0 + lax.erf(pre_act * ROOT_HALF))
        + pre_act * jnp.exp(-0.5 * pre_act * pre_act) * INV_ROOT_TAU
    )


def split_heads(rows):
    return rows.reshape(rows.shape[0], rows.shape[1] // HEAD_DIM, HEAD_DIM)


def attend(query_rows, key_rows, value_rows):
    score_scale = HEAD_DIM ** (-0.5)
    query_heads = split_heads(query_rows)
    key_heads = split_heads(key_rows)
    value_heads = split_heads(value_rows)
    scores = (
        jnp.einsum("qhd,khd->hqk", query_heads, key_heads, preferred_element_type=jnp.float32)
        * score_scale
    )
    row_top = jnp.max(scores, axis=-1, keepdims=True)
    log_total = row_top + jnp.log(jnp.sum(jnp.exp(scores - row_top), axis=-1, keepdims=True))
    weights = jnp.exp(scores - log_total)
    context = jnp.einsum(
        "hqk,khd->qhd",
        weights.astype(jnp.bfloat16),
        value_heads,
        preferred_element_type=jnp.float32,
    )
    return (context.reshape(query_rows.shape).astype(jnp.bfloat16), weights)


def attend_back(query_rows, key_rows, value_rows, weights, context_gradient):
    score_scale = HEAD_DIM ** (-0.5)
    row_shape = query_rows.shape
    query_heads = split_heads(query_rows)
    key_heads = split_heads(key_rows)
    value_heads = split_heads(value_rows)
    gradient_heads = split_heads(context_gradient)
    value_gradient = jnp.einsum(
        "hqk,qhd->khd",
        weights.astype(jnp.bfloat16),
        gradient_heads,
        preferred_element_type=jnp.float32,
    )
    prob_gradient = jnp.einsum(
        "qhd,khd->hqk", gradient_heads, value_heads, preferred_element_type=jnp.float32
    )
    score_gradient = (
        weights
        * (prob_gradient - jnp.sum(weights * prob_gradient, axis=-1, keepdims=True))
        * score_scale
    ).astype(jnp.bfloat16)
    query_gradient = jnp.einsum(
        "hqk,khd->qhd", score_gradient, key_heads, preferred_element_type=jnp.float32
    )
    key_gradient = jnp.einsum(
        "hqk,qhd->khd", score_gradient, query_heads, preferred_element_type=jnp.float32
    )
    return tuple(
        part.reshape(row_shape).astype(jnp.bfloat16)
        for part in (query_gradient, key_gradient, value_gradient)
    )


VECTORS = (0, 1, 3, 6, 8, 9, 10, 12, 14)
MATRICES = (2, 4, 5, 7, 11, 13)
PAD_ROWS = 16


def cut_columns(rows, width):
    blocks = rows.shape[-1] // width
    if blocks == 1:
        return rows
    return jnp.concatenate(
        [rows[..., i * width : (i + 1) * width] for i in range(blocks)], axis=-2
    )


def join_columns(rows, blocks):
    if blocks == 1:
        return rows
    size = rows.shape[-2] // blocks
    return jnp.concatenate(
        [rows[..., i * size : (i + 1) * size, :] for i in range(blocks)], axis=-1
    )


def gather_layer(shards, width):
    pieces = [cut_columns(shards[i], width) for i in MATRICES]
    vector = jnp.concatenate([shards[i] for i in VECTORS])
    vector = jnp.pad(vector, (0, PAD_ROWS * width - vector.shape[0]))
    pieces.append(vector.reshape(PAD_ROWS, width))
    packed = lax.all_gather(jnp.concatenate(pieces, axis=0), "fsdp", axis=0, tiled=False)
    params = [None] * len(shards)
    start = 0
    for i in MATRICES:
        blocks = shards[i].shape[1] // width
        size = shards[i].shape[0] * blocks
        part = join_columns(packed[:, start : start + size], blocks)
        params[i] = part.reshape(-1, shards[i].shape[1])
        start += size
    vectors = packed[:, start:].reshape(packed.shape[0], -1)
    start = 0
    for i in VECTORS:
        size = shards[i].shape[0]
        params[i] = vectors[:, start : start + size].reshape(-1)
        start += size
    return params


def reduce_gradients(gradients, shards, width, seq_size, seq_index, fsdp_size):
    part_width = width // seq_size
    pieces = []
    for i in MATRICES:
        blocks = shards[i].shape[1] // width
        rows = gradients[i].astype(jnp.bfloat16)
        rows = rows.reshape(fsdp_size, shards[i].shape[0], rows.shape[1])
        pieces.append(cut_columns(rows, part_width))
    vector = jnp.concatenate(
        [gradients[i].reshape(fsdp_size, -1) for i in VECTORS], axis=1
    ).astype(jnp.bfloat16)
    vector = jnp.pad(vector, ((0, 0), (0, PAD_ROWS * width - vector.shape[1])))
    vector = vector.reshape(fsdp_size, PAD_ROWS * seq_size, part_width)
    pieces.append(lax.dynamic_slice_in_dim(vector, seq_index * PAD_ROWS, PAD_ROWS, axis=1))
    packed = jnp.concatenate(pieces, axis=1)
    mine = lax.psum_scatter(packed, "fsdp", scatter_dimension=0, tiled=False)
    both = lax.all_gather(mine, "seq", axis=0, tiled=False)
    reduced = [None] * len(shards)
    start = 0
    for i in MATRICES:
        blocks = shards[i].shape[1] // width
        size = shards[i].shape[0] * blocks
        part = join_columns(both[:, start : start + size], blocks)
        whole = jnp.concatenate([part[s] for s in range(seq_size)], axis=-1)
        reduced[i] = whole.astype(jnp.float32)[None]
        start += size
    vector = both[:, start:].reshape(-1).astype(jnp.float32)
    start = 0
    for i in VECTORS:
        size = shards[i].shape[0]
        reduced[i] = vector[start : start + size][None]
        start += size
    return reduced


def on_device(frames_in, cotangent, *stacks):
    width = frames_in.shape[2]
    seq_size = lax.axis_size("seq")
    seq_index = lax.axis_index("seq")
    fsdp_size = lax.axis_size("fsdp")
    shards = [stack[0] for stack in stacks]
    own = frames_in.shape[1]

    mine = jnp.stack([frames_in[0], cotangent[0]])
    if seq_size == 2:
        other = lax.ppermute(mine, "seq", [(0, 1), (1, 0)])
        first = seq_index == 0
        rows = jnp.concatenate(
            [jnp.where(first, mine, other), jnp.where(first, other, mine)], axis=1
        )
    else:
        rows = lax.all_gather(mine, "seq", axis=1, tiled=True)
    residual, upstream = rows[0], rows[1]
    params = gather_layer(shards, width)

    def own_columns(matrix):
        size = matrix.shape[1] // seq_size
        return lax.dynamic_slice_in_dim(matrix, seq_index * size, size, axis=1)

    def own_rows(matrix):
        return lax.dynamic_slice_in_dim(matrix, seq_index * own, own, axis=0)[None]

    wide = [None if i in MATRICES else p.astype(jnp.float32) for i, p in enumerate(params)]

    hidden_wide, normed_in, inv_in = layer_norm(residual, params[0], params[1])
    hidden = hidden_wide.astype(jnp.bfloat16)
    query_rows = (matmul(hidden, params[2]) + wide[3]).astype(jnp.bfloat16)
    key_rows = matmul(hidden, params[4]).astype(jnp.bfloat16)
    value_rows = (matmul(hidden, params[5]) + wide[6]).astype(jnp.bfloat16)
    context, weights = attend(query_rows, key_rows, value_rows)
    middle = residual + matmul(context, params[7]) + wide[8]
    mid_wide, normed_mid, inv_mid = layer_norm(middle, params[9], params[10])
    hidden_mid = mid_wide.astype(jnp.bfloat16)
    pre_act = matmul(hidden_mid, params[11]) + wide[12]
    activated = gelu_exact(pre_act).astype(jnp.bfloat16)
    own_activated = own_rows(activated)[0]
    outputs = own_rows(middle)[0] + matmul(own_activated, params[13]) + wide[14]

    gradients = [None] * len(stacks)
    upstream_low = upstream.astype(jnp.bfloat16)
    gradients[13] = contract_rows(activated, own_columns(upstream_low))
    gradients[14] = jnp.sum(upstream, axis=0)
    pre_gradient = contract_cols(upstream_low, params[13]) * gelu_slope(pre_act)
    pre_low = pre_gradient.astype(jnp.bfloat16)
    gradients[11] = contract_rows(hidden_mid, own_columns(pre_low))
    gradients[12] = jnp.sum(pre_gradient, axis=0)
    mid_hidden_gradient = contract_cols(pre_low, params[11])
    gradients[9] = jnp.sum(mid_hidden_gradient * normed_mid, axis=0)
    gradients[10] = jnp.sum(mid_hidden_gradient, axis=0)
    middle_gradient = upstream + norm_grad(mid_hidden_gradient, normed_mid, inv_mid, params[9])
    middle_low = middle_gradient.astype(jnp.bfloat16)
    gradients[7] = contract_rows(context, own_columns(middle_low))
    gradients[8] = jnp.sum(middle_gradient, axis=0)
    context_gradient = contract_cols(middle_low, params[7]).astype(jnp.bfloat16)
    query_gradient, key_gradient, value_gradient = attend_back(
        query_rows, key_rows, value_rows, weights, context_gradient
    )
    gradients[2] = contract_rows(hidden, own_columns(query_gradient))
    gradients[3] = jnp.sum(query_gradient.astype(jnp.float32), axis=0)
    gradients[4] = contract_rows(hidden, own_columns(key_gradient))
    gradients[5] = contract_rows(hidden, own_columns(value_gradient))
    gradients[6] = jnp.sum(value_gradient.astype(jnp.float32), axis=0)
    hidden_gradient = (
        contract_cols(query_gradient, params[2])
        + contract_cols(key_gradient, params[4])
        + contract_cols(value_gradient, params[5])
    )
    gradients[0] = jnp.sum(hidden_gradient * normed_in, axis=0)
    gradients[1] = jnp.sum(hidden_gradient, axis=0)
    input_gradient = middle_gradient + norm_grad(hidden_gradient, normed_in, inv_in, params[0])
    reduced = reduce_gradients(gradients, shards, width, seq_size, seq_index, fsdp_size)
    return (outputs[None], own_rows(input_gradient), *reduced)


MESH = pl.DeviceIdType.MESH
F32 = jnp.float32
BF16 = jnp.bfloat16


def dot_nt(left, right):
    return lax.dot_general(left, right, (((1,), (1,)), ((), ())), preferred_element_type=F32)


def dot_tn(left, right):
    return lax.dot_general(left, right, (((0,), (0,)), ((), ())), preferred_element_type=F32)


def low(values):
    return values.astype(BF16)


def wide(values):
    return values.astype(F32)


def row_mean(values):
    return jnp.mean(values, axis=-1, keepdims=True)


def column_sum(values):
    return jnp.sum(values, axis=0, keepdims=True)


class Sizes:
    def __init__(self, own, width, hidden, fsdp):
        self.own, self.width, self.hidden, self.fsdp = own, width, hidden, fsdp
        self.frames = 2 * own
        self.half = width // 2
        self.ff = hidden // 2
        self.depth = fsdp // 4
        self.rows = width // fsdp
        self.slab = hidden // fsdp // 2


def encoder_kernel(sz, *refs):
    half, ff, depth, rows, slab = sz.half, sz.ff, sz.depth, sz.rows, sz.slab
    own, frames, width, fsdp = sz.own, sz.frames, sz.width, sz.fsdp
    hops = depth - 1
    sub = slab // 2
    (frames_ref, cot_ref, v_fg, v_fb, wq_ref, v_bq, wk_ref, wv_ref, v_bv, wo_ref, v_bo, v_sg, v_sb,
     wu_ref, v_bu, wd_ref, v_bd) = refs[:17]
    (o_out, o_in, o_fg, o_fb, o_wq, o_bq, o_wk, o_wv, o_bv, o_wo, o_bo, o_sg, o_sb, o_wu, o_bu,
     o_wd, o_bd) = refs[17:34]
    (wqkv, wo, wup, wdown, vecg, vfull, bup, rbuf, gbuf, n_in, n_mid, middle, hidden, hmid, stat_in,
     stat_mid, qkv, prob, cbuf, act, slope, plow, mg, upl, mlow, cg, dqkv, mh_part, mh_send, mh_recv, op_part,
     op_send, op_recv, hg_part, hg_send, hg_recv,
     g_d, s_d, t_d, y_d, zs_d, zr_d, xs_d, xr_d, f_d,
     g_e, s_e, t_e, y_e, zs_e, zr_e, xs_e, xr_e, f_e, both_e,
     g_u0, s_u0, t_u0, y_u0, zs_u0, zr_u0, xs_u0, xr_u0, f_u0,
     g_u1, s_u1, t_u1, y_u1, zs_u1, zr_u1, xs_u1, xr_u1, f_u1,
     g_u2, s_u2, t_u2, y_u2, zs_u2, zr_u2, xs_u2, xr_u2, f_u2,
     g_u3, s_u3, t_u3, y_u3, zs_u3, zr_u3, xs_u3, xr_u3, f_u3,
     g_o, s_o, t_o, y_o, zs_o, zr_o, xs_o, xr_o, f_o,
     g_q, s_q, t_q, y_q, zs_q, zr_q, xs_q, xr_q, f_q,
     g_k, s_k, t_k, y_k, zs_k, zr_k, xs_k, xr_k, f_k,
     g_v, s_v, t_v, y_v, zs_v, zr_v, xs_v, xr_v, f_v,
     v0, v1, v2, v3, vs, vy, vz, vx,
     local_sem, ag_send, ag_recv, rs_send, rs_recv, x_send, x_recv) = refs[34:]

    x = lax.axis_index("seq")
    i = lax.axis_index("fsdp")
    z, y, c = i // 4, lax.rem(i // 2, 2), lax.rem(i, 2)

    def at(z_at, y_at, c_at):
        return (x, z_at * 4 + y_at * 2 + c_at)

    sib, ypeer, xpeer = at(z, y, 1 - c), at(z, 1 - y, c), (1 - x, i)
    zother = [lax.rem(z + d, depth) for d in range(1, depth)]
    zpeers = [at(other, y, c) for other in zother]
    inner = jnp.logical_or(z == 1, z == 2)
    beside = z + 1 - 2 * lax.rem(z, 2)
    second = jnp.where(z < 2, 2, 1)
    far_end = 6 - z - beside - second
    near = [beside, second]
    mine = pl.multiple_of(x * half, 128)
    theirs = pl.multiple_of((1 - x) * half, 128)

    local = [
        pltpu.make_async_copy(wq_ref.at[:, pl.ds(mine, half)], wqkv.at[0, i], local_sem.at[0]),
        pltpu.make_async_copy(wk_ref.at[:, pl.ds(mine, half)], wqkv.at[1, i], local_sem.at[1]),
        pltpu.make_async_copy(wv_ref.at[:, pl.ds(mine, half)], wqkv.at[2, i], local_sem.at[2]),
        pltpu.make_async_copy(wo_ref, wo.at[i], local_sem.at[3]),
        pltpu.make_async_copy(wd_ref.at[pl.ds(pl.multiple_of(x * slab, 16), slab)], wdown.at[i], local_sem.at[4]),
        pltpu.make_async_copy(frames_ref, rbuf.at[x], local_sem.at[5]),
        pltpu.make_async_copy(cot_ref, gbuf.at[x], local_sem.at[6]),
    ]
    for copy in local:
        copy.start()

    barrier = pltpu.get_barrier_semaphore()
    partners = [sib, ypeer, xpeer, *zpeers]
    for partner in partners:
        pl.semaphore_signal(barrier, inc=1, device_id=partner, device_id_type=MESH)

    vecg[i] = jnp.zeros(vecg.shape[1:], F32)
    for at_row, ref in enumerate((v_fg, v_fb, v_bq, v_bv, v_bo, v_sg, v_sb, v_bd)):
        vecg[i, at_row : at_row + 1, 0:rows] = wide(ref[...])
    up_bias = wide(v_bu[...])
    vecg[i, 8:9, 0:slab] = up_bias[:, :slab]
    vecg[i, 9:10, 0:slab] = up_bias[:, slab:]

    pl.semaphore_wait(barrier, len(partners))

    started = []

    def send(src, dst, send_sem, recv_sem, to):
        copy = pltpu.make_async_remote_copy(
            src_ref=src, dst_ref=dst, send_sem=send_sem, recv_sem=recv_sem, device_id=to, device_id_type=MESH
        )
        copy.start()
        started.append(copy)

    def arrived(dst, recv_sem):
        pltpu.make_async_remote_copy(
            src_ref=dst, dst_ref=dst, send_sem=recv_sem, recv_sem=recv_sem, device_id=xpeer, device_id_type=MESH
        ).wait_recv()

    def block(piece, b):
        upper, lower = wdown.at[b, 0:sub], wdown.at[b, sub:slab]
        return (wqkv.at[:, b], vecg.at[b], wo.at[b], wup.at[b], upper, lower)[piece]

    def pass_on(piece, b, slot, to):
        send(block(piece, b), block(piece, b), ag_send.at[piece, slot], ag_recv.at[piece, b], to)

    inner_copies = []

    def pass_inner(piece, b, slot, to):
        copy = pltpu.make_async_remote_copy(
            src_ref=block(piece, b), dst_ref=block(piece, b), send_sem=ag_send.at[piece, slot],
            recv_sem=ag_recv.at[piece, b], device_id=to, device_id_type=MESH
        )
        inner_copies.append(copy)

        @pl.when(inner)
        def _():
            copy.start()

    def own_z(piece):
        pass_on(piece, i, 0, at(second, y, c))
        pass_on(piece, i, 1, at(beside, y, c))
        pass_inner(piece, i, 2, at(far_end, y, c))

    def own_near(piece):
        pass_on(piece, i, hops, ypeer)
        pass_on(piece, i, hops + 1, sib)

    def relay_near(piece):
        for n, other in enumerate(near):
            b = other * 4 + y * 2 + c
            arrived(block(piece, b), ag_recv.at[piece, b])
            pass_on(piece, b, hops + 2 + n, ypeer)
            pass_on(piece, b, 2 * hops + 2 + n, sib)

    def relay_far(piece):
        b = far_end * 4 + y * 2 + c
        arrived(block(piece, b), ag_recv.at[piece, b])
        pass_inner(piece, b, 4 * hops + 3, at(beside, y, c))
        pass_on(piece, b, hops + 4, ypeer)
        pass_on(piece, b, 2 * hops + 4, sib)

    def turned_y():
        b = z * 4 + (1 - y) * 2 + c
        arrived(block(5, b), ag_recv.at[5, b])
        pass_on(5, b, 5, at(second, y, c))
        pass_on(5, b, 6, at(beside, y, c))
        pass_inner(5, b, 7, at(far_end, y, c))
        pass_on(5, b, 8, sib)

    def turned_near():
        for n, other in enumerate(near):
            for m in range(2):
                b = other * 4 + m * 2 + c
                arrived(block(5, b), ag_recv.at[5, b])
                pass_on(5, b, 9 + 2 * n + m, sib)

    def turned_far():
        for m in range(2):
            b = far_end * 4 + m * 2 + c
            arrived(block(5, b), ag_recv.at[5, b])
            pass_inner(5, b, 13 + m, at(beside, y, c))
            pass_on(5, b, 15 + m, sib)

    def relay_y(piece):
        for n, other in enumerate((z, beside, second, far_end)):
            b = other * 4 + (1 - y) * 2 + c
            arrived(block(piece, b), ag_recv.at[piece, b])
            pass_on(piece, b, 3 * hops + 2 + n, sib)

    def finish(piece):
        for k in range(2 * depth):
            b = 2 * k + (1 - c)
            arrived(block(piece, b), ag_recv.at[piece, b])

    for n in range(3):
        local[n].wait()
    own_z(0)
    own_near(0)
    own_z(1)
    own_near(1)
    local[5].wait()
    send(rbuf.at[x], rbuf.at[x], x_send.at[0], x_recv.at[0], xpeer)
    local[3].wait()
    own_z(2)
    own_near(2)
    local[6].wait()
    send(gbuf.at[x], gbuf.at[x], x_send.at[1], x_recv.at[1], xpeer)
    up = wide(wu_ref[...])
    picked = []
    for b in range(fsdp):
        left = up[:, 2 * slab * b : 2 * slab * b + slab]
        right = up[:, 2 * slab * b + slab : 2 * slab * (b + 1)]
        picked.append(jnp.where(x == 0, left, right))
    wup[i] = low(jnp.concatenate(picked, axis=1))
    own_near(3)
    local[4].wait()
    own_near(4)
    own_near(5)

    relay_near(0)
    relay_near(1)
    own_z(3)
    relay_far(0)
    relay_far(1)
    relay_near(2)
    own_z(4)
    relay_y(0)
    relay_y(1)
    finish(1)
    for b in range(fsdp):
        vfull[:, rows * b : rows * (b + 1)] = vecg[b, 0:8, 0:rows]
        bup[:, slab * b : slab * (b + 1)] = jnp.where(x == 0, vecg[b, 8:9, 0:slab], vecg[b, 9:10, 0:slab])
    v0[...] = jnp.zeros_like(v0)

    step = own // 2

    def by_rows(body):
        def one(n, carry):
            s = n // 2
            r0 = pl.multiple_of(lax.rem(n, 2) * step, step)
            body(s, pl.ds(r0, step), pl.ds(pl.multiple_of(n * step, step), step))
            return carry

        lax.fori_loop(0, 4, one, 0)

    arrived(rbuf.at[1 - x], x_recv.at[0])

    def norm_first(s, part, whole):
        r = rbuf[s, part, :]
        centre = r - row_mean(r)
        inv = lax.rsqrt(row_mean(centre * centre) + EPSILON)
        normed = centre * inv
        n_in[s, part, :] = normed
        stat_in[s, part, :] = jnp.broadcast_to(inv, (step, 128))
        hidden[whole, :] = low(normed * vfull[0:1, :] + vfull[1:2, :])

    by_rows(norm_first)
    relay_far(2)
    finish(0)
    for m, bias in ((0, 2), (1, None), (2, 3)):
        made = jnp.dot(hidden[...], wqkv[m].reshape(width, half), preferred_element_type=F32)
        if bias is not None:
            made = made + vfull[bias : bias + 1, pl.ds(mine, half)]
        qkv[m] = low(made)

    first_lane = lax.broadcasted_iota(jnp.int32, (frames, 2 * HEAD_DIM), 1) < HEAD_DIM
    scale = HEAD_DIM**-0.5

    def masked(pair, which):
        keep = first_lane if which == 0 else jnp.logical_not(first_lane)
        return jnp.where(keep, pair, jnp.zeros_like(pair))

    for pair in range(half // (2 * HEAD_DIM)):
        lanes = slice(pair * 2 * HEAD_DIM, (pair + 1) * 2 * HEAD_DIM)
        q2, k2, v2_ = qkv[0, :, lanes], qkv[1, :, lanes], qkv[2, :, lanes]
        parts = []
        for which in range(2):
            scores = dot_nt(masked(q2, which), k2) * scale
            raised = jnp.exp(scores - jnp.max(scores, axis=-1, keepdims=True))
            weights = raised * (1.0 / jnp.sum(raised, axis=-1, keepdims=True))
            prob[2 * pair + which] = weights
            parts.append(jnp.dot(low(weights), v2_, preferred_element_type=F32))
        cbuf[x, :, lanes] = low(jnp.where(first_lane, parts[0], parts[1]))
        if pair == 0:
            relay_y(2)
        if pair == 1:
            relay_near(3)
            own_z(5)
            turned_y()
    send(cbuf.at[x], cbuf.at[x], x_send.at[2], x_recv.at[2], xpeer)
    finish(2)
    relay_far(3)
    arrived(cbuf.at[1 - x], x_recv.at[2])
    context = jnp.concatenate([cbuf[0], cbuf[1]], axis=1)
    for n in range(2):
        cols = slice(n * half, (n + 1) * half)
        made = jnp.dot(context, wo[:, :, cols].reshape(width, half), preferred_element_type=F32)
        made = made + vfull[4:5, cols]
        for s in range(2):
            middle[s, :, cols] = rbuf[s, :, cols] + made[s * own : (s + 1) * own]

    def norm_second(s, part, whole):
        r = middle[s, part, :]
        centre = r - row_mean(r)
        inv = lax.rsqrt(row_mean(centre * centre) + EPSILON)
        normed = centre * inv
        n_mid[s, part, :] = normed
        stat_mid[s, part, :] = jnp.broadcast_to(inv, (step, 128))
        hmid[whole, :] = low(normed * vfull[5:6, :] + vfull[6:7, :])

    by_rows(norm_second)
    relay_near(4)
    relay_y(3)
    arrived(gbuf.at[1 - x], x_recv.at[1])
    for s in range(2):
        upl[s * own : (s + 1) * own, :] = low(gbuf[s])
    v0[7:8, :] = column_sum(gbuf[0]) + column_sum(gbuf[1])
    finish(3)

    chunk = 4 * slab
    chunks = ff // chunk

    def up_chunk(n, carry):
        cols = pl.ds(pl.multiple_of(n * chunk, 128), chunk)
        pre = jnp.dot(hmid[...], wup[:, :, cols].reshape(width, chunk), preferred_element_type=F32)
        pre = pre + bup[:, cols]
        bell = 0.5 * (1.0 + lax.erf(pre * ROOT_HALF))
        act[:, cols] = low(pre * bell)
        slope[:, cols] = bell + pre * jnp.exp(-0.5 * pre * pre) * INV_ROOT_TAU
        return carry

    lax.fori_loop(0, chunks, up_chunk, 0)
    relay_far(4)

    pieces = {
        "d": (0, g_d, s_d, t_d, y_d, zs_d, zr_d, xs_d, xr_d, f_d),
        "e": (7, g_e, s_e, t_e, y_e, zs_e, zr_e, xs_e, xr_e, f_e),
        "u0": (1, g_u0, s_u0, t_u0, y_u0, zs_u0, zr_u0, xs_u0, xr_u0, f_u0),
        "u1": (8, g_u1, s_u1, t_u1, y_u1, zs_u1, zr_u1, xs_u1, xr_u1, f_u1),
        "u2": (9, g_u2, s_u2, t_u2, y_u2, zs_u2, zr_u2, xs_u2, xr_u2, f_u2),
        "u3": (10, g_u3, s_u3, t_u3, y_u3, zs_u3, zr_u3, xs_u3, xr_u3, f_u3),
        "o": (2, g_o, s_o, t_o, y_o, zs_o, zr_o, xs_o, xr_o, f_o),
        "q": (3, g_q, s_q, t_q, y_q, zs_q, zr_q, xs_q, xr_q, f_q),
        "k": (5, g_k, s_k, t_k, y_k, zs_k, zr_k, xs_k, xr_k, f_k),
        "v": (6, g_v, s_v, t_v, y_v, zs_v, zr_v, xs_v, xr_v, f_v),
    }

    def reduce_core(name):
        at_piece, g, s_ = pieces[name][:3]
        send(g.at[:, :, 1 - c], s_, rs_send.at[at_piece, 0], rs_recv.at[at_piece, 0], sib)

    def reduce_y(name):
        at_piece, g, s_, t, yb = pieces[name][:5]
        arrived(s_, rs_recv.at[at_piece, 0])

        def one(n, carry):
            t[n] = low(wide(g[n, 1 - y, c]) + wide(s_[n, 1 - y]))
            return carry

        lax.fori_loop(0, depth, one, 0)
        send(t, yb, rs_send.at[at_piece, 1], rs_recv.at[at_piece, 1], ypeer)

    def reduce_z(name):
        at_piece, g, s_, t, yb, zs, zr, xs, xr, fin = pieces[name]
        arrived(yb, rs_recv.at[at_piece, 1])
        for n, other in enumerate(zother):
            zs[n] = low(wide(g[other, y, c]) + wide(s_[other, y]) + wide(yb[other]))
            send(zs.at[n], zr.at[hops - 1 - n], rs_send.at[at_piece, 2 + n],
                 rs_recv.at[at_piece, 2 + hops - 1 - n], zpeers[n])
        fin[...] = wide(g[z, y, c]) + wide(s_[z, y]) + wide(yb[z])

    def reduce_x(name):
        at_piece, g, s_, t, yb, zs, zr, xs, xr, fin = pieces[name]
        total = fin[...]
        for n in range(hops):
            arrived(zr.at[n], rs_recv.at[at_piece, 2 + n])
            total = total + wide(zr[n])
        fin[...] = total
        xs[...] = low(total)
        send(xs, xr, rs_send.at[at_piece, 2 + hops], rs_recv.at[at_piece, 2 + hops], xpeer)

    def turned_send():
        arrived(s_e, rs_recv.at[7, 0])
        for n, other in enumerate(zother):
            zs_e[n] = low(wide(g_e[other, :, c]) + wide(s_e[other]))
            send(zs_e.at[n], zr_e.at[hops - 1 - n], rs_send.at[7, 2 + n], rs_recv.at[7, 2 + hops - 1 - n], zpeers[n])
        both_e[...] = wide(g_e[z, :, c]) + wide(s_e[z])

    def turned_over():
        for n in range(hops):
            arrived(zr_e.at[n], rs_recv.at[7, 2 + n])
            both_e[...] = both_e[...] + wide(zr_e[n])
        t_e[0] = low(both_e[1 - y])
        send(t_e.at[0], y_e.at[0], rs_send.at[7, 1], rs_recv.at[7, 1], ypeer)

    def turned_x():
        arrived(y_e.at[0], rs_recv.at[7, 1])
        f_e[...] = both_e[y] + wide(y_e[0])
        xs_e[...] = low(f_e[...])
        send(xs_e, xr_e, rs_send.at[7, 2 + hops], rs_recv.at[7, 2 + hops], xpeer)

    def reduced(name):
        at_piece, g, s_, t, yb, zs, zr, xs, xr, fin = pieces[name]
        arrived(xr, rs_recv.at[at_piece, 2 + hops])
        return fin, xr

    def down_chunk(n, carry):
        cols = pl.ds(pl.multiple_of(n * chunk, 128), chunk)
        made = low(dot_tn(act[:, cols], upl[...]))
        made = made.reshape(2, 2, 2, sub, width)
        g_d[n] = made[:, :, 0]
        g_e[n] = made[:, :, 1]
        return carry

    lax.fori_loop(0, chunks, down_chunk, 0)
    reduce_core("e")
    reduce_core("d")
    turned_near()
    relay_y(4)
    turned_far()
    reduce_y("d")
    turned_send()
    finish(4)
    finish(5)


    def back_chunk(n, carry):
        cols = pl.ds(pl.multiple_of(n * chunk, 128), chunk)
        rhs = wdown[pl.ds(n * 4, 4)].reshape(chunk, width)
        pg = dot_nt(upl[...], rhs) * slope[:, cols]
        plow[:, cols] = low(pg)
        bup_sum[:, cols] = column_sum(pg)
        return carry

    bup_sum = bup
    lax.fori_loop(0, chunks, back_chunk, 0)
    for n in range(2):
        cols = slice(n * half, (n + 1) * half)
        made = dot_nt(plow[...], wup[n * fsdp // 2 : (n + 1) * fsdp // 2].reshape(half, ff))
        mh_part[:, cols] = made
        mh_send[n] = low(made)
        send(mh_send.at[n], mh_recv.at[n], x_send.at[3 + 3 * n], x_recv.at[3 + 3 * n], xpeer)

    quarters = ("u0", "u1", "u2", "u3")
    for n, g in enumerate((g_u0, g_u1, g_u2, g_u3)):
        made = low(dot_tn(hmid[...], plow[:, n * ff // 4 : (n + 1) * ff // 4]))
        g[...] = made.reshape(depth, 2, 2, rows, ff // 4)
        reduce_core(quarters[n])

    for n in range(2):
        cols = slice(n * half, (n + 1) * half)
        made = jnp.dot(act[...], wdown[:, :, cols].reshape(ff, half), preferred_element_type=F32)
        for s in range(2):
            op_part[s, :, cols] = made[s * own : (s + 1) * own]
    op_send[...] = low(op_part[1 - x])
    send(op_send, op_recv, x_send.at[4], x_recv.at[4], xpeer)
    for name in quarters:
        reduce_y(name)
    reduce_z("d")

    arrived(mh_recv.at[0], x_recv.at[3])
    arrived(mh_recv.at[1], x_recv.at[6])
    only = jnp.where(x == 0, 1.0, 0.0)

    def norm_second_back(s, part, whole):
        total = mh_part[whole, :] + wide(jnp.concatenate([mh_recv[0, whole, :], mh_recv[1, whole, :]], axis=1))
        normed = n_mid[s, part, :]
        v0[5:6, :] += only * column_sum(total * normed)
        v0[6:7, :] += only * column_sum(total)
        scaled = total * vfull[5:6, :]
        spread = scaled - row_mean(scaled) - normed * row_mean(scaled * normed)
        made = gbuf[s, part, :] + spread * stat_mid[s, part, 0:1]
        mg[s, part, :] = made
        mlow[whole, :] = low(made)
        v0[4:5, :] += only * column_sum(made)

    by_rows(norm_second_back)
    v0[7:8, :] = only * v0[7:8, :]
    cg[...] = low(dot_nt(mlow[...], wo[pl.ds(x * (fsdp // 2), fsdp // 2)].reshape(half, width)))
    reduce_z("u0")
    for n in range(2):
        made = low(dot_tn(cbuf[n], mlow[:, pl.ds(mine, half)]))
        g_o[n * depth // 2 : (n + 1) * depth // 2] = made.reshape(depth // 2, 2, 2, rows, half)
    reduce_core("o")
    reduce_z("u1")

    for pair in range(half // (2 * HEAD_DIM)):
        lanes = slice(pair * 2 * HEAD_DIM, (pair + 1) * 2 * HEAD_DIM)
        q2, k2, v2_, c2 = qkv[0, :, lanes], qkv[1, :, lanes], qkv[2, :, lanes], cg[:, lanes]
        parts = []
        for which in range(2):
            weights = prob[2 * pair + which]
            dv = dot_tn(low(weights), c2)
            dp = dot_nt(masked(c2, which), v2_)
            ds = low(weights * (dp - jnp.sum(weights * dp, axis=-1, keepdims=True)) * scale)
            parts.append((jnp.dot(ds, k2, preferred_element_type=F32), dot_tn(ds, q2), dv))
        for m in range(3):
            dqkv[m, :, lanes] = low(jnp.where(first_lane, parts[0][m], parts[1][m]))
    reduce_y("o")
    reduce_z("u2")
    for m, g, name in ((0, g_q, "q"), (1, g_k, "k"), (2, g_v, "v")):
        made = low(dot_tn(hidden[...], dqkv[m]))
        g[...] = made.reshape(depth, 2, 2, rows, half)
        reduce_core(name)
        if m > 0:
            reduce_y("qk"[m - 1])
    v0[2:3, pl.ds(mine, half)] = column_sum(wide(dqkv[0]))
    v0[3:4, pl.ds(mine, half)] = column_sum(wide(dqkv[2]))
    reduce_z("u3")
    for n in range(2):
        cols = slice(n * half, (n + 1) * half)
        some = slice(n * fsdp // 2, (n + 1) * fsdp // 2)
        made = dot_nt(dqkv[0], wqkv[0, some].reshape(half, half))
        made = made + dot_nt(dqkv[1], wqkv[1, some].reshape(half, half))
        made = made + dot_nt(dqkv[2], wqkv[2, some].reshape(half, half))
        for s in range(2):
            hg_part[s, :, cols] = made[s * own : (s + 1) * own]
    hg_send[...] = low(hg_part[1 - x])
    send(hg_send, hg_recv, x_send.at[5], x_recv.at[5], xpeer)
    reduce_y("v")
    v0[0:1, :] = column_sum(hg_part[0] * n_in[0]) + column_sum(hg_part[1] * n_in[1])
    v0[1:2, :] = column_sum(hg_part[0]) + column_sum(hg_part[1])
    per = ff // width
    for n in range(per):
        sums = bup_sum[:, n * width : (n + 1) * width]
        v0[8 + n : 9 + n, :] = jnp.where(x == 0, sums, jnp.zeros_like(sums))
        v0[8 + per + n : 9 + per + n, :] = jnp.where(x == 0, jnp.zeros_like(sums), sums)
    send(v0, vs, rs_send.at[4, 0], rs_recv.at[4, 0], sib)
    reduce_z("o")
    turned_over()
    reduce_z("q")
    reduce_x("d")
    arrived(vs, rs_recv.at[4, 0])
    v1[...] = v0[...] + vs[...]
    send(v1, vy, rs_send.at[4, 1], rs_recv.at[4, 1], ypeer)

    arrived(op_recv, x_recv.at[4])
    reduce_z("k")
    o_out[...] = middle[x] + (op_part[x] + wide(op_recv[...])) + vfull[7:8, :]
    arrived(hg_recv, x_recv.at[5])
    total = hg_part[x] + wide(hg_recv[...])
    normed = n_in[x]
    scaled = total * vfull[0:1, :]
    spread = scaled - row_mean(scaled) - normed * row_mean(scaled * normed)
    o_in[...] = mg[x] + spread * stat_in[x, :, 0:1]

    reduce_z("v")
    for name in quarters:
        reduce_x(name)
    turned_x()
    arrived(vy, rs_recv.at[4, 1])
    v2[...] = v1[...] + vy[...]
    for n in range(hops):
        send(v2, vz.at[hops - 1 - n], rs_send.at[4, 2 + n], rs_recv.at[4, 2 + hops - 1 - n], zpeers[n])
    reduce_x("o")
    reduce_x("q")
    reduce_x("k")
    reduce_x("v")
    total = v2[...]
    for n in range(hops):
        arrived(vz.at[n], rs_recv.at[4, 2 + n])
        total = total + vz[n]
    v3[...] = total
    send(v3, vx, rs_send.at[4, 2 + hops], rs_recv.at[4, 2 + hops], xpeer)

    fin, got = reduced("d")
    o_wd[pl.ds(pl.multiple_of(x * slab, 16), sub), :] = fin[...]
    o_wd[pl.ds(pl.multiple_of((1 - x) * slab, 16), sub), :] = wide(got[...])
    fin, got = reduced("e")
    o_wd[pl.ds(pl.multiple_of(x * slab + sub, 16), sub), :] = fin[...]
    o_wd[pl.ds(pl.multiple_of((1 - x) * slab + sub, 16), sub), :] = wide(got[...])
    parts = [reduced(name) for name in quarters]
    one = jnp.concatenate([fin[...] for fin, got in parts], axis=1)
    two = jnp.concatenate([wide(got[...]) for fin, got in parts], axis=1)
    left, right = jnp.where(x == 0, one, two), jnp.where(x == 0, two, one)
    woven = []
    for b in range(fsdp):
        woven.append(left[:, b * slab : (b + 1) * slab])
        woven.append(right[:, b * slab : (b + 1) * slab])
    o_wu[...] = jnp.concatenate(woven, axis=1)
    fin, got = reduced("o")
    o_wo[:, pl.ds(mine, half)] = fin[...]
    o_wo[:, pl.ds(theirs, half)] = wide(got[...])
    arrived(vx, rs_recv.at[4, 2 + hops])
    v0_all = v3[...] + vx[...]
    taken = jnp.zeros((8, rows), F32)
    low_part = jnp.zeros((1, slab), F32)
    high_part = jnp.zeros((1, slab), F32)
    in_row = width // slab
    for b in range(fsdp):
        here = jnp.where(i == b, 1.0, 0.0)
        taken = taken + here * v0_all[0:8, b * rows : (b + 1) * rows]
        at_row, lane = 8 + b // in_row, (b % in_row) * slab
        low_part = low_part + here * v0_all[at_row : at_row + 1, lane : lane + slab]
        high_part = high_part + here * v0_all[at_row + per : at_row + per + 1, lane : lane + slab]
    for at_row, ref in enumerate((o_fg, o_fb, o_bq, o_bv, o_bo, o_sg, o_sb, o_bd)):
        ref[...] = taken[at_row : at_row + 1]
    o_bu[...] = jnp.concatenate([low_part, high_part], axis=1)
    for name, ref in (("q", o_wq), ("k", o_wk), ("v", o_wv)):
        fin, got = reduced(name)
        ref[:, pl.ds(mine, half)] = fin[...]
        ref[:, pl.ds(theirs, half)] = wide(got[...])

    for copy in started:
        copy.wait_send()
    for copy in inner_copies:
        pl.when(inner)(copy.wait_send)


def hand_over(*refs):
    count = (len(refs) - 1) // 2
    copies = [pltpu.make_async_copy(refs[n], refs[count + n], refs[-1].at[n]) for n in range(count)]
    for copy in copies:
        copy.start()
    for copy in copies:
        copy.wait()


def fused_on_device(frames_in, cotangent, *stacks):
    fsdp = lax.axis_size("fsdp")
    own, width = frames_in.shape[1:]
    sz = Sizes(own, width, stacks[13].shape[1] * fsdp, fsdp)
    half, ff, depth, rows, slab, frames = sz.half, sz.ff, sz.depth, sz.rows, sz.slab, sz.frames
    args = [frames_in[0], cotangent[0]] + [s if s.ndim == 2 else s[0] for s in stacks]
    in_hbm = {0, 1, 4, 6, 7, 9, 15}
    whole = pl.BlockSpec(memory_space=pltpu.VMEM)
    outs = [jax.ShapeDtypeStruct(a.shape, F32) for a in args]

    def vm(dtype, *dims):
        return pltpu.VMEM(dims, dtype)

    def reduce_scratch(r, w, *both):
        return [
            vm(BF16, depth, 2, 2, r, w), vm(BF16, depth, 2, r, w), vm(BF16, depth, r, w),
            vm(BF16, depth, r, w), vm(BF16, depth - 1, *both, r, w), vm(BF16, depth - 1, *both, r, w),
            vm(BF16, r, w), vm(BF16, r, w), vm(F32, r, w),
        ]

    heads = half // HEAD_DIM
    scratch = [
        vm(BF16, 3, fsdp, rows, half), vm(BF16, fsdp, rows, width), vm(BF16, fsdp, rows, ff),
        vm(BF16, fsdp, slab, width), vm(F32, fsdp, 16, 128), vm(F32, 8, width), vm(F32, 1, ff),
        vm(F32, 2, own, width), vm(F32, 2, own, width), vm(F32, 2, own, width), vm(F32, 2, own, width),
        vm(F32, 2, own, width), vm(BF16, frames, width), vm(BF16, frames, width),
        vm(F32, 2, own, 128), vm(F32, 2, own, 128), vm(BF16, 3, frames, half),
        vm(F32, heads, frames, frames), vm(BF16, 2, frames, half), vm(BF16, frames, ff),
        vm(F32, frames, ff), vm(BF16, frames, ff), vm(F32, 2, own, width), vm(BF16, frames, width),
        vm(BF16, frames, width), vm(BF16, frames, half), vm(BF16, 3, frames, half),
        vm(F32, frames, width), vm(BF16, 2, frames, half), vm(BF16, 2, frames, half),
        vm(F32, 2, own, width), vm(BF16, own, width), vm(BF16, own, width),
        vm(F32, 2, own, width), vm(BF16, own, width), vm(BF16, own, width),
        *reduce_scratch(slab // 2, width), *reduce_scratch(slab // 2, width, 2), vm(F32, 2, slab // 2, width),
        *reduce_scratch(rows, ff // 4), *reduce_scratch(rows, ff // 4),
        *reduce_scratch(rows, ff // 4), *reduce_scratch(rows, ff // 4), *reduce_scratch(rows, half),
        *reduce_scratch(rows, half), *reduce_scratch(rows, half), *reduce_scratch(rows, half),
        vm(F32, 16, width), vm(F32, 16, width), vm(F32, 16, width), vm(F32, 16, width),
        vm(F32, 16, width), vm(F32, 16, width), vm(F32, depth - 1, 16, width), vm(F32, 16, width),
        pltpu.SemaphoreType.DMA((7,)),
        pltpu.SemaphoreType.DMA((6, 4 * depth + 2)), pltpu.SemaphoreType.DMA((6, fsdp)),
        pltpu.SemaphoreType.DMA((11, depth + 2)), pltpu.SemaphoreType.DMA((11, depth + 2)),
        pltpu.SemaphoreType.DMA((7,)), pltpu.SemaphoreType.DMA((7,)),
    ]
    made = pl.pallas_call(
        functools.partial(encoder_kernel, sz),
        out_shape=[vm(F32, *o.shape) for o in outs],
        in_specs=[pl.BlockSpec(memory_space=pl.ANY) if n in in_hbm else whole for n in range(len(args))],
        out_specs=[whole] * len(outs),
        scratch_shapes=scratch,
        compiler_params=pltpu.CompilerParams(
            collective_id=0, has_side_effects=True, vmem_limit_bytes=56 * 2**20
        ),
    )(*args)
    anywhere = [pl.BlockSpec(memory_space=pl.ANY)] * len(outs)
    made = pl.pallas_call(
        hand_over,
        out_shape=outs,
        in_specs=anywhere,
        out_specs=anywhere,
        scratch_shapes=[pltpu.SemaphoreType.DMA((len(outs),))],
    )(*[pltpu.with_memory_space_constraint(m, pltpu.VMEM) for m in made])
    return tuple(o if p.ndim == 2 else o[None] for o, p in zip(made, (frames_in, cotangent, *stacks)))


def fits_kernel(mesh, frames_in, up_weight):
    seq, fsdp = mesh.shape["seq"], mesh.shape["fsdp"]
    width, hidden = up_weight.shape[1:]
    return (
        seq == 2
        and fsdp == 16
        and frames_in.shape[0] == fsdp
        and frames_in.shape[1] % 64 == 0
        and width % (16 * fsdp) == 0
        and width % 256 == 0
        and hidden % (64 * fsdp) == 0
        and hidden * 2 % (128 * fsdp) == 0
        and hidden == 4 * width
    )


def solution(mesh):
    def build(body):
        return jax.shard_map(
            body,
            mesh=mesh,
            in_specs=(
                P("fsdp", "seq", None),
                P("fsdp", "seq", None),
                P(None, "fsdp"),
                P(None, "fsdp"),
                P(None, "fsdp", None),
                P(None, "fsdp"),
                P(None, "fsdp", None),
                P(None, "fsdp", None),
                P(None, "fsdp"),
                P(None, "fsdp", None),
                P(None, "fsdp"),
                P(None, "fsdp"),
                P(None, "fsdp"),
                P(None, "fsdp", None),
                P(None, "fsdp"),
                P(None, "fsdp", None),
                P(None, "fsdp"),
            ),
            out_specs=(
                P("fsdp", "seq", None),
                P("fsdp", "seq", None),
                P(None, "fsdp"),
                P(None, "fsdp"),
                P(None, "fsdp", None),
                P(None, "fsdp"),
                P(None, "fsdp", None),
                P(None, "fsdp", None),
                P(None, "fsdp"),
                P(None, "fsdp", None),
                P(None, "fsdp"),
                P(None, "fsdp"),
                P(None, "fsdp"),
                P(None, "fsdp", None),
                P(None, "fsdp"),
                P(None, "fsdp", None),
                P(None, "fsdp"),
            ),
            check_vma=False,
        )

    def run(*arrays):
        body = fused_on_device if fits_kernel(mesh, arrays[0], arrays[13]) else on_device
        return build(body)(*arrays)

    return run
```
